32 devices in a mesh: expert: 4 (over y, x), hidden: 8 (over z, core).
Axes of the slice: x: 2, y: 2, z: 4, core: 2. Of those that a mesh axis runs over, the one named last changes fastest.
Arguments:
- patches: bfloat16 [32768, 384], P(('expert', 'hidden')), may hold values from -6 to 6
- cotangent: bfloat16 [32768, 384], P(('expert', 'hidden')), may hold values from -6 to 6
- expert_ids: int32 [32768, 4], P(('expert', 'hidden')), may hold values from 0 to 15, all different within a row
- gates: float32 [32768, 4], P(('expert', 'hidden')), may hold values from 0.1 to 0.4
- task_ids: int32 [32768], P(('expert', 'hidden')), may hold values from 0 to 1
- segments: int32 [32, 1024], P(('expert', 'hidden')), may hold values from 0 to 7, never falling along the last dimension, each value on 1 to 512 neighbouring positions
- norm_params: float32 [6, 384], replicated, may hold values from 0.5 to 1.5
- attn_qkv: float32 [384, 1152], replicated, may hold values from -0.3125 to 0.3125
- attn_proj: float32 [384, 384], replicated, may hold values from -1.75 to 1.75
- expert_inner: float32 [1536, 16, 384], P('hidden', 'expert'), may hold values from -0.3125 to 0.3125
- expert_outer: float32 [1536, 16, 384], P('hidden', 'expert'), may hold values from -0.5 to 0.5
- norm_moment: float32 [6, 384], replicated, may hold values from -896 to 896
- qkv_moment: float32 [384, 1152], replicated, may hold values from -512 to 512
- proj_moment: float32 [384, 384], replicated, may hold values from -128 to 128
- inner_moment: float32 [1536, 16, 384], P('hidden', 'expert'), may hold values from -160 to 160
- outer_moment: float32 [1536, 16, 384], P('hidden', 'expert'), may hold values from -80 to 80
- norm_average: float32 [6, 384], replicated, may hold values from 0.5 to 1.5
- qkv_average: float32 [384, 1152], replicated, may hold values from -0.3125 to 0.3125
- proj_average: float32 [384, 384], replicated, may hold values from -1.75 to 1.75
- inner_average: float32 [1536, 16, 384], P('hidden', 'expert'), may hold values from -0.3125 to 0.3125
- outer_average: float32 [1536, 16, 384], P('hidden', 'expert'), may hold values from -0.5 to 0.5
Outputs:
- block_out: bfloat16 [32768, 384], P(('expert', 'hidden'))
- patch_grad: float32 [32768, 384], P(('expert', 'hidden'))
- expert_load: float32 [16], replicated
- norm_new: float32 [6, 384], replicated
- norm_moment_new: float32 [6, 384], replicated
- norm_average_new: float32 [6, 384], replicated
- qkv_new: float32 [384, 1152], replicated
- qkv_moment_new: float32 [384, 1152], replicated
- qkv_average_new: float32 [384, 1152], replicated
- proj_new: float32 [384, 384], replicated
- proj_moment_new: float32 [384, 384], replicated
- proj_average_new: float32 [384, 384], replicated
- inner_new: float32 [1536, 16, 384], P('hidden', 'expert')
- inner_moment_new: float32 [1536, 16, 384], P('hidden', 'expert')
- inner_average_new: float32 [1536, 16, 384], P('hidden', 'expert')
- outer_new: float32 [1536, 16, 384], P('hidden', 'expert')
- outer_moment_new: float32 [1536, 16, 384], P('hidden', 'expert')
- outer_average_new: float32 [1536, 16, 384], P('hidden', 'expert')
The draws below stay inside these ranges and needn't reach their ends.
Inputs may be any that keep to these rules, and one draw needn't show every extreme that they name: `expert_ids`: each row names 4 different experts. `segments`: in each row the numbers never fall and each image has 1 to 512 slots.
All inputs are finite; a program needn't handle non-finite values.
Results may differ from the reference program's by a relative error of at most 0.012.
The reference program's roundings to bfloat16 on the way count: a program that leaves them out, or rounds other values in their place, can miss the bound.
Values may be sent and summed in bfloat16 or wider, within the bound.
No kernel may reach another device: no remote copies, remote signals or barrier semaphores. Data moves between devices by JAX's collectives and lax.ppermute only.
A program may use at most 320 MiB of HBM per device.

```python
import math
import jax
import jax.numpy as jnp
import numpy as np
from jax import lax

D = 384
HEADS = 6
HEAD = 64
EXPERTS = 16
FF = 1536
TOP = 4
TASKS = 2
TOK_DEV = 1024
SEQS = 32
TOKENS = 32768
CAP = 320
SEGS = 8
SEG_MOST = 512


def touch_ends(array, rng, least, largest):
    place = [jax.random.randint(jax.random.fold_in(rng, axis), (), 0, length) for axis, length in enumerate(array.shape)]
    main_axis = array.shape.index(max(array.shape))
    neighbour = place[:main_axis] + [(place[main_axis] + 1) % array.shape[main_axis]] + place[main_axis + 1:]
    return array.at[tuple(place)].set(least).at[tuple(neighbour)].set(largest)


def levels(rng, dims, cuts, least, largest):
    def one(dim, parts):
        heights = jax.random.uniform(jax.random.fold_in(jax.random.fold_in(rng, 6), dim), (parts,), jnp.float32, least / len(cuts), largest / len(cuts))
        return jnp.repeat(jnp.exp(heights), dims[dim] // parts).reshape((-1,) + (1,) * (len(dims) - dim - 1))

    loudness = one(*cuts[0])
    for cut in cuts[1:]:
        loudness = loudness * one(*cut)
    return loudness


def distinct(key, rows, count, top, lift):
    order = jax.random.permutation(jax.random.fold_in(key, 1), count)
    favour = order
    for power in range(3):
        favour = favour * favour // count
    favour = favour * lift // count
    lots = jax.random.randint(jax.random.fold_in(key, 2), (rows, count), 0, 4096) + favour
    holders = jax.random.permutation(jax.random.fold_in(key, 3), rows)[jnp.arange(count) % rows]
    lots = jnp.where(jnp.arange(rows)[:, None] == holders[None, :], 1 << 14, lots)
    score = lots * count + jnp.arange(count)
    return lax.top_k(score.astype(jnp.int32), top)[1].astype(jnp.int32)


def profile(number_of, total, most, lean):
    loads = [(1 << 20) // math.isqrt(grade ** lean) + 1 for grade in range(2, number_of + 1)]
    surplus, given = total - most - (number_of - 1), [1] * (number_of - 1)
    while surplus > 0:
        candidates = [i for i in range(number_of - 1) if given[i] < most]
        whole, budget = sum([loads[i] for i in candidates]), surplus
        for i in candidates:
            addition = min(most - given[i], max(1, budget * loads[i] // whole), surplus)
            given[i] = given[i] + addition
            surplus = surplus - addition
    return np.array([most] + given)


def uneven_parts(rng, number_of, total, reach, skew):
    if number_of == 2:
        one = jax.random.randint(rng, (), max(1, total - reach), min(reach, total - 1) + 1)
        return jnp.stack([one, total - one])
    sizes = jnp.asarray(profile(number_of, total, reach, skew), jnp.int32)
    couples = (number_of - 1) // 2
    source_of, sink = sizes[1:1 + 2 * couples:2], sizes[2:2 + 2 * couples:2]
    margin = jnp.minimum(source_of - 1, reach - sink)
    moved = jax.random.randint(jax.random.fold_in(rng, 1), (couples,), 0, 1 << 20) % (margin + 1)
    sizes = sizes.at[1:1 + 2 * couples:2].set(source_of - moved).at[2:2 + 2 * couples:2].set(sink + moved)
    return sizes[jax.random.permutation(jax.random.fold_in(rng, 2), number_of)]


def gaussian(own_key, extent, deviation, bound, cuts=(), kind=jnp.bfloat16):
    values = jax.random.normal(own_key, extent, jnp.float32) * deviation
    if len(cuts) > 0:
        values = levels(own_key, extent, cuts, -0.22, 0.18) * values
    return jnp.clip(values, min=-bound, max=bound).astype(kind)


def setup_inputs(seed: int = 0) -> dict:
    splits = jax.random.split(jax.random.key(seed), 22)
    return {
        "patches": gaussian(splits[0], (TOKENS, D), 1.0, 6.0, ((0, 32),)),
        "cotangent": gaussian(splits[1], (TOKENS, D), 1.0, 6.0, ((0, 32),)),
        "expert_ids": distinct(splits[2], TOKENS, EXPERTS, TOP, 2048),
        "gates": jnp.clip(0.1 + 0.3 * jax.random.uniform(splits[3], (TOKENS, TOP), jnp.float32) ** levels(splits[3], (TOKENS, TOP), ((0, 32),), -0.2, 0.2), 0.1, 0.4),
        "task_ids": touch_ends(jax.random.randint(splits[4], (TOKENS,), 0, TASKS), jax.random.fold_in(splits[4], 1), 0, TASKS - 1).astype(jnp.int32),
        "segments": jax.vmap(lambda own: jnp.searchsorted(jnp.cumsum(uneven_parts(own, SEGS, TOK_DEV, SEG_MOST, 1)), jnp.arange(TOK_DEV), side="right"))(jax.random.split(splits[5], SEQS)).reshape((SEQS, TOK_DEV)).astype(jnp.int32),
        "norm_params": jnp.clip(jax.random.uniform(splits[6], (2 + 2 * TASKS, D), jnp.float32, 0.5, 1.5), 0.5, 1.5),
        "attn_qkv": gaussian(splits[7], (D, 3 * D), D ** -0.5, 0.3125, (), jnp.float32),
        "attn_proj": gaussian(splits[8], (D, D), (D // 32) ** -0.5, 1.75, (), jnp.float32),
        "expert_inner": gaussian(splits[9], (FF, EXPERTS, D), D ** -0.5, 0.3125, ((0, 8), (1, 4)), jnp.float32),
        "expert_outer": gaussian(splits[10], (FF, EXPERTS, D), (FF // 12) ** -0.5, 0.5, ((0, 8), (1, 4)), jnp.float32),
        "norm_moment": gaussian(splits[11], (2 + 2 * TASKS, D), (0.8 * TOKENS ** 0.5), 896.0, (), jnp.float32),
        "qkv_moment": gaussian(splits[12], (D, 3 * D), (0.5 * TOKENS ** 0.5), 512.0, (), jnp.float32),
        "proj_moment": gaussian(splits[13], (D, D), (0.13 * TOKENS ** 0.5), 128.0, (), jnp.float32),
        "inner_moment": gaussian(splits[14], (FF, EXPERTS, D), (0.15 * TOKENS ** 0.5), 160.0, ((0, 8), (1, 4)), jnp.float32),
        "outer_moment": gaussian(splits[15], (FF, EXPERTS, D), (0.075 * TOKENS ** 0.5), 80.0, ((0, 8), (1, 4)), jnp.float32),
        "norm_average": jnp.clip(jax.random.uniform(splits[16], (2 + 2 * TASKS, D), jnp.float32, 0.5, 1.5), 0.5, 1.5),
        "qkv_average": gaussian(splits[17], (D, 3 * D), D ** -0.5, 0.3125, (), jnp.float32),
        "proj_average": gaussian(splits[18], (D, D), (D // 32) ** -0.5, 1.75, (), jnp.float32),
        "inner_average": gaussian(splits[19], (FF, EXPERTS, D), D ** -0.5, 0.3125, ((0, 8), (1, 4)), jnp.float32),
        "outer_average": gaussian(splits[20], (FF, EXPERTS, D), (FF // 12) ** -0.5, 0.5, ((0, 8), (1, 4)), jnp.float32),
    }


MOMENT_DECAY = 0.9
AVERAGE_DECAY = 0.9
RATE_NORM = 0.23
RATE_QKV = 0.064
RATE_PROJ = 1.4
RATE_INNER = 0.21
RATE_OUTER = 0.73
NORM_EPS = 1e-06
MASKED = -1e+30

@jax.custom_vjp
def low(v):
    return lax.optimization_barrier(v.astype(jnp.bfloat16)).astype(jnp.float32)

@jax.custom_vjp
def low_back(v):
    return v

def low_keep(v):
    return (low(v), None)

def low_pass(kept, grad):
    return (grad,)

def back_keep(v):
    return (v, None)

def back_low(kept, grad):
    return (low(grad),)
low.defvjp(low_keep, low_pass)
low_back.defvjp(back_keep, back_low)

def product(left, right):
    return jnp.dot(left, right, precision=lax.Precision.HIGHEST, preferred_element_type=jnp.float32)

def layer_norm(values):
    center = values - lax.optimization_barrier(jnp.mean(values, axis=-1, keepdims=True))
    spread = lax.optimization_barrier(jnp.mean(center * center, axis=-1, keepdims=True))
    return center * lax.rsqrt(spread + NORM_EPS)

def routing(expert_ids):
    flat_ids = expert_ids.reshape(SEQS, TOK_DEV * TOP)
    onehot = (flat_ids[:, :, None] == jnp.arange(EXPERTS, dtype=jnp.int32)[None, None, :]).astype(jnp.int32)
    slot_place = (lax.optimization_barrier(jnp.sum(onehot * jnp.cumsum(onehot, axis=1), axis=2)) - 1).astype(jnp.int32)
    is_kept = slot_place < CAP
    counts = lax.optimization_barrier(jnp.sum(onehot * is_kept[:, :, None].astype(jnp.int32), axis=(0, 1))).astype(jnp.int32)
    device_row = jnp.arange(SEQS, dtype=jnp.int32)[:, None]
    pair_index = jnp.arange(TOK_DEV * TOP, dtype=jnp.int32)[None, :]
    column = jnp.where(is_kept, flat_ids * CAP + slot_place, EXPERTS * CAP).astype(jnp.int32)
    token_index = (device_row * TOK_DEV + pair_index // TOP).astype(jnp.int32)
    source = jnp.full((SEQS, EXPERTS * CAP + 1), TOKENS, jnp.int32)
    source = source.at[device_row, column].set(token_index)[:, :EXPERTS * CAP]
    source = jnp.transpose(source.reshape(SEQS, EXPERTS, CAP), (1, 0, 2)).reshape(EXPERTS, SEQS * CAP)
    pick_row = jnp.where(is_kept, flat_ids * (SEQS * CAP) + device_row * CAP + slot_place, EXPERTS * SEQS * CAP)
    return (source, pick_row.astype(jnp.int32).reshape(TOKENS, TOP), counts)

def attend(pieces):
    block_qkv, seg_marks = pieces
    query_heads = block_qkv[:, :, 0]
    key_heads = block_qkv[:, :, 1]
    value_heads = block_qkv[:, :, 2]
    scores = jnp.einsum('gqhd,gkhd->ghqk', query_heads, key_heads, precision=lax.Precision.HIGHEST)
    scores = low_back(scores * HEAD ** (-0.5))
    same_image = seg_marks[:, None, :, None] == seg_marks[:, None, None, :]
    scores = jnp.where(same_image, scores, MASKED)
    row_peak = lax.optimization_barrier(jnp.max(scores, axis=-1, keepdims=True))
    row_exp = jnp.exp(scores - row_peak)
    weights = low(row_exp / lax.optimization_barrier(jnp.sum(row_exp, axis=-1, keepdims=True)))
    mixed = jnp.einsum('ghqk,gkhd->gqhd', weights, value_heads, precision=lax.Precision.HIGHEST)
    return low(low_back(mixed))

def block(patches, norm_params, attn_qkv, attn_proj, expert_inner, expert_outer, gates, task_ids, segments, source, pick_row):
    normed_one = layer_norm(patches) * norm_params[0] + norm_params[1]
    joined = low(low_back(product(low(normed_one), low(attn_qkv))))
    group_size = min(SEQS, max(1, 4096 // TOK_DEV))
    heads = joined.reshape(SEQS // group_size, group_size, TOK_DEV, 3, HEADS, HEAD)
    seg_marks = segments.reshape(SEQS // group_size, group_size, TOK_DEV)
    mixed = lax.map(jax.checkpoint(attend), (heads, seg_marks)).reshape(TOKENS, D)
    hidden_one = patches + low_back(product(mixed, low(attn_proj)))
    normed_two = layer_norm(hidden_one) * norm_params[2 + task_ids] + norm_params[2 + TASKS + task_ids]
    moe_pad = jnp.concatenate([low(normed_two), jnp.zeros((1, D), jnp.float32)], axis=0)

    def expert(pieces):
        rows_index, inner_part, outer_part = pieces
        rows_in = low_back(moe_pad[rows_index])
        pre_act = low_back(jnp.einsum('rd,fd->rf', rows_in, inner_part, precision=lax.Precision.HIGHEST))
        act_val = low(jax.nn.gelu(pre_act, approximate=False))
        return low(low_back(product(act_val, outer_part)))
    inner_all = jnp.transpose(low(expert_inner), (1, 0, 2))
    outer_all = jnp.transpose(low(expert_outer), (1, 0, 2))
    expert_rows = lax.map(jax.checkpoint(expert), (source, inner_all, outer_all))
    table = jnp.concatenate([expert_rows.reshape(EXPERTS * SEQS * CAP, D), jnp.zeros((1, D), jnp.float32)], axis=0)
    routed = table[pick_row]
    return hidden_one + lax.optimization_barrier(jnp.sum(gates[:, :, None] * routed, axis=1))

def nesterov(weight, moment, average, grad, rate):
    moment_new = MOMENT_DECAY * moment + grad
    weight_new = weight - rate * (grad + MOMENT_DECAY * moment_new)
    average_new = AVERAGE_DECAY * average + (1.0 - AVERAGE_DECAY) * weight_new
    return (weight_new, moment_new, average_new)

def reference(patches, cotangent, expert_ids, gates, task_ids, segments, norm_params, attn_qkv, attn_proj, expert_inner, expert_outer, norm_moment, qkv_moment, proj_moment, inner_moment, outer_moment, norm_average, qkv_average, proj_average, inner_average, outer_average):
    source, pick_row, counts = routing(expert_ids)

    def forward(inputs, norms, qkv_weight, proj_weight, inner_weight, outer_weight):
        return block(inputs, norms, qkv_weight, proj_weight, inner_weight, outer_weight, gates, task_ids, segments, source, pick_row)
    result, pullback = jax.vjp(forward, patches.astype(jnp.float32), norm_params, attn_qkv, attn_proj, expert_inner, expert_outer)
    patch_grad, norm_grad, qkv_grad, proj_grad, inner_grad, outer_grad = pullback(cotangent.astype(jnp.float32))
    root_tokens = math.sqrt(TOKENS)
    norm_new = nesterov(norm_params, norm_moment, norm_average, norm_grad, RATE_NORM / root_tokens)
    qkv_new = nesterov(attn_qkv, qkv_moment, qkv_average, qkv_grad, RATE_QKV / root_tokens)
    proj_new = nesterov(attn_proj, proj_moment, proj_average, proj_grad, RATE_PROJ / root_tokens)
    inner_new = nesterov(expert_inner, inner_moment, inner_average, inner_grad, RATE_INNER / root_tokens)
    outer_new = nesterov(expert_outer, outer_moment, outer_average, outer_grad, RATE_OUTER / root_tokens)
    expert_load = counts.astype(jnp.float32) * (EXPERTS / (TOKENS * TOP))
    return (result.astype(jnp.bfloat16), patch_grad, expert_load, norm_new[0], norm_new[1], norm_new[2], qkv_new[0], qkv_new[1], qkv_new[2], proj_new[0], proj_new[1], proj_new[2], inner_new[0], inner_new[1], inner_new[2], outer_new[0], outer_new[1], outer_new[2])
```

```python
import math

import jax
import jax.numpy as jnp
from jax import lax
from jax.sharding import PartitionSpec as P

D = 384
HEADS = 6
HEAD = 64
EXPERTS = 16
TOP = 4
TASKS = 2
CAP = 320


MOMENT_DECAY = 0.9
AVERAGE_DECAY = 0.9
RATE_NORM = 0.23
RATE_QKV = 0.064
RATE_PROJ = 1.4
RATE_INNER = 0.21
RATE_OUTER = 0.73
NORM_EPS = 1e-06
MASKED = -1e30


def layer_norm(values):
    center = values - jnp.mean(values, axis=-1, keepdims=True)
    spread = jnp.mean(center * center, axis=-1, keepdims=True)
    return center * lax.rsqrt(spread + NORM_EPS)


def first_norm(values, gain_row, offset_row):
    return layer_norm(values) * gain_row + offset_row


def exact_gelu(values):
    return jax.nn.gelu(values, approximate=False)


def routing(expert_ids, groups):
    flat_ids = expert_ids.reshape(-1)
    pair_count = flat_ids.shape[0]
    local_count = EXPERTS // groups
    onehot = (flat_ids[:, None] == jnp.arange(EXPERTS, dtype=jnp.int32)[None, :]).astype(jnp.int32)
    slot_place = jnp.sum(onehot * jnp.cumsum(onehot, axis=0), axis=1) - 1
    is_kept = slot_place < CAP
    slot_total = EXPERTS * CAP
    target = (flat_ids % local_count * groups + flat_ids // local_count) * CAP + slot_place
    target = jnp.where(is_kept, target, slot_total)
    source = jnp.full((slot_total + 1,), pair_count, jnp.int32)
    source = source.at[target].set(jnp.arange(pair_count, dtype=jnp.int32))[:slot_total]
    counts = jnp.sum(onehot * is_kept[:, None].astype(jnp.int32), axis=0)
    return (target, source, counts)


def attend_forward(query_heads, key_heads, value_heads, seg_marks, block_rows):
    score_scale = HEAD ** (-0.5)
    seq_length = query_heads.shape[0]
    outputs = []
    log_sums = []
    for row_start in range(0, seq_length, block_rows):
        query_rows = query_heads[row_start : row_start + block_rows]
        marks_rows = seg_marks[row_start : row_start + block_rows]
        scores = (
            jnp.einsum("qhd,khd->hqk", query_rows, key_heads, preferred_element_type=jnp.float32)
            * score_scale
        )
        scores = jnp.where(marks_rows[None, :, None] == seg_marks[None, None, :], scores, MASKED)
        row_peak = jnp.max(scores, axis=-1, keepdims=True)
        row_exp = jnp.exp(scores - row_peak)
        row_total = jnp.sum(row_exp, axis=-1, keepdims=True)
        weights_low = (row_exp / row_total).astype(jnp.bfloat16)
        mixed_rows = jnp.einsum(
            "hqk,khd->qhd", weights_low, value_heads, preferred_element_type=jnp.float32
        )
        outputs.append(mixed_rows.astype(jnp.bfloat16))
        log_sums.append(row_peak + jnp.log(row_total))
    return (jnp.concatenate(outputs, axis=0), log_sums)


def attend_backward(
    query_heads, key_heads, value_heads, seg_marks, mixed_grad, log_sums, block_rows
):
    score_scale = HEAD ** (-0.5)
    seq_length = query_heads.shape[0]
    key_grad = jnp.zeros(key_heads.shape, jnp.float32)
    value_grad = jnp.zeros(value_heads.shape, jnp.float32)
    query_grads = []
    for block_index in range(seq_length // block_rows):
        row_start = block_index * block_rows
        query_rows = query_heads[row_start : row_start + block_rows]
        marks_rows = seg_marks[row_start : row_start + block_rows]
        grad_rows = mixed_grad[row_start : row_start + block_rows]
        scores = (
            jnp.einsum("qhd,khd->hqk", query_rows, key_heads, preferred_element_type=jnp.float32)
            * score_scale
        )
        scores = jnp.where(marks_rows[None, :, None] == seg_marks[None, None, :], scores, MASKED)
        probs = jnp.exp(scores - log_sums[block_index])
        probs_low = probs.astype(jnp.bfloat16)
        value_grad = value_grad + jnp.einsum(
            "hqk,qhd->khd", probs_low, grad_rows, preferred_element_type=jnp.float32
        )
        prob_grad = jnp.einsum(
            "qhd,khd->hqk", grad_rows, value_heads, preferred_element_type=jnp.float32
        )
        row_dot = jnp.sum(prob_grad * probs, axis=-1, keepdims=True)
        score_grad = (probs * (prob_grad - row_dot)).astype(jnp.bfloat16)
        query_grads.append(
            jnp.einsum("hqk,khd->qhd", score_grad, key_heads, preferred_element_type=jnp.float32)
            * score_scale
        )
        key_grad = (
            key_grad
            + jnp.einsum("hqk,qhd->khd", score_grad, query_rows, preferred_element_type=jnp.float32)
            * score_scale
        )
    return (jnp.concatenate(query_grads, axis=0), key_grad, value_grad)


def expert_forward(rows_in, inner_part, outer_part):
    pre_act = jnp.einsum("erd,fed->erf", rows_in, inner_part, preferred_element_type=jnp.float32)
    act_low = exact_gelu(pre_act).astype(jnp.bfloat16)
    return jnp.einsum("erf,fed->erd", act_low, outer_part, preferred_element_type=jnp.float32)


def expert_backward_parts(rows_in, rows_grad, inner_part, outer_part):
    pre_act = jnp.einsum("erd,fed->erf", rows_in, inner_part, preferred_element_type=jnp.float32)
    act_val, gelu_back = jax.vjp(exact_gelu, pre_act)
    act_low = act_val.astype(jnp.bfloat16)
    act_grad = jnp.einsum("erd,fed->erf", rows_grad, outer_part, preferred_element_type=jnp.float32)
    pre_grad = gelu_back(act_grad)[0].astype(jnp.bfloat16)
    input_grad = jnp.einsum(
        "erf,fed->erd", pre_grad, inner_part, preferred_element_type=jnp.float32
    )
    return (input_grad, pre_grad, act_low)


def butterfly_sum(value, wire):
    sizes = [("hidden", lax.axis_size("hidden")), ("expert", lax.axis_size("expert"))]
    steps = []
    for axis, size in sizes:
        bit = 1
        while bit < size:
            steps.append((axis, size, bit))
            bit *= 2
    steps = steps[:1] + [s for s in steps if s[0] == "expert"] + [s for s in steps[1:] if s[0] == "hidden"]
    value = value.astype(jnp.float32)
    done = []
    for axis, size, bit in steps:
        half = value.shape[0] // 2
        if value.shape[0] % 2 or half % 8:
            break
        done.append((axis, size, bit))
        upper = (lax.axis_index(axis) & bit) > 0
        low_half, high_half = value[:half], value[half:]
        keep = jnp.where(upper, high_half, low_half)
        send = jnp.where(upper, low_half, high_half).astype(wire)
        got = lax.ppermute(send, axis, [(i, i ^ bit) for i in range(size)])
        value = keep + got.astype(jnp.float32)
    for axis, size, bit in steps[len(done):]:
        got = lax.ppermute(value.astype(wire), axis, [(i, i ^ bit) for i in range(size)])
        value = value + got.astype(jnp.float32)
    value = value.astype(wire)
    for axis, size, bit in done[::-1]:
        upper = (lax.axis_index(axis) & bit) > 0
        got = lax.ppermute(value, axis, [(i, i ^ bit) for i in range(size)])
        first = jnp.where(upper, got, value)
        second = jnp.where(upper, value, got)
        value = jnp.concatenate([first, second], axis=0)
    return value.astype(jnp.float32)


def nesterov(weight, moment, average, grad, rate):
    moment_new = MOMENT_DECAY * moment + grad
    weight_new = weight - rate * (grad + MOMENT_DECAY * moment_new)
    average_new = AVERAGE_DECAY * average + (1.0 - AVERAGE_DECAY) * weight_new
    return (weight_new, moment_new, average_new)


def body(
    patches,
    cotangent,
    expert_ids,
    gates,
    task_ids,
    segments,
    norm_params,
    attn_qkv,
    attn_proj,
    expert_inner,
    expert_outer,
    norm_moment,
    qkv_moment,
    proj_moment,
    inner_moment,
    outer_moment,
    norm_average,
    qkv_average,
    proj_average,
    inner_average,
    outer_average,
):
    groups = lax.axis_size("expert")
    tok_count = patches.shape[0]
    tokens_all = tok_count * groups * lax.axis_size("hidden")
    local_count = EXPERTS // groups
    block_rows = min(512, tok_count)
    inputs = patches.astype(jnp.float32)
    seg_marks = segments[0]
    normed_one, first_back = jax.vjp(first_norm, inputs, norm_params[0], norm_params[1])
    attn_in = normed_one.astype(jnp.bfloat16)
    qkv_low = attn_qkv.astype(jnp.bfloat16)
    proj_low = attn_proj.astype(jnp.bfloat16)
    joined = jnp.dot(attn_in, qkv_low, preferred_element_type=jnp.float32).astype(jnp.bfloat16)
    joined = joined.reshape(tok_count, 3, HEADS, HEAD)
    query_heads = joined[:, 0]
    key_heads = joined[:, 1]
    value_heads = joined[:, 2]
    mixed, log_sums = attend_forward(query_heads, key_heads, value_heads, seg_marks, block_rows)
    mixed = mixed.reshape(tok_count, D)
    hidden_one = inputs + jnp.dot(mixed, proj_low, preferred_element_type=jnp.float32)
    task_hot = (task_ids[:, None] == jnp.arange(TASKS, dtype=jnp.int32)[None, :]).astype(
        jnp.float32
    )

    def second_norm(values, table):
        gain_rows = jnp.dot(task_hot, table[:TASKS], precision=lax.Precision.HIGHEST)
        bias_rows = jnp.dot(task_hot, table[TASKS:], precision=lax.Precision.HIGHEST)
        return layer_norm(values) * gain_rows + bias_rows

    normed_two, second_back = jax.vjp(second_norm, hidden_one, norm_params[2:])
    moe_in = normed_two.astype(jnp.bfloat16)
    target, source, counts = routing(expert_ids, groups)
    moe_pad = jnp.concatenate([moe_in, jnp.zeros((1, D), jnp.bfloat16)], axis=0)
    slots_out = moe_pad[source // TOP].reshape(local_count, groups, CAP, D)
    rows_in = lax.all_to_all(slots_out, "expert", split_axis=1, concat_axis=1, tiled=True).reshape(
        local_count, groups * CAP, D
    )
    own_units = expert_inner.shape[0]
    inner_low = expert_inner.astype(jnp.bfloat16).reshape(own_units, local_count * D)
    outer_low = expert_outer.astype(jnp.bfloat16).reshape(own_units, local_count * D)
    inner_all, outer_all = (
        lax.all_gather(inner_low, "hidden", axis=0, tiled=True).reshape(-1, local_count, D),
        lax.all_gather(outer_low, "hidden", axis=0, tiled=True).reshape(-1, local_count, D),
    )
    expert_sum = expert_forward(rows_in, inner_all, outer_all)
    returned = lax.all_to_all(
        expert_sum.astype(jnp.bfloat16).reshape(local_count, groups, CAP, D),
        "expert",
        split_axis=1,
        concat_axis=1,
        tiled=True,
    )
    back_pad = jnp.concatenate(
        [returned.reshape(EXPERTS * CAP, D), jnp.zeros((1, D), jnp.bfloat16)], axis=0
    )
    routed = back_pad[target].reshape(tok_count, TOP, D)
    moe_sum = jnp.sum(gates[:, :, None] * routed.astype(jnp.float32), axis=1)
    block_out = (hidden_one + moe_sum).astype(jnp.bfloat16)
    out_grad = cotangent.astype(jnp.float32)
    pair_grad = (
        (gates[:, :, None] * out_grad[:, None, :]).astype(jnp.bfloat16).reshape(tok_count * TOP, D)
    )
    pair_pad = jnp.concatenate([pair_grad, jnp.zeros((1, D), jnp.bfloat16)], axis=0)
    slots_grad = pair_pad[source].reshape(local_count, groups, CAP, D)
    rows_grad = lax.all_to_all(
        slots_grad, "expert", split_axis=1, concat_axis=1, tiled=True
    ).reshape(local_count, groups * CAP, D)
    input_grad, pre_grad_all, act_all = expert_backward_parts(
        rows_in, rows_grad, inner_all, outer_all
    )
    def weight_sums(left, right):
        parts = [
            jnp.einsum("rf,rd->fd", left[e], right[e], preferred_element_type=jnp.float32).astype(jnp.bfloat16)
            for e in range(local_count)
        ]
        full = jnp.concatenate(parts, axis=1)
        mine = lax.psum_scatter(full, "hidden", scatter_dimension=0, tiled=True)
        return mine.astype(jnp.float32).reshape(own_units, local_count, D)

    inner_grad = weight_sums(pre_grad_all, rows_in)
    outer_grad = weight_sums(act_all, rows_grad)
    back_rows = lax.all_to_all(
        input_grad.astype(jnp.bfloat16).reshape(local_count, groups, CAP, D),
        "expert",
        split_axis=1,
        concat_axis=1,
        tiled=True,
    )
    grad_pad = jnp.concatenate(
        [back_rows.reshape(EXPERTS * CAP, D), jnp.zeros((1, D), jnp.bfloat16)], axis=0
    )
    moe_grad = jnp.sum(grad_pad[target].reshape(tok_count, TOP, D).astype(jnp.float32), axis=1)
    hidden_grad, table_grad = second_back(moe_grad)
    hidden_grad = hidden_grad + out_grad
    attn_grad_low = hidden_grad.astype(jnp.bfloat16)
    proj_grad = jnp.einsum("td,te->de", mixed, attn_grad_low, preferred_element_type=jnp.float32)
    mixed_grad = jnp.einsum(
        "te,de->td", attn_grad_low, proj_low, preferred_element_type=jnp.float32
    )
    mixed_grad = mixed_grad.astype(jnp.bfloat16).reshape(tok_count, HEADS, HEAD)
    query_grad, key_grad, value_grad = attend_backward(
        query_heads, key_heads, value_heads, seg_marks, mixed_grad, log_sums, block_rows
    )
    joined_grad = (
        jnp.stack([query_grad, key_grad, value_grad], axis=1)
        .reshape(tok_count, 3 * D)
        .astype(jnp.bfloat16)
    )
    qkv_grad = jnp.einsum("td,te->de", attn_in, joined_grad, preferred_element_type=jnp.float32)
    attn_in_grad = jnp.einsum("te,de->td", joined_grad, qkv_low, preferred_element_type=jnp.float32)
    input_first, gain_grad, offset_grad = first_back(attn_in_grad)
    patch_grad = hidden_grad + input_first
    norm_grad = jnp.concatenate([gain_grad[None], offset_grad[None], table_grad], axis=0)
    big = jnp.concatenate([qkv_grad, proj_grad], axis=1)
    pad_rows = -big.shape[0] % 512
    big = jnp.concatenate([big, jnp.zeros((pad_rows, big.shape[1]), jnp.float32)], axis=0)
    big_sum = butterfly_sum(big, jnp.bfloat16)[:D]
    qkv_sum, proj_sum = big_sum[:, : 3 * D], big_sum[:, 3 * D :]
    count_row = jnp.pad(counts.astype(jnp.float32), (0, D - EXPERTS))[None]
    small = jnp.concatenate([norm_grad, count_row, jnp.zeros((1, D), jnp.float32)], axis=0)
    small_sum = butterfly_sum(small, jnp.float32)
    norm_sum, count_sum = small_sum[:6], small_sum[6, :EXPERTS]
    expert_load = count_sum * (EXPERTS / (tokens_all * TOP))
    root_tokens = math.sqrt(tokens_all)
    norm_new = nesterov(norm_params, norm_moment, norm_average, norm_sum, RATE_NORM / root_tokens)
    qkv_new = nesterov(attn_qkv, qkv_moment, qkv_average, qkv_sum, RATE_QKV / root_tokens)
    proj_new = nesterov(attn_proj, proj_moment, proj_average, proj_sum, RATE_PROJ / root_tokens)
    inner_new = nesterov(
        expert_inner, inner_moment, inner_average, inner_grad, RATE_INNER / root_tokens
    )
    outer_new = nesterov(
        expert_outer, outer_moment, outer_average, outer_grad, RATE_OUTER / root_tokens
    )
    return (
        block_out,
        patch_grad,
        expert_load,
        norm_new[0],
        norm_new[1],
        norm_new[2],
        qkv_new[0],
        qkv_new[1],
        qkv_new[2],
        proj_new[0],
        proj_new[1],
        proj_new[2],
        inner_new[0],
        inner_new[1],
        inner_new[2],
        outer_new[0],
        outer_new[1],
        outer_new[2],
    )


def solution(mesh):
    return jax.shard_map(
        body,
        mesh=mesh,
        in_specs=(
            P(("expert", "hidden"), None),
            P(("expert", "hidden"), None),
            P(("expert", "hidden"), None),
            P(("expert", "hidden"), None),
            P(("expert", "hidden")),
            P(("expert", "hidden"), None),
            P(),
            P(),
            P(),
            P("hidden", "expert", None),
            P("hidden", "expert", None),
            P(),
            P(),
            P(),
            P("hidden", "expert", None),
            P("hidden", "expert", None),
            P(),
            P(),
            P(),
            P("hidden", "expert", None),
            P("hidden", "expert", None),
        ),
        out_specs=(
            P(("expert", "hidden"), None),
            P(("expert", "hidden"), None),
            P(),
            P(),
            P(),
            P(),
            P(),
            P(),
            P(),
            P(),
            P(),
            P(),
            P("hidden", "expert", None),
            P("hidden", "expert", None),
            P("hidden", "expert", None),
            P("hidden", "expert", None),
            P("hidden", "expert", None),
            P("hidden", "expert", None),
        ),
        check_vma=False,
    )
```

```python
import functools
import math

import jax
import jax.numpy as jnp
from jax import lax
from jax.experimental import pallas as pl
from jax.experimental.pallas import tpu as pltpu
from jax.sharding import PartitionSpec as P

D = 384
HEADS = 6
HEAD = 64
EXPERTS = 16
TOP = 4
TASKS = 2
CAP = 320


MOMENT_DECAY = 0.9
AVERAGE_DECAY = 0.9
RATE_NORM = 0.23
RATE_QKV = 0.064
RATE_PROJ = 1.4
RATE_INNER = 0.21
RATE_OUTER = 0.73
NORM_EPS = 1e-06
MASKED = -1e30
VMEM_MOST = 67043328


def layer_norm(values):
    center = values - jnp.mean(values, axis=-1, keepdims=True)
    spread = jnp.mean(center * center, axis=-1, keepdims=True)
    return center * lax.rsqrt(spread + NORM_EPS)


def first_norm(values, gain_row, offset_row):
    return layer_norm(values) * gain_row + offset_row


def attend_forward(query_heads, key_heads, value_heads, seg_marks, block_rows):
    score_scale = HEAD ** (-0.5)
    seq_length = query_heads.shape[0]
    outputs = []
    log_sums = []
    for row_start in range(0, seq_length, block_rows):
        query_rows = query_heads[row_start : row_start + block_rows]
        marks_rows = seg_marks[row_start : row_start + block_rows]
        scores = (
            jnp.einsum("qhd,khd->hqk", query_rows, key_heads, preferred_element_type=jnp.float32)
            * score_scale
        )
        scores = jnp.where(marks_rows[None, :, None] == seg_marks[None, None, :], scores, MASKED)
        row_peak = jnp.max(scores, axis=-1, keepdims=True)
        row_exp = jnp.exp(scores - row_peak)
        row_total = jnp.sum(row_exp, axis=-1, keepdims=True)
        weights_low = (row_exp / row_total).astype(jnp.bfloat16)
        mixed_rows = jnp.einsum(
            "hqk,khd->qhd", weights_low, value_heads, preferred_element_type=jnp.float32
        )
        outputs.append(mixed_rows.astype(jnp.bfloat16))
        log_sums.append(row_peak + jnp.log(row_total))
    return (jnp.concatenate(outputs, axis=0), log_sums)


def attend_backward(
    query_heads, key_heads, value_heads, seg_marks, mixed_grad, log_sums, block_rows
):
    score_scale = HEAD ** (-0.5)
    seq_length = query_heads.shape[0]
    key_grad = jnp.zeros(key_heads.shape, jnp.float32)
    value_grad = jnp.zeros(value_heads.shape, jnp.float32)
    query_grads = []
    for block_index in range(seq_length // block_rows):
        row_start = block_index * block_rows
        query_rows = query_heads[row_start : row_start + block_rows]
        marks_rows = seg_marks[row_start : row_start + block_rows]
        grad_rows = mixed_grad[row_start : row_start + block_rows]
        scores = (
            jnp.einsum("qhd,khd->hqk", query_rows, key_heads, preferred_element_type=jnp.float32)
            * score_scale
        )
        scores = jnp.where(marks_rows[None, :, None] == seg_marks[None, None, :], scores, MASKED)
        probs = jnp.exp(scores - log_sums[block_index])
        probs_low = probs.astype(jnp.bfloat16)
        value_grad = value_grad + jnp.einsum(
            "hqk,qhd->khd", probs_low, grad_rows, preferred_element_type=jnp.float32
        )
        prob_grad = jnp.einsum(
            "qhd,khd->hqk", grad_rows, value_heads, preferred_element_type=jnp.float32
        )
        row_dot = jnp.sum(prob_grad * probs, axis=-1, keepdims=True)
        score_grad = (probs * (prob_grad - row_dot)).astype(jnp.bfloat16)
        query_grads.append(
            jnp.einsum("hqk,khd->qhd", score_grad, key_heads, preferred_element_type=jnp.float32)
            * score_scale
        )
        key_grad = (
            key_grad
            + jnp.einsum("hqk,qhd->khd", score_grad, query_rows, preferred_element_type=jnp.float32)
            * score_scale
        )
    return (jnp.concatenate(query_grads, axis=0), key_grad, value_grad)


def route_kernel(first_expert, ids_ref, gates_ref, rows_ref, gate_rows_ref, cols_ref):
    slots, _, tokens = ids_ref.shape
    count = rows_ref.shape[1]
    before = (
        lax.broadcasted_iota(jnp.int32, (tokens, tokens), 0)
        <= lax.broadcasted_iota(jnp.int32, (tokens, tokens), 1)
    )
    before = jnp.where(before, 1.0, 0.0).astype(jnp.bfloat16)
    hot_rows = []
    for slot in range(slots):
        for expert in range(count):
            hot = jnp.zeros((1, tokens), jnp.float32)
            gate = jnp.zeros((1, tokens), jnp.float32)
            name = (first_expert[0] + expert).astype(jnp.float32)
            for choice in range(TOP):
                same = ids_ref[slot, choice : choice + 1, :] == name
                hot = jnp.where(same, 1.0, hot)
                gate = jnp.where(same, gates_ref[slot, choice : choice + 1, :], gate)
            hot_rows.append(hot)
            gate_rows_ref[slot, expert : expert + 1, :] = gate
    hot_all = jnp.concatenate(hot_rows, axis=0)
    place = jnp.dot(hot_all.astype(jnp.bfloat16), before, preferred_element_type=jnp.float32) - 1.0
    place = jnp.where((hot_all > 0.5) & (place < CAP), place, -1.0)
    for slot in range(slots):
        rows_ref[slot] = place[slot * count : (slot + 1) * count].astype(jnp.int32)
    wide = jnp.concatenate([place, jnp.full((128 - place.shape[0], tokens), -1.0, jnp.float32)], axis=0)
    cols_ref[...] = jnp.transpose(wide).astype(jnp.int32)


def route(first_expert, ids_all, gates_all, count):
    slots, _, tokens = ids_all.shape
    vmem = pl.BlockSpec(memory_space=pltpu.VMEM)
    return pl.pallas_call(
        route_kernel,
        out_shape=(
            jax.ShapeDtypeStruct((slots, count, tokens), jnp.int32),
            jax.ShapeDtypeStruct((slots, count, tokens), jnp.float32),
            jax.ShapeDtypeStruct((tokens, 128), jnp.int32),
        ),
        in_specs=[pl.BlockSpec(memory_space=pltpu.SMEM), vmem, vmem],
        out_specs=(vmem, vmem, vmem),
        name="route",
    )(first_expert, ids_all, gates_all)


NT = (((1,), (1,)), ((), ()))
NN = (((1,), (0,)), ((), ()))
TN = (((0,), (0,)), ((), ()))


def mxu(left, right, dims=NN):
    return lax.dot_general(left, right, dims, preferred_element_type=jnp.float32)


def moe_kernel(
    offset, count, has_start, last, chunk, rows_ref, gate_rows_ref, cols_ref, *rest
):
    slots, _, tokens = rows_ref.shape
    rest = list(rest)
    u_refs, g_refs, rest = rest[:slots], rest[slots : 2 * slots], rest[2 * slots :]
    inner_ref, outer_ref, rest = rest[0], rest[1], rest[2:]
    if has_start:
        start_ref, rest = rest[0], rest[1:]
    out_count = 2 * slots if last else 1
    sums_refs, grads_ref, rest = rest[:out_count], rest[out_count], rest[out_count + 1 :]
    x_buf, dy_buf, act_buf, dpre_buf, gate_buf, sum_buf = rest[:6]
    step = pl.program_id(0)
    width = u_refs[0].shape[1]
    units = inner_ref.shape[0]
    for slot in range(slots):
        place = rows_ref[slot, pl.ds(offset + step, 1), :]
        same = lax.broadcasted_iota(jnp.int32, (CAP, tokens), 0) == place
        pick = jnp.where(same, 1.0, 0.0).astype(jnp.bfloat16)
        gate = jnp.sum(
            jnp.where(same, gate_rows_ref[slot, pl.ds(offset + step, 1), :], 0.0), axis=1, keepdims=True
        )
        span = pl.ds(slot * CAP, CAP)
        x_buf[span, :] = mxu(pick, u_refs[slot][...]).astype(jnp.bfloat16)
        dy_buf[span, :] = (gate * mxu(pick, g_refs[slot][...])).astype(jnp.bfloat16)
        gate_buf[span, :] = jnp.broadcast_to(gate, (CAP, 128))

    def part(index, carry):
        at = pl.multiple_of(index * chunk, chunk)
        span = pl.ds(at, chunk)
        rows_in = x_buf[...]
        rows_grad = dy_buf[...]
        pre = mxu(rows_in, inner_ref[span, :], NT)
        act_grad = mxu(rows_grad, outer_ref[span, :], NT)
        phi = 0.5 + 0.5 * lax.erf(pre * math.sqrt(0.5))
        bell = jnp.exp(pre * pre * -0.5) * (1.0 / math.sqrt(2.0 * math.pi))
        act = (pre * phi).astype(jnp.bfloat16)
        dpre = (act_grad * (phi + pre * bell)).astype(jnp.bfloat16)
        act_buf[:, span] = act
        dpre_buf[:, span] = dpre
        grads_ref[span, :width] = mxu(dpre, rows_in, TN).astype(jnp.bfloat16)
        grads_ref[span, width:] = mxu(act, rows_grad, TN).astype(jnp.bfloat16)
        return carry

    lax.fori_loop(0, units // chunk, part, 0)
    result = mxu(act_buf[...], outer_ref[...])
    gate_wide = jnp.concatenate([gate_buf[...]] * (width // 128), axis=1)
    x_buf[...] = (gate_wide * result).astype(jnp.bfloat16)
    dy_buf[...] = mxu(dpre_buf[...], inner_ref[...]).astype(jnp.bfloat16)

    if has_start:
        @pl.when(step == 0)
        def _():
            copy = pltpu.make_async_copy(start_ref, sum_buf, rest[6])
            copy.start()
            copy.wait()

    for slot in range(slots):
        lane = slot * count + offset + step
        wide = lax.broadcasted_iota(jnp.int32, (tokens, 128), 1) == lane
        column = jnp.sum(jnp.where(wide, cols_ref[...], 0), axis=1, keepdims=True)
        same = lax.broadcasted_iota(jnp.int32, (tokens, CAP), 1) == column
        spread = jnp.where(same, 1.0, 0.0).astype(jnp.bfloat16)
        span = pl.ds(slot * CAP, CAP)
        for side, buf in enumerate((x_buf, dy_buf)):
            add = mxu(spread, buf[span, :])
            lanes = slice(side * width, (side + 1) * width)
            if has_start:
                sum_buf[slot, :, lanes] = sum_buf[slot, :, lanes] + add
            else:
                first = jnp.where(step == 0, 0.0, 1.0)
                old = sum_buf[slot, :, lanes]
                sum_buf[slot, :, lanes] = jnp.where(first > 0.5, old, 0.0) + add

    @pl.when(step == pl.num_programs(0) - 1)
    def _():
        if last:
            for slot in range(slots):
                sums_refs[slot][...] = sum_buf[slot, :, width:].astype(jnp.bfloat16)
                sums_refs[slots + slot][...] = sum_buf[slot, :, :width].astype(jnp.bfloat16)
        else:
            sums_refs[0][...] = sum_buf[...]


def moe(rows, gate_rows, cols, u_all, g_all, weights, offset, start, last):
    slots, count, tokens = rows.shape
    width = u_all[0].shape[1]
    units = weights.shape[0]
    steps = weights.shape[1] // (2 * width)
    pairs = slots * CAP
    once = pl.Buffered(1)

    def whole(array):
        return pl.BlockSpec(array.shape, lambda e: (0,) * array.ndim, pipeline_mode=once)

    sums_shape = (slots, tokens, 2 * width)
    scratch = [
        pltpu.VMEM((pairs, width), jnp.bfloat16),
        pltpu.VMEM((pairs, width), jnp.bfloat16),
        pltpu.VMEM((pairs, units), jnp.bfloat16),
        pltpu.VMEM((pairs, units), jnp.bfloat16),
        pltpu.VMEM((pairs, 128), jnp.float32),
        pltpu.VMEM(sums_shape, jnp.float32),
    ]
    operands = [rows, gate_rows, cols, *u_all, *g_all, weights, weights]
    in_specs = [whole(a) for a in operands[:-2]] + [
        pl.BlockSpec((units, width), lambda e: (0, 2 * e)),
        pl.BlockSpec((units, width), lambda e: (0, 2 * e + 1)),
    ]
    if start is not None:
        operands.append(start)
        in_specs.append(pl.BlockSpec(memory_space=pl.ANY))
        scratch.append(pltpu.SemaphoreType.DMA)
    if last:
        sums_out = (jax.ShapeDtypeStruct((tokens, width), jnp.bfloat16),) * (2 * slots)
    else:
        sums_out = (jax.ShapeDtypeStruct(sums_shape, jnp.float32),)
    flops = steps * pairs * width * (12 * units + 8 * tokens)
    return pl.pallas_call(
        functools.partial(moe_kernel, offset, count, start is not None, last, units // 3),
        out_shape=sums_out + (jax.ShapeDtypeStruct((units, steps * 2 * width), jnp.bfloat16),),
        grid_spec=pltpu.PrefetchScalarGridSpec(
            num_scalar_prefetch=0,
            grid=(steps,),
            in_specs=in_specs,
            out_specs=tuple(whole(s) for s in sums_out)
            + (pl.BlockSpec((units, 2 * width), lambda e: (0, e)),),
            scratch_shapes=scratch,
        ),
        compiler_params=pltpu.CompilerParams(
            dimension_semantics=("arbitrary",), vmem_limit_bytes=VMEM_MOST
        ),
        cost_estimate=pl.CostEstimate(flops=flops, bytes_accessed=40 << 20, transcendentals=0),
        name="moe",
    )(*operands)


def to_peers(arrays, groups):
    return [arrays[0]] + [
        lax.ppermute(arrays[k], "expert", [(i, i ^ k) for i in range(groups)]) for k in range(1, groups)
    ]


def butterfly_sum(value, wire):
    sizes = [("hidden", lax.axis_size("hidden")), ("expert", lax.axis_size("expert"))]
    steps = []
    for axis, size in sizes:
        bit = 1
        while bit < size:
            steps.append((axis, size, bit))
            bit *= 2
    steps = steps[:1] + [s for s in steps if s[0] == "expert"] + [s for s in steps[1:] if s[0] == "hidden"]
    value = value.astype(jnp.float32)
    done = []
    for axis, size, bit in steps:
        half = value.shape[0] // 2
        if value.shape[0] % 2 or half % 8:
            break
        done.append((axis, size, bit))
        upper = (lax.axis_index(axis) & bit) > 0
        low_half, high_half = value[:half], value[half:]
        keep = jnp.where(upper, high_half, low_half)
        send = jnp.where(upper, low_half, high_half).astype(wire)
        got = lax.ppermute(send, axis, [(i, i ^ bit) for i in range(size)])
        value = keep + got.astype(jnp.float32)
    for axis, size, bit in steps[len(done):]:
        got = lax.ppermute(value.astype(wire), axis, [(i, i ^ bit) for i in range(size)])
        value = value + got.astype(jnp.float32)
    value = value.astype(wire)
    for axis, size, bit in done[::-1]:
        upper = (lax.axis_index(axis) & bit) > 0
        got = lax.ppermute(value, axis, [(i, i ^ bit) for i in range(size)])
        first = jnp.where(upper, got, value)
        second = jnp.where(upper, value, got)
        value = jnp.concatenate([first, second], axis=0)
    return value.astype(jnp.float32)


def nesterov(weight, moment, average, grad, rate):
    moment_new = MOMENT_DECAY * moment + grad
    weight_new = weight - rate * (grad + MOMENT_DECAY * moment_new)
    average_new = AVERAGE_DECAY * average + (1.0 - AVERAGE_DECAY) * weight_new
    return (weight_new, moment_new, average_new)


def body(
    patches,
    cotangent,
    expert_ids,
    gates,
    task_ids,
    segments,
    norm_params,
    attn_qkv,
    attn_proj,
    expert_inner,
    expert_outer,
    norm_moment,
    qkv_moment,
    proj_moment,
    inner_moment,
    outer_moment,
    norm_average,
    qkv_average,
    proj_average,
    inner_average,
    outer_average,
):
    groups = lax.axis_size("expert")
    tok_count = patches.shape[0]
    tokens_all = tok_count * groups * lax.axis_size("hidden")
    local_count = EXPERTS // groups
    block_rows = min(512, tok_count)
    own_units = expert_inner.shape[0]
    half = local_count // 2 * 2 * D
    both = jnp.stack([expert_inner, expert_outer], axis=2).astype(jnp.bfloat16)
    both = both.reshape(own_units, local_count * 2 * D)
    weights = [
        lax.all_gather(both[:, :half], "hidden", axis=0, tiled=True),
        lax.all_gather(both[:, half:], "hidden", axis=0, tiled=True),
    ]
    table = jnp.concatenate([expert_ids.astype(jnp.float32).T, gates.T], axis=0)
    tables = jnp.stack(to_peers([table] * groups, groups))
    g_all = to_peers([cotangent] * groups, groups)
    first_expert = (lax.axis_index("expert") * local_count).astype(jnp.int32).reshape(1)
    rows, gate_rows, cols = route(first_expert, tables[:, :TOP], tables[:, TOP:], local_count)
    named = jnp.sum(
        (expert_ids[:, :, None] == jnp.arange(EXPERTS, dtype=jnp.int32)).astype(jnp.float32), axis=(0, 1)
    )
    counts = jnp.minimum(named, float(CAP))
    inputs = patches.astype(jnp.float32)
    seg_marks = segments[0]
    normed_one, first_back = jax.vjp(first_norm, inputs, norm_params[0], norm_params[1])
    attn_in = normed_one.astype(jnp.bfloat16)
    qkv_low = attn_qkv.astype(jnp.bfloat16)
    proj_low = attn_proj.astype(jnp.bfloat16)
    joined = jnp.dot(attn_in, qkv_low, preferred_element_type=jnp.float32).astype(jnp.bfloat16)
    joined = joined.reshape(tok_count, 3, HEADS, HEAD)
    query_heads = joined[:, 0]
    key_heads = joined[:, 1]
    value_heads = joined[:, 2]
    mixed, log_sums = attend_forward(query_heads, key_heads, value_heads, seg_marks, block_rows)
    mixed = mixed.reshape(tok_count, D)
    hidden_one = inputs + jnp.dot(mixed, proj_low, preferred_element_type=jnp.float32)
    task_hot = (task_ids[:, None] == jnp.arange(TASKS, dtype=jnp.int32)[None, :]).astype(
        jnp.float32
    )

    def second_norm(values, table):
        gain_rows = jnp.dot(task_hot, table[:TASKS], precision=lax.Precision.HIGHEST)
        bias_rows = jnp.dot(task_hot, table[TASKS:], precision=lax.Precision.HIGHEST)
        return layer_norm(values) * gain_rows + bias_rows

    normed_two, second_back = jax.vjp(second_norm, hidden_one, norm_params[2:])
    moe_in = normed_two.astype(jnp.bfloat16)
    u_all = to_peers([moe_in] * groups, groups)
    sums, grads_first = moe(rows, gate_rows, cols, u_all, g_all, weights[0], 0, None, False)
    *parts, grads_second = moe(
        rows, gate_rows, cols, u_all, g_all, weights[1], local_count // 2, sums, True
    )
    du_parts = to_peers(parts[:groups], groups)
    y_parts = to_peers(parts[groups:], groups)
    moe_grad = sum(p.astype(jnp.float32) for p in du_parts)
    moe_sum = sum(p.astype(jnp.float32) for p in y_parts)
    block_out = (hidden_one + moe_sum).astype(jnp.bfloat16)
    out_grad = cotangent.astype(jnp.float32)
    owned = [
        lax.psum_scatter(g, "hidden", scatter_dimension=0, tiled=True)
        for g in (grads_first, grads_second)
    ]
    owned = jnp.concatenate(owned, axis=1).astype(jnp.float32)
    owned = owned.reshape(own_units, local_count, 2, D)
    inner_grad, outer_grad = owned[:, :, 0], owned[:, :, 1]
    hidden_grad, table_grad = second_back(moe_grad)
    hidden_grad = hidden_grad + out_grad
    attn_grad_low = hidden_grad.astype(jnp.bfloat16)
    proj_grad = jnp.einsum("td,te->de", mixed, attn_grad_low, preferred_element_type=jnp.float32)
    mixed_grad = jnp.einsum(
        "te,de->td", attn_grad_low, proj_low, preferred_element_type=jnp.float32
    )
    mixed_grad = mixed_grad.astype(jnp.bfloat16).reshape(tok_count, HEADS, HEAD)
    query_grad, key_grad, value_grad = attend_backward(
        query_heads, key_heads, value_heads, seg_marks, mixed_grad, log_sums, block_rows
    )
    joined_grad = (
        jnp.stack([query_grad, key_grad, value_grad], axis=1)
        .reshape(tok_count, 3 * D)
        .astype(jnp.bfloat16)
    )
    qkv_grad = jnp.einsum("td,te->de", attn_in, joined_grad, preferred_element_type=jnp.float32)
    attn_in_grad = jnp.einsum("te,de->td", joined_grad, qkv_low, preferred_element_type=jnp.float32)
    input_first, gain_grad, offset_grad = first_back(attn_in_grad)
    patch_grad = hidden_grad + input_first
    norm_grad = jnp.concatenate([gain_grad[None], offset_grad[None], table_grad], axis=0)
    big = jnp.concatenate([qkv_grad, proj_grad], axis=1)
    pad_rows = -big.shape[0] % 512
    big = jnp.concatenate([big, jnp.zeros((pad_rows, big.shape[1]), jnp.float32)], axis=0)
    big_sum = butterfly_sum(big, jnp.bfloat16)[:D]
    qkv_sum, proj_sum = big_sum[:, : 3 * D], big_sum[:, 3 * D :]
    count_row = jnp.pad(counts, (0, D - EXPERTS))[None]
    small = jnp.concatenate([norm_grad, count_row, jnp.zeros((1, D), jnp.float32)], axis=0)
    small_sum = butterfly_sum(small, jnp.float32)
    norm_sum, count_sum = small_sum[:6], small_sum[6, :EXPERTS]
    expert_load = count_sum * (EXPERTS / (tokens_all * TOP))
    root_tokens = math.sqrt(tokens_all)
    norm_new = nesterov(norm_params, norm_moment, norm_average, norm_sum, RATE_NORM / root_tokens)
    qkv_new = nesterov(attn_qkv, qkv_moment, qkv_average, qkv_sum, RATE_QKV / root_tokens)
    proj_new = nesterov(attn_proj, proj_moment, proj_average, proj_sum, RATE_PROJ / root_tokens)
    inner_new = nesterov(
        expert_inner, inner_moment, inner_average, inner_grad, RATE_INNER / root_tokens
    )
    outer_new = nesterov(
        expert_outer, outer_moment, outer_average, outer_grad, RATE_OUTER / root_tokens
    )
    return (
        block_out,
        patch_grad,
        expert_load,
        norm_new[0],
        norm_new[1],
        norm_new[2],
        qkv_new[0],
        qkv_new[1],
        qkv_new[2],
        proj_new[0],
        proj_new[1],
        proj_new[2],
        inner_new[0],
        inner_new[1],
        inner_new[2],
        outer_new[0],
        outer_new[1],
        outer_new[2],
    )


def solution(mesh):
    return jax.shard_map(
        body,
        mesh=mesh,
        in_specs=(
            P(("expert", "hidden"), None),
            P(("expert", "hidden"), None),
            P(("expert", "hidden"), None),
            P(("expert", "hidden"), None),
            P(("expert", "hidden")),
            P(("expert", "hidden"), None),
            P(),
            P(),
            P(),
            P("hidden", "expert", None),
            P("hidden", "expert", None),
            P(),
            P(),
            P(),
            P("hidden", "expert", None),
            P("hidden", "expert", None),
            P(),
            P(),
            P(),
            P("hidden", "expert", None),
            P("hidden", "expert", None),
        ),
        out_specs=(
            P(("expert", "hidden"), None),
            P(("expert", "hidden"), None),
            P(),
            P(),
            P(),
            P(),
            P(),
            P(),
            P(),
            P(),
            P(),
            P(),
            P("hidden", "expert", None),
            P("hidden", "expert", None),
            P("hidden", "expert", None),
            P("hidden", "expert", None),
            P("hidden", "expert", None),
            P("hidden", "expert", None),
        ),
        check_vma=False,
    )
```

```python
import functools
import math

import jax
import jax.numpy as jnp
from jax import lax
from jax.experimental import pallas as pl
from jax.experimental.pallas import tpu as pltpu
from jax.sharding import PartitionSpec as P

D = 384
HEADS = 6
HEAD = 64
EXPERTS = 16
TOP = 4
TASKS = 2
CAP = 320


MOMENT_DECAY = 0.9
AVERAGE_DECAY = 0.9
RATE_NORM = 0.23
RATE_QKV = 0.064
RATE_PROJ = 1.4
RATE_INNER = 0.21
RATE_OUTER = 0.73
NORM_EPS = 1e-06
MASKED = -1e30
VMEM_MOST = 67043328


def route_kernel(first_expert, ids_ref, gates_ref, rows_ref, gate_rows_ref, cols_ref):
    slots, _, tokens = ids_ref.shape
    count = rows_ref.shape[1]
    before = (
        lax.broadcasted_iota(jnp.int32, (tokens, tokens), 0)
        <= lax.broadcasted_iota(jnp.int32, (tokens, tokens), 1)
    )
    before = jnp.where(before, 1.0, 0.0).astype(jnp.bfloat16)
    hot_rows = []
    for slot in range(slots):
        for expert in range(count):
            hot = jnp.zeros((1, tokens), jnp.float32)
            gate = jnp.zeros((1, tokens), jnp.float32)
            name = (first_expert[0] + expert).astype(jnp.float32)
            for choice in range(TOP):
                same = ids_ref[slot, choice : choice + 1, :] == name
                hot = jnp.where(same, 1.0, hot)
                gate = jnp.where(same, gates_ref[slot, choice : choice + 1, :], gate)
            hot_rows.append(hot)
            gate_rows_ref[slot, expert : expert + 1, :] = gate
    hot_all = jnp.concatenate(hot_rows, axis=0)
    place = jnp.dot(hot_all.astype(jnp.bfloat16), before, preferred_element_type=jnp.float32) - 1.0
    place = jnp.where((hot_all > 0.5) & (place < CAP), place, -1.0)
    for slot in range(slots):
        rows_ref[slot] = place[slot * count : (slot + 1) * count].astype(jnp.int32)
    wide = jnp.concatenate([place, jnp.full((128 - place.shape[0], tokens), -1.0, jnp.float32)], axis=0)
    cols_ref[...] = jnp.transpose(wide).astype(jnp.int32)


def route(first_expert, ids_all, gates_all, count):
    slots, _, tokens = ids_all.shape
    vmem = pl.BlockSpec(memory_space=pltpu.VMEM)
    return pl.pallas_call(
        route_kernel,
        out_shape=(
            jax.ShapeDtypeStruct((slots, count, tokens), jnp.int32),
            jax.ShapeDtypeStruct((slots, count, tokens), jnp.float32),
            jax.ShapeDtypeStruct((tokens, 128), jnp.int32),
        ),
        in_specs=[pl.BlockSpec(memory_space=pltpu.SMEM), vmem, vmem],
        out_specs=(vmem, vmem, vmem),
        name="route",
    )(first_expert, ids_all, gates_all)


NT = (((1,), (1,)), ((), ()))
NN = (((1,), (0,)), ((), ()))
TN = (((0,), (0,)), ((), ()))


def mxu(left, right, dims=NN):
    return lax.dot_general(left, right, dims, preferred_element_type=jnp.float32)


def moe_kernel(
    offset, count, has_start, last, chunk, rows_ref, gate_rows_ref, cols_ref, *rest
):
    slots, _, tokens = rows_ref.shape
    rest = list(rest)
    u_refs, g_refs, rest = rest[:slots], rest[slots : 2 * slots], rest[2 * slots :]
    inner_ref, outer_ref, rest = rest[0], rest[1], rest[2:]
    if has_start:
        start_ref, rest = rest[0], rest[1:]
    out_count = 2 * slots if last else 1
    sums_refs, grads_ref, rest = rest[:out_count], rest[out_count], rest[out_count + 1 :]
    x_buf, dy_buf, act_buf, dpre_buf, gate_buf, sum_buf = rest[:6]
    step = pl.program_id(0)
    width = u_refs[0].shape[1]
    units = inner_ref.shape[0]
    for slot in range(slots):
        place = rows_ref[slot, pl.ds(offset + step, 1), :]
        same = lax.broadcasted_iota(jnp.int32, (CAP, tokens), 0) == place
        pick = jnp.where(same, 1.0, 0.0).astype(jnp.bfloat16)
        gate = jnp.sum(
            jnp.where(same, gate_rows_ref[slot, pl.ds(offset + step, 1), :], 0.0), axis=1, keepdims=True
        )
        span = pl.ds(slot * CAP, CAP)
        x_buf[span, :] = mxu(pick, u_refs[slot][...]).astype(jnp.bfloat16)
        dy_buf[span, :] = (gate * mxu(pick, g_refs[slot][...])).astype(jnp.bfloat16)
        gate_buf[span, :] = jnp.broadcast_to(gate, (CAP, 128))

    def part(index, carry):
        at = pl.multiple_of(index * chunk, chunk)
        span = pl.ds(at, chunk)
        rows_in = x_buf[...]
        rows_grad = dy_buf[...]
        pre = mxu(rows_in, inner_ref[span, :], NT)
        act_grad = mxu(rows_grad, outer_ref[span, :], NT)
        phi = 0.5 + 0.5 * lax.erf(pre * math.sqrt(0.5))
        bell = jnp.exp(pre * pre * -0.5) * (1.0 / math.sqrt(2.0 * math.pi))
        act = (pre * phi).astype(jnp.bfloat16)
        dpre = (act_grad * (phi + pre * bell)).astype(jnp.bfloat16)
        act_buf[:, span] = act
        dpre_buf[:, span] = dpre
        grads_ref[span, :width] = mxu(dpre, rows_in, TN).astype(jnp.bfloat16)
        grads_ref[span, width:] = mxu(act, rows_grad, TN).astype(jnp.bfloat16)
        return carry

    lax.fori_loop(0, units // chunk, part, 0)
    result = mxu(act_buf[...], outer_ref[...])
    gate_wide = jnp.concatenate([gate_buf[...]] * (width // 128), axis=1)
    x_buf[...] = (gate_wide * result).astype(jnp.bfloat16)
    dy_buf[...] = mxu(dpre_buf[...], inner_ref[...]).astype(jnp.bfloat16)

    if has_start:
        @pl.when(step == 0)
        def _():
            copy = pltpu.make_async_copy(start_ref, sum_buf, rest[6])
            copy.start()
            copy.wait()

    for slot in range(slots):
        lane = slot * count + offset + step
        wide = lax.broadcasted_iota(jnp.int32, (tokens, 128), 1) == lane
        column = jnp.sum(jnp.where(wide, cols_ref[...], 0), axis=1, keepdims=True)
        same = lax.broadcasted_iota(jnp.int32, (tokens, CAP), 1) == column
        spread = jnp.where(same, 1.0, 0.0).astype(jnp.bfloat16)
        span = pl.ds(slot * CAP, CAP)
        for side, buf in enumerate((x_buf, dy_buf)):
            add = mxu(spread, buf[span, :])
            lanes = slice(side * width, (side + 1) * width)
            if has_start:
                sum_buf[slot, :, lanes] = sum_buf[slot, :, lanes] + add
            else:
                first = jnp.where(step == 0, 0.0, 1.0)
                old = sum_buf[slot, :, lanes]
                sum_buf[slot, :, lanes] = jnp.where(first > 0.5, old, 0.0) + add

    @pl.when(step == pl.num_programs(0) - 1)
    def _():
        if last:
            for slot in range(slots):
                sums_refs[slot][...] = sum_buf[slot, :, width:].astype(jnp.bfloat16)
                sums_refs[slots + slot][...] = sum_buf[slot, :, :width].astype(jnp.bfloat16)
        else:
            sums_refs[0][...] = sum_buf[...]


def moe(rows, gate_rows, cols, u_all, g_all, weights, offset, start, last):
    slots, count, tokens = rows.shape
    width = u_all[0].shape[1]
    units = weights.shape[0]
    steps = weights.shape[1] // (2 * width)
    pairs = slots * CAP
    once = pl.Buffered(1)

    def whole(array):
        return pl.BlockSpec(array.shape, lambda e: (0,) * array.ndim, pipeline_mode=once)

    sums_shape = (slots, tokens, 2 * width)
    scratch = [
        pltpu.VMEM((pairs, width), jnp.bfloat16),
        pltpu.VMEM((pairs, width), jnp.bfloat16),
        pltpu.VMEM((pairs, units), jnp.bfloat16),
        pltpu.VMEM((pairs, units), jnp.bfloat16),
        pltpu.VMEM((pairs, 128), jnp.float32),
        pltpu.VMEM(sums_shape, jnp.float32),
    ]
    operands = [rows, gate_rows, cols, *u_all, *g_all, weights, weights]
    in_specs = [whole(a) for a in operands[:-2]] + [
        pl.BlockSpec((units, width), lambda e: (0, 2 * e)),
        pl.BlockSpec((units, width), lambda e: (0, 2 * e + 1)),
    ]
    if start is not None:
        operands.append(start)
        in_specs.append(pl.BlockSpec(memory_space=pl.ANY))
        scratch.append(pltpu.SemaphoreType.DMA)
    if last:
        sums_out = (jax.ShapeDtypeStruct((tokens, width), jnp.bfloat16),) * (2 * slots)
    else:
        sums_out = (jax.ShapeDtypeStruct(sums_shape, jnp.float32),)
    flops = steps * pairs * width * (12 * units + 8 * tokens)
    return pl.pallas_call(
        functools.partial(moe_kernel, offset, count, start is not None, last, units // 3),
        out_shape=sums_out + (jax.ShapeDtypeStruct((units, steps * 2 * width), jnp.bfloat16),),
        grid_spec=pltpu.PrefetchScalarGridSpec(
            num_scalar_prefetch=0,
            grid=(steps,),
            in_specs=in_specs,
            out_specs=tuple(whole(s) for s in sums_out)
            + (pl.BlockSpec((units, 2 * width), lambda e: (0, e)),),
            scratch_shapes=scratch,
        ),
        compiler_params=pltpu.CompilerParams(
            dimension_semantics=("arbitrary",), vmem_limit_bytes=VMEM_MOST
        ),
        cost_estimate=pl.CostEstimate(flops=flops, bytes_accessed=40 << 20, transcendentals=0),
        name="moe",
    )(*operands)


def unit_rows(values):
    center = values - jnp.mean(values, axis=1, keepdims=True)
    rate = lax.rsqrt(jnp.mean(center * center, axis=1, keepdims=True) + NORM_EPS)
    return center * rate, rate


def unit_rows_back(unit, rate, grad):
    mean_grad = jnp.mean(grad, axis=1, keepdims=True)
    mean_dot = jnp.mean(grad * unit, axis=1, keepdims=True)
    return rate * (grad - mean_grad - unit * mean_dot)


def as_column(row):
    wide = jnp.broadcast_to(row.astype(jnp.float32), (128, row.shape[1]))
    return jnp.transpose(wide)


def key_range(marks_ref, row_start, block, blocks):
    first = marks_ref[row_start]
    last = marks_ref[row_start + block - 1]
    begin = jnp.int32(0)
    end = jnp.int32(0)
    for index in range(blocks):
        begin = begin + jnp.where(marks_ref[index * block + block - 1] < first, 1, 0)
        end = end + jnp.where(marks_ref[index * block] <= last, 1, 0)
    return begin, end


def head_masks(block):
    low_half = lax.broadcasted_iota(jnp.int32, (block, 2 * HEAD), 1) < HEAD
    return low_half, jnp.logical_not(low_half)


def attend_kernel(
    block, marks_ref, x_ref, norm_ref, qkv_ref, proj_ref, seg_ref, task_ref,
    joined_ref, key_t_ref, mixed_ref, mixed_t_ref, logs_ref, hidden_ref, u_ref, value_t, column,
):
    tokens = x_ref.shape[0]
    blocks = tokens // block
    qkv_low = qkv_ref[...].astype(jnp.bfloat16)
    proj_low = proj_ref[...].astype(jnp.bfloat16)
    column[...] = as_column(seg_ref[...])

    def project(index, carry):
        span = pl.ds(pl.multiple_of(index * block, block), block)
        unit, _ = unit_rows(x_ref[span, :].astype(jnp.float32))
        attn_in = (unit * norm_ref[0:1, :] + norm_ref[1:2, :]).astype(jnp.bfloat16)
        joined = mxu(attn_in, qkv_low)
        joined_ref[span, :] = joined.astype(jnp.bfloat16)
        key_t_ref[:, span] = jnp.transpose(joined[:, D : 2 * D]).astype(jnp.bfloat16)
        value_t[:, span] = jnp.transpose(joined[:, 2 * D :]).astype(jnp.bfloat16)
        return carry

    lax.fori_loop(0, blocks, project, 0)

    def rows(index, carry):
        start = pl.multiple_of(index * block, block)
        span = pl.ds(start, block)
        begin, end = key_range(marks_ref, index * block, block, blocks)
        seg_row = seg_ref[:, span].astype(jnp.float32)
        masks = head_masks(block)
        for pair in range(HEADS // 2):
            lanes = slice(pair * 2 * HEAD, (pair + 1) * 2 * HEAD)
            query = joined_ref[span, lanes] * jnp.bfloat16(HEAD ** (-0.5))
            queries = [jnp.where(m, query, jnp.zeros_like(query)) for m in masks]

            def keys(at, state):
                key_span = pl.ds(pl.multiple_of(at * block, block), block)
                key_pair = joined_ref[key_span, D + pair * 2 * HEAD : D + (pair + 1) * 2 * HEAD]
                seg_col = jnp.concatenate([column[key_span, :]] * (block // 128), axis=1)
                same = seg_col == seg_row
                out = []
                for side in range(2):
                    peak, total, acc = state[side]
                    head = 2 * pair + side
                    scores = jnp.where(same, mxu(key_pair, queries[side], NT), MASKED)
                    new_peak = jnp.maximum(peak, jnp.max(scores, axis=0, keepdims=True))
                    weights = jnp.exp(scores - new_peak)
                    fix = jnp.exp(peak - new_peak)
                    total = total * fix + jnp.sum(weights, axis=0, keepdims=True)
                    value = value_t[head * HEAD : (head + 1) * HEAD, key_span]
                    acc = acc * fix + mxu(value, weights.astype(jnp.bfloat16))
                    out.append((new_peak, total, acc))
                return tuple(out)

            zero = (
                jnp.full((1, block), MASKED, jnp.float32),
                jnp.zeros((1, block), jnp.float32),
                jnp.zeros((HEAD, block), jnp.float32),
            )
            done = lax.fori_loop(begin, end, keys, (zero, zero))
            for side in range(2):
                peak, total, acc = done[side]
                head = 2 * pair + side
                mixed_t_ref[head * HEAD : (head + 1) * HEAD, span] = (acc / total).astype(jnp.bfloat16)
                logs_ref[head : head + 1, span] = peak + jnp.log(total)
        mixed = jnp.transpose(mixed_t_ref[:, span].astype(jnp.float32)).astype(jnp.bfloat16)
        mixed_ref[span, :] = mixed
        hidden = x_ref[span, :].astype(jnp.float32) + mxu(mixed, proj_low)
        hidden_ref[span, :] = hidden
        task = jnp.concatenate([as_column(task_ref[:, span])] * (D // 128), axis=1) > 0.5
        gain = jnp.where(task, norm_ref[3:4, :], norm_ref[2:3, :])
        bias = jnp.where(task, norm_ref[5:6, :], norm_ref[4:5, :])
        unit, _ = unit_rows(hidden)
        u_ref[span, :] = (unit * gain + bias).astype(jnp.bfloat16)
        return carry

    lax.fori_loop(0, blocks, rows, 0)


def attend(marks, x, norm, qkv, proj, seg, task):
    tokens = x.shape[0]
    block = min(256, tokens)
    vmem = pl.BlockSpec(memory_space=pltpu.VMEM)
    low = jnp.bfloat16
    return pl.pallas_call(
        functools.partial(attend_kernel, block),
        out_shape=(
            jax.ShapeDtypeStruct((tokens, 3 * D), low),
            jax.ShapeDtypeStruct((D, tokens), low),
            jax.ShapeDtypeStruct((tokens, D), low),
            jax.ShapeDtypeStruct((D, tokens), low),
            jax.ShapeDtypeStruct((8, tokens), jnp.float32),
            jax.ShapeDtypeStruct((tokens, D), jnp.float32),
            jax.ShapeDtypeStruct((tokens, D), low),
        ),
        in_specs=[pl.BlockSpec(memory_space=pltpu.SMEM)] + [vmem] * 6,
        out_specs=(vmem,) * 7,
        scratch_shapes=[pltpu.VMEM((D, tokens), low), pltpu.VMEM((tokens, 128), jnp.float32)],
        compiler_params=pltpu.CompilerParams(vmem_limit_bytes=48 << 20),
        cost_estimate=pl.CostEstimate(flops=8 << 30, bytes_accessed=12 << 20, transcendentals=6 << 20),
        name="attend",
    )(marks, x, norm, qkv, proj, seg, task)


def attend_back_kernel(
    block, slots, marks_ref, x_ref, norm_ref, qkv_ref, proj_ref, seg_ref, task_ref, out_grad_ref,
    joined_ref, key_t_ref, mixed_ref, mixed_t_ref, logs_ref, hidden_ref, *rest
):
    du_refs, rest = rest[:slots], rest[slots:]
    patch_ref, weight_ref, norms_ref, grads, attn_in, key_grad, value_grad, column = rest
    tokens = x_ref.shape[0]
    blocks = tokens // block
    qkv_low = qkv_ref[...].astype(jnp.bfloat16)
    proj_low = proj_ref[...].astype(jnp.bfloat16)
    column[...] = as_column(seg_ref[...])
    key_grad[...] = jnp.zeros_like(key_grad)
    value_grad[...] = jnp.zeros_like(value_grad)
    norms_ref[...] = jnp.zeros_like(norms_ref)
    weight_ref[...] = jnp.zeros_like(weight_ref)

    def rows(index, carry):
        start = pl.multiple_of(index * block, block)
        span = pl.ds(start, block)
        du = du_refs[0][span, :].astype(jnp.float32)
        for ref in du_refs[1:]:
            du = du + ref[span, :].astype(jnp.float32)
        task = jnp.concatenate([as_column(task_ref[:, span])] * (D // 128), axis=1) > 0.5
        gain = jnp.where(task, norm_ref[3:4, :], norm_ref[2:3, :])
        unit, rate = unit_rows(hidden_ref[span, :])
        first = jnp.where(task, 0.0, du)
        second = jnp.where(task, du, 0.0)
        norms_ref[2:3, :] += jnp.sum(first * unit, axis=0, keepdims=True)
        norms_ref[3:4, :] += jnp.sum(second * unit, axis=0, keepdims=True)
        norms_ref[4:5, :] += jnp.sum(first, axis=0, keepdims=True)
        norms_ref[5:6, :] += jnp.sum(second, axis=0, keepdims=True)
        hidden_grad = out_grad_ref[span, :].astype(jnp.float32) + unit_rows_back(unit, rate, du * gain)
        patch_ref[span, :] = hidden_grad
        grad_low = hidden_grad.astype(jnp.bfloat16)
        weight_ref[D:, D:] += mxu(mixed_ref[span, :], grad_low, TN)
        mixed_grad = mxu(grad_low, proj_low, NT).astype(jnp.bfloat16)
        mixed_grad_t = mxu(proj_low, grad_low, NT).astype(jnp.bfloat16).astype(jnp.float32)
        dots = mixed_grad_t * mixed_t_ref[:, span].astype(jnp.float32)
        begin, end = key_range(marks_ref, index * block, block, blocks)
        seg_row = seg_ref[:, span].astype(jnp.float32)
        masks = head_masks(block)
        query_grads = []
        for pair in range(HEADS // 2):
            lanes = slice(pair * 2 * HEAD, (pair + 1) * 2 * HEAD)
            query = joined_ref[span, lanes] * jnp.bfloat16(HEAD ** (-0.5))
            queries = [jnp.where(m, query, jnp.zeros_like(query)) for m in masks]
            grad_pair = mixed_grad[:, lanes]
            out_grads = [jnp.where(m, grad_pair, jnp.zeros_like(grad_pair)) for m in masks]
            deltas = []
            logs = []
            for side in range(2):
                head = 2 * pair + side
                deltas.append(jnp.sum(dots[head * HEAD : (head + 1) * HEAD], axis=0, keepdims=True))
                logs.append(logs_ref[head : head + 1, span])

            def keys(at, state):
                key_span = pl.ds(pl.multiple_of(at * block, block), block)
                key_pair = joined_ref[key_span, D + pair * 2 * HEAD : D + (pair + 1) * 2 * HEAD]
                value_pair = joined_ref[key_span, 2 * D + pair * 2 * HEAD : 2 * D + (pair + 1) * 2 * HEAD]
                seg_col = jnp.concatenate([column[key_span, :]] * (block // 128), axis=1)
                same = seg_col == seg_row
                out = []
                key_sum = key_grad[key_span, lanes]
                value_sum = value_grad[key_span, lanes]
                for side in range(2):
                    head = 2 * pair + side
                    scores = jnp.where(same, mxu(key_pair, queries[side], NT), MASKED)
                    probs = jnp.exp(scores - logs[side])
                    prob_grad = mxu(value_pair, out_grads[side], NT)
                    score_grad = (probs * (prob_grad - deltas[side])).astype(jnp.bfloat16)
                    value_sum = value_sum + mxu(probs.astype(jnp.bfloat16), out_grads[side])
                    key_sum = key_sum + mxu(score_grad, queries[side])
                    key_t = key_t_ref[head * HEAD : (head + 1) * HEAD, key_span]
                    out.append(state[side] + mxu(key_t, score_grad))
                key_grad[key_span, lanes] = key_sum
                value_grad[key_span, lanes] = value_sum
                return tuple(out)

            zero = jnp.zeros((HEAD, block), jnp.float32)
            query_grads.extend(lax.fori_loop(begin, end, keys, (zero, zero)))
        query_grad_t = jnp.concatenate(query_grads, axis=0) * HEAD ** (-0.5)
        grads[span, :D] = jnp.transpose(query_grad_t).astype(jnp.bfloat16)
        return carry

    lax.fori_loop(0, blocks, rows, 0)

    def finish(index, carry):
        span = pl.ds(pl.multiple_of(index * block, block), block)
        grads[span, D : 2 * D] = key_grad[span, :].astype(jnp.bfloat16)
        grads[span, 2 * D :] = value_grad[span, :].astype(jnp.bfloat16)
        unit, rate = unit_rows(x_ref[span, :].astype(jnp.float32))
        attn_in[span, :] = (unit * norm_ref[0:1, :] + norm_ref[1:2, :]).astype(jnp.bfloat16)
        joined_grad = grads[span, :]
        in_grad = mxu(joined_grad, qkv_low, NT)
        norms_ref[0:1, :] += jnp.sum(in_grad * unit, axis=0, keepdims=True)
        norms_ref[1:2, :] += jnp.sum(in_grad, axis=0, keepdims=True)
        patch_ref[span, :] += unit_rows_back(unit, rate, in_grad * norm_ref[0:1, :])
        return carry

    lax.fori_loop(0, blocks, finish, 0)
    weight_ref[:D, :] = mxu(attn_in[...], grads[:, : 2 * D], TN)
    weight_ref[D:, :D] = mxu(attn_in[...], grads[:, 2 * D :], TN)


def attend_back(marks, x, norm, qkv, proj, seg, task, out_grad, saved, du_parts):
    tokens = x.shape[0]
    block = min(256, tokens)
    vmem = pl.BlockSpec(memory_space=pltpu.VMEM)
    operands = [marks, x, norm, qkv, proj, seg, task, out_grad, *saved, *du_parts]
    return pl.pallas_call(
        functools.partial(attend_back_kernel, block, len(du_parts)),
        out_shape=(
            jax.ShapeDtypeStruct((tokens, D), jnp.float32),
            jax.ShapeDtypeStruct((2 * D, 2 * D), jnp.float32),
            jax.ShapeDtypeStruct((8, D), jnp.float32),
        ),
        in_specs=[pl.BlockSpec(memory_space=pltpu.SMEM)] + [vmem] * (len(operands) - 1),
        out_specs=(vmem,) * 3,
        scratch_shapes=[
            pltpu.VMEM((tokens, 3 * D), jnp.bfloat16),
            pltpu.VMEM((tokens, D), jnp.bfloat16),
            pltpu.VMEM((tokens, D), jnp.float32),
            pltpu.VMEM((tokens, D), jnp.float32),
            pltpu.VMEM((tokens, 128), jnp.float32),
        ],
        compiler_params=pltpu.CompilerParams(vmem_limit_bytes=52 << 20),
        cost_estimate=pl.CostEstimate(flops=24 << 30, bytes_accessed=24 << 20, transcendentals=6 << 20),
        name="attend_back",
    )(*operands)


def to_peers(arrays, groups):
    return [arrays[0]] + [
        lax.ppermute(arrays[k], "expert", [(i, i ^ k) for i in range(groups)]) for k in range(1, groups)
    ]


def butterfly_sum(value, wire):
    sizes = [("hidden", lax.axis_size("hidden")), ("expert", lax.axis_size("expert"))]
    steps = []
    for axis, size in sizes:
        bit = 1
        while bit < size:
            steps.append((axis, size, bit))
            bit *= 2
    steps = steps[:1] + [s for s in steps if s[0] == "expert"] + [s for s in steps[1:] if s[0] == "hidden"]
    value = value.astype(jnp.float32)
    done = []
    for axis, size, bit in steps:
        half = value.shape[0] // 2
        if value.shape[0] % 2 or half % 8:
            break
        done.append((axis, size, bit))
        upper = (lax.axis_index(axis) & bit) > 0
        low_half, high_half = value[:half], value[half:]
        keep = jnp.where(upper, high_half, low_half)
        send = jnp.where(upper, low_half, high_half).astype(wire)
        got = lax.ppermute(send, axis, [(i, i ^ bit) for i in range(size)])
        value = keep + got.astype(jnp.float32)
    for axis, size, bit in steps[len(done):]:
        got = lax.ppermute(value.astype(wire), axis, [(i, i ^ bit) for i in range(size)])
        value = value + got.astype(jnp.float32)
    value = value.astype(wire)
    for axis, size, bit in done[::-1]:
        upper = (lax.axis_index(axis) & bit) > 0
        got = lax.ppermute(value, axis, [(i, i ^ bit) for i in range(size)])
        first = jnp.where(upper, got, value)
        second = jnp.where(upper, value, got)
        value = jnp.concatenate([first, second], axis=0)
    return value.astype(jnp.float32)


def nesterov(weight, moment, average, grad, rate):
    moment_new = MOMENT_DECAY * moment + grad
    weight_new = weight - rate * (grad + MOMENT_DECAY * moment_new)
    average_new = AVERAGE_DECAY * average + (1.0 - AVERAGE_DECAY) * weight_new
    return (weight_new, moment_new, average_new)


def body(
    patches,
    cotangent,
    expert_ids,
    gates,
    task_ids,
    segments,
    norm_params,
    attn_qkv,
    attn_proj,
    expert_inner,
    expert_outer,
    norm_moment,
    qkv_moment,
    proj_moment,
    inner_moment,
    outer_moment,
    norm_average,
    qkv_average,
    proj_average,
    inner_average,
    outer_average,
):
    groups = lax.axis_size("expert")
    tok_count = patches.shape[0]
    tokens_all = tok_count * groups * lax.axis_size("hidden")
    local_count = EXPERTS // groups
    own_units = expert_inner.shape[0]
    half = local_count // 2 * 2 * D
    both = jnp.stack([expert_inner, expert_outer], axis=2).astype(jnp.bfloat16)
    both = both.reshape(own_units, local_count * 2 * D)
    weights = [
        lax.all_gather(both[:, :half], "hidden", axis=0, tiled=True),
        lax.all_gather(both[:, half:], "hidden", axis=0, tiled=True),
    ]
    table = jnp.concatenate([expert_ids.astype(jnp.float32).T, gates.T], axis=0)
    tables = jnp.stack(to_peers([table] * groups, groups))
    g_all = to_peers([cotangent] * groups, groups)
    first_expert = (lax.axis_index("expert") * local_count).astype(jnp.int32).reshape(1)
    rows, gate_rows, cols = route(first_expert, tables[:, :TOP], tables[:, TOP:], local_count)
    named = jnp.sum(
        (expert_ids[:, :, None] == jnp.arange(EXPERTS, dtype=jnp.int32)).astype(jnp.float32), axis=(0, 1)
    )
    counts = jnp.minimum(named, float(CAP))
    marks = segments[0]
    task_row = task_ids[None]
    *saved, moe_in = attend(marks, patches, norm_params, attn_qkv, attn_proj, segments, task_row)
    hidden_one = saved[-1]
    u_all = to_peers([moe_in] * groups, groups)
    sums, grads_first = moe(rows, gate_rows, cols, u_all, g_all, weights[0], 0, None, False)
    *parts, grads_second = moe(
        rows, gate_rows, cols, u_all, g_all, weights[1], local_count // 2, sums, True
    )
    du_parts = to_peers(parts[:groups], groups)
    y_parts = to_peers(parts[groups:], groups)
    moe_sum = sum(p.astype(jnp.float32) for p in y_parts)
    block_out = (hidden_one + moe_sum).astype(jnp.bfloat16)
    owned = [
        lax.psum_scatter(g, "hidden", scatter_dimension=0, tiled=True)
        for g in (grads_first, grads_second)
    ]
    owned = jnp.concatenate(owned, axis=1).astype(jnp.float32)
    owned = owned.reshape(own_units, local_count, 2, D)
    inner_grad, outer_grad = owned[:, :, 0], owned[:, :, 1]
    patch_grad, big, norm_grad = attend_back(
        marks, patches, norm_params, attn_qkv, attn_proj, segments, task_row, cotangent, saved, du_parts
    )
    big_sum = butterfly_sum(big, jnp.bfloat16)
    qkv_sum = jnp.concatenate([big_sum[:D], big_sum[D:, :D]], axis=1)
    proj_sum = big_sum[D:, D:]
    count_row = jnp.pad(counts, (0, D - EXPERTS))[None]
    small = jnp.concatenate([norm_grad[:6], count_row, jnp.zeros((1, D), jnp.float32)], axis=0)
    small_sum = butterfly_sum(small, jnp.float32)
    norm_sum, count_sum = small_sum[:6], small_sum[6, :EXPERTS]
    expert_load = count_sum * (EXPERTS / (tokens_all * TOP))
    root_tokens = math.sqrt(tokens_all)
    norm_new = nesterov(norm_params, norm_moment, norm_average, norm_sum, RATE_NORM / root_tokens)
    qkv_new = nesterov(attn_qkv, qkv_moment, qkv_average, qkv_sum, RATE_QKV / root_tokens)
    proj_new = nesterov(attn_proj, proj_moment, proj_average, proj_sum, RATE_PROJ / root_tokens)
    inner_new = nesterov(
        expert_inner, inner_moment, inner_average, inner_grad, RATE_INNER / root_tokens
    )
    outer_new = nesterov(
        expert_outer, outer_moment, outer_average, outer_grad, RATE_OUTER / root_tokens
    )
    return (
        block_out,
        patch_grad,
        expert_load,
        norm_new[0],
        norm_new[1],
        norm_new[2],
        qkv_new[0],
        qkv_new[1],
        qkv_new[2],
        proj_new[0],
        proj_new[1],
        proj_new[2],
        inner_new[0],
        inner_new[1],
        inner_new[2],
        outer_new[0],
        outer_new[1],
        outer_new[2],
    )


def solution(mesh):
    return jax.shard_map(
        body,
        mesh=mesh,
        in_specs=(
            P(("expert", "hidden"), None),
            P(("expert", "hidden"), None),
            P(("expert", "hidden"), None),
            P(("expert", "hidden"), None),
            P(("expert", "hidden")),
            P(("expert", "hidden"), None),
            P(),
            P(),
            P(),
            P("hidden", "expert", None),
            P("hidden", "expert", None),
            P(),
            P(),
            P(),
            P("hidden", "expert", None),
            P("hidden", "expert", None),
            P(),
            P(),
            P(),
            P("hidden", "expert", None),
            P("hidden", "expert", None),
        ),
        out_specs=(
            P(("expert", "hidden"), None),
            P(("expert", "hidden"), None),
            P(),
            P(),
            P(),
            P(),
            P(),
            P(),
            P(),
            P(),
            P(),
            P(),
            P("hidden", "expert", None),
            P("hidden", "expert", None),
            P("hidden", "expert", None),
            P("hidden", "expert", None),
            P("hidden", "expert", None),
            P("hidden", "expert", None),
        ),
        check_vma=False,
    )
```

```python
import functools
import math

import jax
import jax.numpy as jnp
from jax import lax
from jax.experimental import pallas as pl
from jax.experimental.pallas import tpu as pltpu
from jax.sharding import PartitionSpec as P

D = 384
HEADS = 6
HEAD = 64
EXPERTS = 16
TOP = 4
CAP = 320


MOMENT_DECAY = 0.9
AVERAGE_DECAY = 0.9
RATE_NORM = 0.23
RATE_QKV = 0.064
RATE_PROJ = 1.4
RATE_INNER = 0.21
RATE_OUTER = 0.73
NORM_EPS = 1e-06
MASKED = -1e30
VMEM_MOST = 67043328
DIGITS = 9


def route_kernel(first_expert, ids_ref, gates_ref, rows_ref, gate_rows_ref, cols_ref):
    slots, _, tokens = ids_ref.shape
    count = rows_ref.shape[1]
    before = (
        lax.broadcasted_iota(jnp.int32, (tokens, tokens), 0)
        <= lax.broadcasted_iota(jnp.int32, (tokens, tokens), 1)
    )
    before = jnp.where(before, 1.0, 0.0).astype(jnp.bfloat16)
    hot_rows = []
    for slot in range(slots):
        for expert in range(count):
            hot = jnp.zeros((1, tokens), jnp.float32)
            gate = jnp.zeros((1, tokens), jnp.float32)
            name = (first_expert[0] + expert).astype(jnp.float32)
            for choice in range(TOP):
                same = ids_ref[slot, choice : choice + 1, :] == name
                hot = jnp.where(same, 1.0, hot)
                gate = jnp.where(same, gates_ref[slot, choice : choice + 1, :], gate)
            hot_rows.append(hot)
            gate_rows_ref[slot, expert : expert + 1, :] = gate
    hot_all = jnp.concatenate(hot_rows, axis=0)
    place = jnp.dot(hot_all.astype(jnp.bfloat16), before, preferred_element_type=jnp.float32) - 1.0
    place = jnp.where((hot_all > 0.5) & (place < CAP), place, -1.0)
    for slot in range(slots):
        rows_ref[slot] = place[slot * count : (slot + 1) * count].astype(jnp.int32)
    wide = jnp.concatenate([place, jnp.full((128 - place.shape[0], tokens), -1.0, jnp.float32)], axis=0)
    cols_ref[...] = jnp.transpose(wide).astype(jnp.int32)


def route(first_expert, ids_all, gates_all, count):
    slots, _, tokens = ids_all.shape
    vmem = pl.BlockSpec(memory_space=pltpu.VMEM)
    return pl.pallas_call(
        route_kernel,
        out_shape=(
            jax.ShapeDtypeStruct((slots, count, tokens), jnp.int32),
            jax.ShapeDtypeStruct((slots, count, tokens), jnp.float32),
            jax.ShapeDtypeStruct((tokens, 128), jnp.int32),
        ),
        in_specs=[pl.BlockSpec(memory_space=pltpu.SMEM), vmem, vmem],
        out_specs=(vmem, vmem, vmem),
        name="route",
    )(first_expert, ids_all, gates_all)


NT = (((1,), (1,)), ((), ()))
NN = (((1,), (0,)), ((), ()))
TN = (((0,), (0,)), ((), ()))


def mxu(left, right, dims=NN):
    return lax.dot_general(left, right, dims, preferred_element_type=jnp.float32)


def moe_kernel(
    offset, count, has_start, last, chunk, rows_ref, gate_rows_ref, cols_ref, *rest
):
    slots, _, tokens = rows_ref.shape
    rest = list(rest)
    u_refs, g_refs, rest = rest[:slots], rest[slots : 2 * slots], rest[2 * slots :]
    inner_ref, outer_ref, rest = rest[0], rest[1], rest[2:]
    if has_start:
        start_ref, rest = rest[0], rest[1:]
    out_count = 2 * slots if last else 1
    sums_refs, grads_ref, rest = rest[:out_count], rest[out_count], rest[out_count + 1 :]
    x_buf, dy_buf, act_buf, dpre_buf, gate_buf, sum_buf = rest[:6]
    step = pl.program_id(0)
    width = u_refs[0].shape[1]
    units = inner_ref.shape[0]
    for slot in range(slots):
        place = rows_ref[slot, pl.ds(offset + step, 1), :]
        same = lax.broadcasted_iota(jnp.int32, (CAP, tokens), 0) == place
        pick = jnp.where(same, 1.0, 0.0).astype(jnp.bfloat16)
        gate = jnp.sum(
            jnp.where(same, gate_rows_ref[slot, pl.ds(offset + step, 1), :], 0.0), axis=1, keepdims=True
        )
        span = pl.ds(slot * CAP, CAP)
        x_buf[span, :] = mxu(pick, u_refs[slot][...]).astype(jnp.bfloat16)
        dy_buf[span, :] = (gate * mxu(pick, g_refs[slot][...])).astype(jnp.bfloat16)
        gate_buf[span, :] = jnp.broadcast_to(gate, (CAP, 128))

    def part(index, carry):
        at = pl.multiple_of(index * chunk, chunk)
        span = pl.ds(at, chunk)
        rows_in = x_buf[...]
        rows_grad = dy_buf[...]
        pre = mxu(rows_in, inner_ref[span, :], NT)
        act_grad = mxu(rows_grad, outer_ref[span, :], NT)
        phi = 0.5 + 0.5 * lax.erf(pre * math.sqrt(0.5))
        bell = jnp.exp(pre * pre * -0.5) * (1.0 / math.sqrt(2.0 * math.pi))
        act = (pre * phi).astype(jnp.bfloat16)
        dpre = (act_grad * (phi + pre * bell)).astype(jnp.bfloat16)
        act_buf[:, span] = act
        dpre_buf[:, span] = dpre
        grads_ref[span, :width] = mxu(dpre, rows_in, TN).astype(jnp.bfloat16)
        grads_ref[span, width:] = mxu(act, rows_grad, TN).astype(jnp.bfloat16)
        return carry

    lax.fori_loop(0, units // chunk, part, 0)
    result = mxu(act_buf[...], outer_ref[...])
    gate_wide = jnp.concatenate([gate_buf[...]] * (width // 128), axis=1)
    x_buf[...] = (gate_wide * result).astype(jnp.bfloat16)
    dy_buf[...] = mxu(dpre_buf[...], inner_ref[...]).astype(jnp.bfloat16)

    if has_start:
        @pl.when(step == 0)
        def _():
            copy = pltpu.make_async_copy(start_ref, sum_buf, rest[6])
            copy.start()
            copy.wait()

    for slot in range(slots):
        lane = slot * count + offset + step
        wide = lax.broadcasted_iota(jnp.int32, (tokens, 128), 1) == lane
        column = jnp.sum(jnp.where(wide, cols_ref[...], 0), axis=1, keepdims=True)
        same = lax.broadcasted_iota(jnp.int32, (tokens, CAP), 1) == column
        spread = jnp.where(same, 1.0, 0.0).astype(jnp.bfloat16)
        span = pl.ds(slot * CAP, CAP)
        for side, buf in enumerate((x_buf, dy_buf)):
            add = mxu(spread, buf[span, :])
            lanes = slice(side * width, (side + 1) * width)
            if has_start:
                sum_buf[slot, :, lanes] = sum_buf[slot, :, lanes] + add
            else:
                first = jnp.where(step == 0, 0.0, 1.0)
                old = sum_buf[slot, :, lanes]
                sum_buf[slot, :, lanes] = jnp.where(first > 0.5, old, 0.0) + add

    @pl.when(step == pl.num_programs(0) - 1)
    def _():
        if last:
            for slot in range(slots):
                sums_refs[slot][...] = sum_buf[slot, :, width:].astype(jnp.bfloat16)
                sums_refs[slots + slot][...] = sum_buf[slot, :, :width].astype(jnp.bfloat16)
        else:
            sums_refs[0][...] = sum_buf[...]


def moe(rows, gate_rows, cols, u_all, g_all, weights, offset, start, last):
    slots, count, tokens = rows.shape
    width = u_all[0].shape[1]
    units = weights.shape[0]
    steps = weights.shape[1] // (2 * width)
    pairs = slots * CAP
    once = pl.Buffered(1)

    def whole(array):
        return pl.BlockSpec(array.shape, lambda e: (0,) * array.ndim, pipeline_mode=once)

    sums_shape = (slots, tokens, 2 * width)
    scratch = [
        pltpu.VMEM((pairs, width), jnp.bfloat16),
        pltpu.VMEM((pairs, width), jnp.bfloat16),
        pltpu.VMEM((pairs, units), jnp.bfloat16),
        pltpu.VMEM((pairs, units), jnp.bfloat16),
        pltpu.VMEM((pairs, 128), jnp.float32),
        pltpu.VMEM(sums_shape, jnp.float32),
    ]
    operands = [rows, gate_rows, cols, *u_all, *g_all, weights, weights]
    in_specs = [whole(a) for a in operands[:-2]] + [
        pl.BlockSpec((units, width), lambda e: (0, 2 * e)),
        pl.BlockSpec((units, width), lambda e: (0, 2 * e + 1)),
    ]
    if start is not None:
        operands.append(start)
        in_specs.append(pl.BlockSpec(memory_space=pl.ANY))
        scratch.append(pltpu.SemaphoreType.DMA)
    if last:
        sums_out = (jax.ShapeDtypeStruct((tokens, width), jnp.bfloat16),) * (2 * slots)
    else:
        sums_out = (jax.ShapeDtypeStruct(sums_shape, jnp.float32),)
    flops = steps * pairs * width * (12 * units + 8 * tokens)
    return pl.pallas_call(
        functools.partial(moe_kernel, offset, count, start is not None, last, units // 3),
        out_shape=sums_out + (jax.ShapeDtypeStruct((units, steps * 2 * width), jnp.bfloat16),),
        grid_spec=pltpu.PrefetchScalarGridSpec(
            num_scalar_prefetch=0,
            grid=(steps,),
            in_specs=in_specs,
            out_specs=tuple(whole(s) for s in sums_out)
            + (pl.BlockSpec((units, 2 * width), lambda e: (0, e)),),
            scratch_shapes=scratch,
        ),
        compiler_params=pltpu.CompilerParams(
            dimension_semantics=("arbitrary",), vmem_limit_bytes=VMEM_MOST
        ),
        cost_estimate=pl.CostEstimate(flops=flops, bytes_accessed=40 << 20, transcendentals=0),
        name="moe",
    )(*operands)


def unit_rows(values):
    center = values - jnp.mean(values, axis=1, keepdims=True)
    rate = lax.rsqrt(jnp.mean(center * center, axis=1, keepdims=True) + NORM_EPS)
    return center * rate, rate


def unit_rows_back(unit, rate, grad):
    mean_grad = jnp.mean(grad, axis=1, keepdims=True)
    mean_dot = jnp.mean(grad * unit, axis=1, keepdims=True)
    return rate * (grad - mean_grad - unit * mean_dot)


def as_column(row):
    wide = jnp.broadcast_to(row.astype(jnp.float32), (128, row.shape[1]))
    return jnp.transpose(wide)


def key_range(marks_ref, row_start, block, blocks):
    first = marks_ref[row_start]
    last = marks_ref[row_start + block - 1]
    begin = jnp.int32(0)
    end = jnp.int32(0)
    for index in range(blocks):
        begin = begin + jnp.where(marks_ref[index * block + block - 1] < first, 1, 0)
        end = end + jnp.where(marks_ref[index * block] <= last, 1, 0)
    return begin, end


def head_masks(block):
    low_half = lax.broadcasted_iota(jnp.int32, (block, 2 * HEAD), 1) < HEAD
    return low_half, jnp.logical_not(low_half)


def attend_kernel(
    block, marks_ref, x_ref, norm_ref, qkv_ref, proj_ref, seg_ref, task_ref,
    joined_ref, key_t_ref, mixed_ref, mixed_t_ref, logs_ref, hidden_ref, u_ref, value_t, column,
):
    tokens = x_ref.shape[0]
    blocks = tokens // block
    qkv_low = qkv_ref[...].astype(jnp.bfloat16)
    proj_low = proj_ref[...].astype(jnp.bfloat16)
    column[...] = as_column(seg_ref[...])

    def project(index, carry):
        span = pl.ds(pl.multiple_of(index * block, block), block)
        unit, _ = unit_rows(x_ref[span, :].astype(jnp.float32))
        attn_in = (unit * norm_ref[0:1, :] + norm_ref[1:2, :]).astype(jnp.bfloat16)
        joined = mxu(attn_in, qkv_low)
        joined_ref[span, :] = joined.astype(jnp.bfloat16)
        key_t_ref[:, span] = jnp.transpose(joined[:, D : 2 * D]).astype(jnp.bfloat16)
        value_t[:, span] = jnp.transpose(joined[:, 2 * D :]).astype(jnp.bfloat16)
        return carry

    lax.fori_loop(0, blocks, project, 0)

    def rows(index, carry):
        start = pl.multiple_of(index * block, block)
        span = pl.ds(start, block)
        begin, end = key_range(marks_ref, index * block, block, blocks)
        seg_row = seg_ref[:, span].astype(jnp.float32)
        masks = head_masks(block)
        for pair in range(HEADS // 2):
            lanes = slice(pair * 2 * HEAD, (pair + 1) * 2 * HEAD)
            query = joined_ref[span, lanes] * jnp.bfloat16(HEAD ** (-0.5))
            queries = [jnp.where(m, query, jnp.zeros_like(query)) for m in masks]

            def keys(at, state):
                key_span = pl.ds(pl.multiple_of(at * block, block), block)
                key_pair = joined_ref[key_span, D + pair * 2 * HEAD : D + (pair + 1) * 2 * HEAD]
                seg_col = jnp.concatenate([column[key_span, :]] * (block // 128), axis=1)
                same = seg_col == seg_row
                out = []
                for side in range(2):
                    peak, total, acc = state[side]
                    head = 2 * pair + side
                    scores = jnp.where(same, mxu(key_pair, queries[side], NT), MASKED)
                    new_peak = jnp.maximum(peak, jnp.max(scores, axis=0, keepdims=True))
                    weights = jnp.exp(scores - new_peak)
                    fix = jnp.exp(peak - new_peak)
                    total = total * fix + jnp.sum(weights, axis=0, keepdims=True)
                    value = value_t[head * HEAD : (head + 1) * HEAD, key_span]
                    acc = acc * fix + mxu(value, weights.astype(jnp.bfloat16))
                    out.append((new_peak, total, acc))
                return tuple(out)

            zero = (
                jnp.full((1, block), MASKED, jnp.float32),
                jnp.zeros((1, block), jnp.float32),
                jnp.zeros((HEAD, block), jnp.float32),
            )
            done = lax.fori_loop(begin, end, keys, (zero, zero))
            for side in range(2):
                peak, total, acc = done[side]
                head = 2 * pair + side
                mixed_t_ref[head * HEAD : (head + 1) * HEAD, span] = (acc / total).astype(jnp.bfloat16)
                logs_ref[head : head + 1, span] = peak + jnp.log(total)
        mixed = jnp.transpose(mixed_t_ref[:, span].astype(jnp.float32)).astype(jnp.bfloat16)
        mixed_ref[span, :] = mixed
        hidden = x_ref[span, :].astype(jnp.float32) + mxu(mixed, proj_low)
        hidden_ref[span, :] = hidden
        task = jnp.concatenate([as_column(task_ref[:, span])] * (D // 128), axis=1) > 0.5
        gain = jnp.where(task, norm_ref[3:4, :], norm_ref[2:3, :])
        bias = jnp.where(task, norm_ref[5:6, :], norm_ref[4:5, :])
        unit, _ = unit_rows(hidden)
        u_ref[span, :] = (unit * gain + bias).astype(jnp.bfloat16)
        return carry

    lax.fori_loop(0, blocks, rows, 0)


def attend(marks, x, norm, qkv, proj, seg, task):
    tokens = x.shape[0]
    block = min(256, tokens)
    vmem = pl.BlockSpec(memory_space=pltpu.VMEM)
    low = jnp.bfloat16
    return pl.pallas_call(
        functools.partial(attend_kernel, block),
        out_shape=(
            jax.ShapeDtypeStruct((tokens, 3 * D), low),
            jax.ShapeDtypeStruct((D, tokens), low),
            jax.ShapeDtypeStruct((tokens, D), low),
            jax.ShapeDtypeStruct((D, tokens), low),
            jax.ShapeDtypeStruct((8, tokens), jnp.float32),
            jax.ShapeDtypeStruct((tokens, D), jnp.float32),
            jax.ShapeDtypeStruct((tokens, D), low),
        ),
        in_specs=[pl.BlockSpec(memory_space=pltpu.SMEM)] + [vmem] * 6,
        out_specs=(vmem,) * 7,
        scratch_shapes=[pltpu.VMEM((D, tokens), low), pltpu.VMEM((tokens, 128), jnp.float32)],
        compiler_params=pltpu.CompilerParams(vmem_limit_bytes=48 << 20),
        cost_estimate=pl.CostEstimate(flops=8 << 30, bytes_accessed=12 << 20, transcendentals=6 << 20),
        name="attend",
    )(marks, x, norm, qkv, proj, seg, task)


def attend_back_kernel(
    block, slots, marks_ref, x_ref, norm_ref, qkv_ref, proj_ref, seg_ref, task_ref, out_grad_ref,
    joined_ref, key_t_ref, mixed_ref, mixed_t_ref, logs_ref, hidden_ref, *rest
):
    du_refs, digits_ref, rest = rest[:slots], rest[slots], rest[slots + 1 :]
    patch_ref, weight_ref, grads, attn_in, norms_ref, key_grad, value_grad, column = rest
    tokens = x_ref.shape[0]
    blocks = tokens // block
    qkv_low = qkv_ref[...].astype(jnp.bfloat16)
    proj_low = proj_ref[...].astype(jnp.bfloat16)
    column[...] = as_column(seg_ref[...])
    key_grad[...] = jnp.zeros_like(key_grad)
    value_grad[...] = jnp.zeros_like(value_grad)
    norms_ref[...] = jnp.zeros_like(norms_ref)
    weight_ref[...] = jnp.zeros_like(weight_ref)

    def rows(index, carry):
        start = pl.multiple_of(index * block, block)
        span = pl.ds(start, block)
        du = du_refs[0][span, :].astype(jnp.float32)
        for ref in du_refs[1:]:
            du = du + ref[span, :].astype(jnp.float32)
        task = jnp.concatenate([as_column(task_ref[:, span])] * (D // 128), axis=1) > 0.5
        gain = jnp.where(task, norm_ref[3:4, :], norm_ref[2:3, :])
        unit, rate = unit_rows(hidden_ref[span, :])
        first = jnp.where(task, 0.0, du)
        second = jnp.where(task, du, 0.0)
        norms_ref[2:3, :] += jnp.sum(first * unit, axis=0, keepdims=True)
        norms_ref[3:4, :] += jnp.sum(second * unit, axis=0, keepdims=True)
        norms_ref[4:5, :] += jnp.sum(first, axis=0, keepdims=True)
        norms_ref[5:6, :] += jnp.sum(second, axis=0, keepdims=True)
        hidden_grad = out_grad_ref[span, :].astype(jnp.float32) + unit_rows_back(unit, rate, du * gain)
        patch_ref[span, :] = hidden_grad
        grad_low = hidden_grad.astype(jnp.bfloat16)
        weight_ref[D:, D : 2 * D] += mxu(mixed_ref[span, :], grad_low, TN)
        mixed_grad = mxu(grad_low, proj_low, NT).astype(jnp.bfloat16)
        mixed_grad_t = mxu(proj_low, grad_low, NT).astype(jnp.bfloat16).astype(jnp.float32)
        dots = mixed_grad_t * mixed_t_ref[:, span].astype(jnp.float32)
        begin, end = key_range(marks_ref, index * block, block, blocks)
        seg_row = seg_ref[:, span].astype(jnp.float32)
        masks = head_masks(block)
        query_grads = []
        for pair in range(HEADS // 2):
            lanes = slice(pair * 2 * HEAD, (pair + 1) * 2 * HEAD)
            query = joined_ref[span, lanes] * jnp.bfloat16(HEAD ** (-0.5))
            queries = [jnp.where(m, query, jnp.zeros_like(query)) for m in masks]
            grad_pair = mixed_grad[:, lanes]
            out_grads = [jnp.where(m, grad_pair, jnp.zeros_like(grad_pair)) for m in masks]
            deltas = []
            logs = []
            for side in range(2):
                head = 2 * pair + side
                deltas.append(jnp.sum(dots[head * HEAD : (head + 1) * HEAD], axis=0, keepdims=True))
                logs.append(logs_ref[head : head + 1, span])

            def keys(at, state):
                key_span = pl.ds(pl.multiple_of(at * block, block), block)
                key_pair = joined_ref[key_span, D + pair * 2 * HEAD : D + (pair + 1) * 2 * HEAD]
                value_pair = joined_ref[key_span, 2 * D + pair * 2 * HEAD : 2 * D + (pair + 1) * 2 * HEAD]
                seg_col = jnp.concatenate([column[key_span, :]] * (block // 128), axis=1)
                same = seg_col == seg_row
                out = []
                key_sum = key_grad[key_span, lanes]
                value_sum = value_grad[key_span, lanes]
                for side in range(2):
                    head = 2 * pair + side
                    scores = jnp.where(same, mxu(key_pair, queries[side], NT), MASKED)
                    probs = jnp.exp(scores - logs[side])
                    prob_grad = mxu(value_pair, out_grads[side], NT)
                    score_grad = (probs * (prob_grad - deltas[side])).astype(jnp.bfloat16)
                    value_sum = value_sum + mxu(probs.astype(jnp.bfloat16), out_grads[side])
                    key_sum = key_sum + mxu(score_grad, queries[side])
                    key_t = key_t_ref[head * HEAD : (head + 1) * HEAD, key_span]
                    out.append(state[side] + mxu(key_t, score_grad))
                key_grad[key_span, lanes] = key_sum
                value_grad[key_span, lanes] = value_sum
                return tuple(out)

            zero = jnp.zeros((HEAD, block), jnp.float32)
            query_grads.extend(lax.fori_loop(begin, end, keys, (zero, zero)))
        query_grad_t = jnp.concatenate(query_grads, axis=0) * HEAD ** (-0.5)
        grads[span, :D] = jnp.transpose(query_grad_t).astype(jnp.bfloat16)
        return carry

    lax.fori_loop(0, blocks, rows, 0)

    def finish(index, carry):
        span = pl.ds(pl.multiple_of(index * block, block), block)
        grads[span, D : 2 * D] = key_grad[span, :].astype(jnp.bfloat16)
        grads[span, 2 * D :] = value_grad[span, :].astype(jnp.bfloat16)
        unit, rate = unit_rows(x_ref[span, :].astype(jnp.float32))
        attn_in[span, :] = (unit * norm_ref[0:1, :] + norm_ref[1:2, :]).astype(jnp.bfloat16)
        joined_grad = grads[span, :]
        in_grad = mxu(joined_grad, qkv_low, NT)
        norms_ref[0:1, :] += jnp.sum(in_grad * unit, axis=0, keepdims=True)
        norms_ref[1:2, :] += jnp.sum(in_grad, axis=0, keepdims=True)
        patch_ref[span, :] += unit_rows_back(unit, rate, in_grad * norm_ref[0:1, :])
        return carry

    lax.fori_loop(0, blocks, finish, 0)
    weight_ref[:D, : 2 * D] = mxu(attn_in[...], grads[:, : 2 * D], TN)
    weight_ref[D:, :D] = mxu(attn_in[...], grads[:, 2 * D :], TN)
    for part in range(D // 128):
        weight_ref[part * 8 : part * 8 + 8, 2 * D :] = norms_ref[:, part * 128 : (part + 1) * 128]
    weight_ref[24 : 24 + digits_ref.shape[0], 2 * D :] = digits_ref[...]


def attend_back(marks, x, norm, qkv, proj, seg, task, out_grad, saved, du_parts, digits):
    tokens = x.shape[0]
    block = min(256, tokens)
    vmem = pl.BlockSpec(memory_space=pltpu.VMEM)
    operands = [marks, x, norm, qkv, proj, seg, task, out_grad, *saved, *du_parts, digits]
    return pl.pallas_call(
        functools.partial(attend_back_kernel, block, len(du_parts)),
        out_shape=(
            jax.ShapeDtypeStruct((tokens, D), jnp.float32),
            jax.ShapeDtypeStruct((2 * D, 2 * D + 128), jnp.float32),
        ),
        in_specs=[pl.BlockSpec(memory_space=pltpu.SMEM)] + [vmem] * (len(operands) - 1),
        out_specs=(vmem,) * 2,
        scratch_shapes=[
            pltpu.VMEM((tokens, 3 * D), jnp.bfloat16),
            pltpu.VMEM((tokens, D), jnp.bfloat16),
            pltpu.VMEM((8, D), jnp.float32),
            pltpu.VMEM((tokens, D), jnp.float32),
            pltpu.VMEM((tokens, D), jnp.float32),
            pltpu.VMEM((tokens, 128), jnp.float32),
        ],
        compiler_params=pltpu.CompilerParams(vmem_limit_bytes=52 << 20),
        cost_estimate=pl.CostEstimate(flops=24 << 30, bytes_accessed=24 << 20, transcendentals=6 << 20),
        name="attend_back",
    )(*operands)


def to_peers(arrays, groups):
    return [arrays[0]] + [
        lax.ppermute(arrays[k], "expert", [(i, i ^ k) for i in range(groups)]) for k in range(1, groups)
    ]


def butterfly_sum(value, wire):
    sizes = [("hidden", lax.axis_size("hidden")), ("expert", lax.axis_size("expert"))]
    steps = []
    for axis, size in sizes:
        bit = 1
        while bit < size:
            steps.append((axis, size, bit))
            bit *= 2
    steps = steps[:1] + [s for s in steps if s[0] == "expert"] + [s for s in steps[1:] if s[0] == "hidden"]
    value = value.astype(jnp.float32)
    done = []
    for axis, size, bit in steps:
        half = value.shape[0] // 2
        if value.shape[0] % 2 or half % 8:
            break
        done.append((axis, size, bit))
        upper = (lax.axis_index(axis) & bit) > 0
        low_half, high_half = value[:half], value[half:]
        keep = jnp.where(upper, high_half, low_half)
        send = jnp.where(upper, low_half, high_half).astype(wire)
        got = lax.ppermute(send, axis, [(i, i ^ bit) for i in range(size)])
        value = keep + got.astype(jnp.float32)
    for axis, size, bit in steps[len(done):]:
        got = lax.ppermute(value.astype(wire), axis, [(i, i ^ bit) for i in range(size)])
        value = value + got.astype(jnp.float32)
    value = value.astype(wire)
    for axis, size, bit in done[::-1]:
        upper = (lax.axis_index(axis) & bit) > 0
        got = lax.ppermute(value, axis, [(i, i ^ bit) for i in range(size)])
        first = jnp.where(upper, got, value)
        second = jnp.where(upper, value, got)
        value = jnp.concatenate([first, second], axis=0)
    return value.astype(jnp.float32)


def nesterov(weight, moment, average, grad, rate):
    moment_new = MOMENT_DECAY * moment + grad
    weight_new = weight - rate * (grad + MOMENT_DECAY * moment_new)
    average_new = AVERAGE_DECAY * average + (1.0 - AVERAGE_DECAY) * weight_new
    return (weight_new, moment_new, average_new)


def body(
    patches,
    cotangent,
    expert_ids,
    gates,
    task_ids,
    segments,
    norm_params,
    attn_qkv,
    attn_proj,
    expert_inner,
    expert_outer,
    norm_moment,
    qkv_moment,
    proj_moment,
    inner_moment,
    outer_moment,
    norm_average,
    qkv_average,
    proj_average,
    inner_average,
    outer_average,
):
    groups = lax.axis_size("expert")
    tok_count = patches.shape[0]
    tokens_all = tok_count * groups * lax.axis_size("hidden")
    local_count = EXPERTS // groups
    own_units = expert_inner.shape[0]
    half = local_count // 2 * 2 * D
    both = jnp.stack([expert_inner, expert_outer], axis=2).astype(jnp.bfloat16)
    both = both.reshape(own_units, local_count * 2 * D)
    weights = [
        lax.all_gather(both[:, :half], "hidden", axis=0, tiled=True),
        lax.all_gather(both[:, half:], "hidden", axis=0, tiled=True),
    ]
    table = jnp.concatenate([expert_ids.astype(jnp.float32).T, gates.T], axis=0)
    tables = to_peers([table] * groups, groups)
    g_all = to_peers([cotangent] * groups, groups)
    first_expert = (lax.axis_index("expert") * local_count).astype(jnp.int32).reshape(1)
    tables = jnp.stack(tables)
    rows, gate_rows, cols = route(first_expert, tables[:, :TOP], tables[:, TOP:], local_count)
    named = jnp.sum(
        (expert_ids[:, :, None] == jnp.arange(EXPERTS, dtype=jnp.int32)).astype(jnp.int32), axis=(0, 1)
    )
    counts = jnp.minimum(named, CAP)
    digits = (counts[None, :] >> jnp.arange(16, dtype=jnp.int32)[:, None]) & 1
    digits = jnp.pad(digits.astype(jnp.float32), ((0, 0), (0, 128 - EXPERTS)))
    marks = segments[0]
    task_row = task_ids[None]
    *saved, moe_in = attend(marks, patches, norm_params, attn_qkv, attn_proj, segments, task_row)
    hidden_one = saved[-1]
    u_all = to_peers([moe_in] * groups, groups)
    sums, grads_first = moe(rows, gate_rows, cols, u_all, g_all, weights[0], 0, None, False)
    *parts, grads_second = moe(
        rows, gate_rows, cols, u_all, g_all, weights[1], local_count // 2, sums, True
    )
    du_parts = to_peers(parts[:groups], groups)
    y_parts = to_peers(parts[groups:], groups)
    moe_sum = sum(p.astype(jnp.float32) for p in y_parts)
    block_out = (hidden_one + moe_sum).astype(jnp.bfloat16)
    owned = []
    for grads in (grads_first, grads_second):
        owned.append(lax.psum_scatter(grads, "hidden", scatter_dimension=0, tiled=True))
    owned = jnp.concatenate(owned, axis=1).astype(jnp.float32)
    owned = owned.reshape(own_units, local_count, 2, D)
    inner_grad, outer_grad = owned[:, :, 0], owned[:, :, 1]
    patch_grad, big = attend_back(
        marks, patches, norm_params, attn_qkv, attn_proj, segments, task_row, cotangent, saved,
        du_parts, digits,
    )
    big_sum = butterfly_sum(big, jnp.bfloat16)
    qkv_sum = jnp.concatenate([big_sum[:D, : 2 * D], big_sum[D:, :D]], axis=1)
    proj_sum = big_sum[D:, D : 2 * D]
    extra = big_sum[:, 2 * D :]
    norm_sum = jnp.concatenate([extra[8 * p : 8 * p + 6] for p in range(D // 128)], axis=1)
    powers = 2.0 ** jnp.arange(DIGITS, dtype=jnp.float32)
    count_sum = jnp.sum(extra[24 : 24 + DIGITS, :EXPERTS] * powers[:, None], axis=0)
    expert_load = count_sum * (EXPERTS / (tokens_all * TOP))
    root_tokens = math.sqrt(tokens_all)
    norm_new = nesterov(norm_params, norm_moment, norm_average, norm_sum, RATE_NORM / root_tokens)
    qkv_new = nesterov(attn_qkv, qkv_moment, qkv_average, qkv_sum, RATE_QKV / root_tokens)
    proj_new = nesterov(attn_proj, proj_moment, proj_average, proj_sum, RATE_PROJ / root_tokens)
    inner_new = nesterov(
        expert_inner, inner_moment, inner_average, inner_grad, RATE_INNER / root_tokens
    )
    outer_new = nesterov(
        expert_outer, outer_moment, outer_average, outer_grad, RATE_OUTER / root_tokens
    )
    return (
        block_out,
        patch_grad,
        expert_load,
        norm_new[0],
        norm_new[1],
        norm_new[2],
        qkv_new[0],
        qkv_new[1],
        qkv_new[2],
        proj_new[0],
        proj_new[1],
        proj_new[2],
        inner_new[0],
        inner_new[1],
        inner_new[2],
        outer_new[0],
        outer_new[1],
        outer_new[2],
    )


def solution(mesh):
    return jax.shard_map(
        body,
        mesh=mesh,
        in_specs=(
            P(("expert", "hidden"), None),
            P(("expert", "hidden"), None),
            P(("expert", "hidden"), None),
            P(("expert", "hidden"), None),
            P(("expert", "hidden")),
            P(("expert", "hidden"), None),
            P(),
            P(),
            P(),
            P("hidden", "expert", None),
            P("hidden", "expert", None),
            P(),
            P(),
            P(),
            P("hidden", "expert", None),
            P("hidden", "expert", None),
            P(),
            P(),
            P(),
            P("hidden", "expert", None),
            P("hidden", "expert", None),
        ),
        out_specs=(
            P(("expert", "hidden"), None),
            P(("expert", "hidden"), None),
            P(),
            P(),
            P(),
            P(),
            P(),
            P(),
            P(),
            P(),
            P(),
            P(),
            P("hidden", "expert", None),
            P("hidden", "expert", None),
            P("hidden", "expert", None),
            P("hidden", "expert", None),
            P("hidden", "expert", None),
            P("hidden", "expert", None),
        ),
        check_vma=False,
    )
```

```python
import functools
import math

import jax
import jax.numpy as jnp
from jax import lax
from jax.experimental import pallas as pl
from jax.experimental.pallas import tpu as pltpu
from jax.sharding import PartitionSpec as P

D = 384
HEADS = 6
HEAD = 64
EXPERTS = 16
TOP = 4
CAP = 320


MOMENT_DECAY = 0.9
AVERAGE_DECAY = 0.9
RATE_NORM = 0.23
RATE_QKV = 0.064
RATE_PROJ = 1.4
RATE_INNER = 0.21
RATE_OUTER = 0.73
NORM_EPS = 1e-06
MASKED = -1e30
VMEM_MOST = 67043328
DIGITS = 9


def route_kernel(first_expert, ids_ref, gates_ref, rows_ref, gate_rows_ref, cols_ref):
    slots, _, tokens = ids_ref.shape
    count = rows_ref.shape[1]
    before = (
        lax.broadcasted_iota(jnp.int32, (tokens, tokens), 0)
        <= lax.broadcasted_iota(jnp.int32, (tokens, tokens), 1)
    )
    before = jnp.where(before, 1.0, 0.0).astype(jnp.bfloat16)
    hot_rows = []
    for slot in range(slots):
        for expert in range(count):
            hot = jnp.zeros((1, tokens), jnp.float32)
            gate = jnp.zeros((1, tokens), jnp.float32)
            name = (first_expert[0] + expert).astype(jnp.float32)
            for choice in range(TOP):
                same = ids_ref[slot, choice : choice + 1, :] == name
                hot = jnp.where(same, 1.0, hot)
                gate = jnp.where(same, gates_ref[slot, choice : choice + 1, :], gate)
            hot_rows.append(hot)
            gate_rows_ref[slot, expert : expert + 1, :] = gate
    hot_all = jnp.concatenate(hot_rows, axis=0)
    place = jnp.dot(hot_all.astype(jnp.bfloat16), before, preferred_element_type=jnp.float32) - 1.0
    place = jnp.where((hot_all > 0.5) & (place < CAP), place, -1.0)
    for slot in range(slots):
        rows_ref[slot] = place[slot * count : (slot + 1) * count].astype(jnp.int32)
    wide = jnp.concatenate([place, jnp.full((128 - place.shape[0], tokens), -1.0, jnp.float32)], axis=0)
    cols_ref[...] = jnp.transpose(wide).astype(jnp.int32)


def route(first_expert, ids_all, gates_all, count):
    slots, _, tokens = ids_all.shape
    vmem = pl.BlockSpec(memory_space=pltpu.VMEM)
    return pl.pallas_call(
        route_kernel,
        out_shape=(
            jax.ShapeDtypeStruct((slots, count, tokens), jnp.int32),
            jax.ShapeDtypeStruct((slots, count, tokens), jnp.float32),
            jax.ShapeDtypeStruct((tokens, 128), jnp.int32),
        ),
        in_specs=[pl.BlockSpec(memory_space=pltpu.SMEM), vmem, vmem],
        out_specs=(vmem, vmem, vmem),
        name="route",
    )(first_expert, ids_all, gates_all)


NT = (((1,), (1,)), ((), ()))
NN = (((1,), (0,)), ((), ()))
TN = (((0,), (0,)), ((), ()))


def mxu(left, right, dims=NN):
    return lax.dot_general(left, right, dims, preferred_element_type=jnp.float32)


def dispatch(rows_ref, gate_rows_ref, u_refs, g_refs, lane, x_out, dy_out, gate_out):
    slots, _, tokens = rows_ref.shape
    for slot in range(slots):
        place = rows_ref[slot, pl.ds(lane, 1), :]
        same = lax.broadcasted_iota(jnp.int32, (CAP, tokens), 0) == place
        pick = jnp.where(same, 1.0, 0.0).astype(jnp.bfloat16)
        gate = jnp.sum(jnp.where(same, gate_rows_ref[slot, pl.ds(lane, 1), :], 0.0), axis=1, keepdims=True)
        span = pl.ds(slot * CAP, CAP)
        x_out[span, :] = mxu(pick, u_refs[slot][...]).astype(jnp.bfloat16)
        dy_out[span, :] = (gate * mxu(pick, g_refs[slot][...])).astype(jnp.bfloat16)
        gate_out[span, :] = jnp.broadcast_to(gate, (CAP, 128))


def combine(cols_ref, lanes, step, buf, sum_buf, fresh):
    tokens = cols_ref.shape[0]
    for slot, lane in enumerate(lanes):
        wide = lax.broadcasted_iota(jnp.int32, (tokens, 128), 1) == lane
        column = jnp.sum(jnp.where(wide, cols_ref[...], 0), axis=1, keepdims=True)
        same = lax.broadcasted_iota(jnp.int32, (tokens, CAP), 1) == column
        spread = jnp.where(same, 1.0, 0.0).astype(jnp.bfloat16)
        add = mxu(spread, buf[pl.ds(slot * CAP, CAP), :])
        old = sum_buf[slot]
        if fresh:
            old = jnp.where(step > 0, old, 0.0)
        sum_buf[slot] = old + add


def gelu_pair(pre, act_grad):
    phi = 0.5 + 0.5 * lax.erf(pre * math.sqrt(0.5))
    bell = jnp.exp(pre * pre * -0.5) * (1.0 / math.sqrt(2.0 * math.pi))
    return (pre * phi).astype(jnp.bfloat16), (act_grad * (phi + pre * bell)).astype(jnp.bfloat16)


def times_gate(gate, result):
    gate_wide = jnp.concatenate([gate] * (result.shape[1] // 128), axis=1)
    return (gate_wide * result).astype(jnp.bfloat16)


def slot_lanes(slots, count, offset, step):
    return [slot * count + offset + step for slot in range(slots)]


def moe_full_kernel(offset, chunk, slots, rows_ref, gate_rows_ref, cols_ref, *rest):
    u_refs, g_refs, rest = rest[:slots], rest[slots : 2 * slots], rest[2 * slots :]
    inner_ref, outer_ref, y_ref, du_ref, grads_ref = rest[:5]
    x_buf, dy_buf, act_buf, dpre_buf, gate_buf, y_buf, du_buf = rest[5:]
    step = pl.program_id(0)
    width = inner_ref.shape[1]
    dispatch(rows_ref, gate_rows_ref, u_refs, g_refs, offset + step, x_buf, dy_buf, gate_buf)

    def part(index, carry):
        span = pl.ds(pl.multiple_of(index * chunk, chunk), chunk)
        rows_in = x_buf[...]
        rows_grad = dy_buf[...]
        act, dpre = gelu_pair(mxu(rows_in, inner_ref[span, :], NT), mxu(rows_grad, outer_ref[span, :], NT))
        act_buf[:, span] = act
        dpre_buf[:, span] = dpre
        grads_ref[span, :width] = mxu(dpre, rows_in, TN).astype(jnp.bfloat16)
        grads_ref[span, width:] = mxu(act, rows_grad, TN).astype(jnp.bfloat16)
        return carry

    lax.fori_loop(0, inner_ref.shape[0] // chunk, part, 0)
    x_buf[...] = times_gate(gate_buf[...], mxu(act_buf[...], outer_ref[...]))
    dy_buf[...] = mxu(dpre_buf[...], inner_ref[...]).astype(jnp.bfloat16)
    lanes = slot_lanes(slots, rows_ref.shape[1], offset, step)
    combine(cols_ref, lanes, step, x_buf, y_buf, True)
    combine(cols_ref, lanes, step, dy_buf, du_buf, True)

    @pl.when(step == pl.num_programs(0) - 1)
    def _():
        y_ref[...] = y_buf[...]
        du_ref[...] = du_buf[...]


def fetch(start_ref, sum_buf, sem):
    @pl.when(pl.program_id(0) == 0)
    def _():
        copy = pltpu.make_async_copy(start_ref, sum_buf, sem)
        copy.start()
        copy.wait()


def finish_sums(out_refs, sum_buf):
    @pl.when(pl.program_id(0) == pl.num_programs(0) - 1)
    def _():
        for slot, ref in enumerate(out_refs):
            ref[...] = sum_buf[slot].astype(jnp.bfloat16)


def moe_front_kernel(offset, chunk, slots, rows_ref, gate_rows_ref, cols_ref, *rest):
    u_refs, g_refs, rest = rest[:slots], rest[slots : 2 * slots], rest[2 * slots :]
    inner_ref, outer_ref, start_ref, rest = rest[0], rest[1], rest[2], rest[3:]
    du_refs, rest = rest[:slots], rest[slots:]
    x_ref, dy_ref, gate_ref, act_ref, dpre_ref, buf, sum_buf, sem = rest
    step = pl.program_id(0)
    fetch(start_ref, sum_buf, sem)
    dispatch(rows_ref, gate_rows_ref, u_refs, g_refs, offset + step, x_ref, dy_ref, gate_ref)

    def part(index, carry):
        span = pl.ds(pl.multiple_of(index * chunk, chunk), chunk)
        act, dpre = gelu_pair(mxu(x_ref[...], inner_ref[span, :], NT), mxu(dy_ref[...], outer_ref[span, :], NT))
        act_ref[:, span] = act
        dpre_ref[:, span] = dpre
        return carry

    lax.fori_loop(0, inner_ref.shape[0] // chunk, part, 0)
    buf[...] = mxu(dpre_ref[...], inner_ref[...]).astype(jnp.bfloat16)
    combine(cols_ref, slot_lanes(slots, rows_ref.shape[1], offset, step), step, buf, sum_buf, False)
    finish_sums(du_refs, sum_buf)


def moe_rest_kernel(offset, chunk, slots, count, cols_ref, x_ref, dy_ref, gate_ref, act_ref, dpre_ref, *rest):
    outer_ref, start_ref, rest = rest[0], rest[1], rest[2:]
    y_refs, rest = rest[:slots], rest[slots:]
    grads_ref, buf, sum_buf, sem = rest
    step = pl.program_id(0)
    width = x_ref.shape[1]
    fetch(start_ref, sum_buf, sem)

    def part(index, carry):
        span = pl.ds(pl.multiple_of(index * chunk, chunk), chunk)
        grads_ref[span, :width] = mxu(dpre_ref[:, span], x_ref[...], TN).astype(jnp.bfloat16)
        grads_ref[span, width:] = mxu(act_ref[:, span], dy_ref[...], TN).astype(jnp.bfloat16)
        return carry

    lax.fori_loop(0, outer_ref.shape[0] // chunk, part, 0)
    buf[...] = times_gate(gate_ref[...], mxu(act_ref[...], outer_ref[...]))
    combine(cols_ref, slot_lanes(slots, count, offset, step), step, buf, sum_buf, False)
    finish_sums(y_refs, sum_buf)


def once(array):
    return pl.BlockSpec(array.shape, lambda e: (0,) * len(array.shape), pipeline_mode=pl.Buffered(1))


def moe_call(kernel, steps, operands, in_specs, outs, out_specs, scratch, flops):
    return pl.pallas_call(
        kernel,
        out_shape=tuple(outs),
        grid_spec=pltpu.PrefetchScalarGridSpec(
            num_scalar_prefetch=0, grid=(steps,), in_specs=in_specs, out_specs=tuple(out_specs),
            scratch_shapes=scratch,
        ),
        compiler_params=pltpu.CompilerParams(
            dimension_semantics=("arbitrary",), vmem_limit_bytes=VMEM_MOST
        ),
        cost_estimate=pl.CostEstimate(flops=flops, bytes_accessed=40 << 20, transcendentals=0),
    )(*operands)


def moe_sizes(slots, tokens, weights, width):
    units = weights.shape[0]
    steps = weights.shape[1] // (2 * width)
    pairs = slots * CAP
    low, full = jnp.bfloat16, jnp.float32
    sums = jax.ShapeDtypeStruct((slots, tokens, width), full)
    part = jax.ShapeDtypeStruct((tokens, width), low)
    inner = pl.BlockSpec((units, width), lambda e: (0, 2 * e))
    outer = pl.BlockSpec((units, width), lambda e: (0, 2 * e + 1))
    grads = jax.ShapeDtypeStruct((units, steps * 2 * width), low)
    grads_spec = pl.BlockSpec((units, 2 * width), lambda e: (0, e))
    return units, steps, pairs, sums, part, inner, outer, grads, grads_spec


def moe_full(rows, gate_rows, cols, u_all, g_all, weights, offset):
    slots, _, tokens = rows.shape
    width = u_all[0].shape[1]
    units, steps, pairs, sums, _, inner, outer, grads, grads_spec = moe_sizes(slots, tokens, weights, width)
    operands = [rows, gate_rows, cols, *u_all, *g_all, weights, weights]
    low, full = jnp.bfloat16, jnp.float32
    scratch = [pltpu.VMEM((pairs, width), low)] * 2 + [pltpu.VMEM((pairs, units), low)] * 2
    scratch += [pltpu.VMEM((pairs, 128), full)] + [pltpu.VMEM(sums.shape, full)] * 2
    return moe_call(
        functools.partial(moe_full_kernel, offset, units // 3, slots), steps, operands,
        [once(a) for a in operands[:-2]] + [inner, outer],
        [sums, sums, grads], [once(sums), once(sums), grads_spec], scratch,
        steps * pairs * width * (12 * units + 8 * tokens),
    )


def moe_front(rows, gate_rows, cols, u_all, g_all, weights, offset, start):
    slots, _, tokens = rows.shape
    width = u_all[0].shape[1]
    units, steps, pairs, sums, part, inner, outer, _, _ = moe_sizes(slots, tokens, weights, width)
    operands = [rows, gate_rows, cols, *u_all, *g_all, weights, weights, start]
    low, full = jnp.bfloat16, jnp.float32
    kept = [((pairs, width), low), ((pairs, width), low), ((pairs, 128), full)]
    kept += [((pairs, units), low), ((pairs, units), low)]
    outs = [part] * slots + [jax.ShapeDtypeStruct((steps,) + shape, kind) for shape, kind in kept]
    specs = [once(part)] * slots
    specs += [pl.BlockSpec((pl.Squeezed(),) + shape, lambda e: (e, 0, 0)) for shape, _ in kept]
    return moe_call(
        functools.partial(moe_front_kernel, offset, units // 3, slots), steps, operands,
        [once(a) for a in operands[:-3]] + [inner, outer, pl.BlockSpec(memory_space=pl.ANY)],
        outs, specs,
        [pltpu.VMEM((pairs, width), low), pltpu.VMEM(sums.shape, full), pltpu.SemaphoreType.DMA],
        steps * pairs * width * (6 * units + 6 * tokens),
    )


def moe_rest(cols, kept, weights, offset, count, start):
    slots, tokens, width = start.shape
    units, steps, pairs, sums, part, _, outer, grads, grads_spec = moe_sizes(slots, tokens, weights, width)
    operands = [cols, *kept, weights, start]
    low, full = jnp.bfloat16, jnp.float32
    in_specs = [once(cols)]
    in_specs += [pl.BlockSpec((pl.Squeezed(),) + a.shape[1:], lambda e: (e, 0, 0)) for a in kept]
    return moe_call(
        functools.partial(moe_rest_kernel, offset, units // 3, slots, count), steps, operands,
        in_specs + [outer, pl.BlockSpec(memory_space=pl.ANY)],
        [part] * slots + [grads], [once(part)] * slots + [grads_spec],
        [pltpu.VMEM((pairs, width), low), pltpu.VMEM(sums.shape, full), pltpu.SemaphoreType.DMA],
        steps * pairs * width * (6 * units + 2 * tokens),
    )


def unit_rows(values):
    center = values - jnp.mean(values, axis=1, keepdims=True)
    rate = lax.rsqrt(jnp.mean(center * center, axis=1, keepdims=True) + NORM_EPS)
    return center * rate, rate


def unit_rows_back(unit, rate, grad):
    mean_grad = jnp.mean(grad, axis=1, keepdims=True)
    mean_dot = jnp.mean(grad * unit, axis=1, keepdims=True)
    return rate * (grad - mean_grad - unit * mean_dot)


def as_column(row):
    wide = jnp.broadcast_to(row.astype(jnp.float32), (128, row.shape[1]))
    return jnp.transpose(wide)


def key_range(marks_ref, row_start, block, blocks):
    first = marks_ref[row_start]
    last = marks_ref[row_start + block - 1]
    begin = jnp.int32(0)
    end = jnp.int32(0)
    for index in range(blocks):
        begin = begin + jnp.where(marks_ref[index * block + block - 1] < first, 1, 0)
        end = end + jnp.where(marks_ref[index * block] <= last, 1, 0)
    return begin, end


def head_masks(block):
    low_half = lax.broadcasted_iota(jnp.int32, (block, 2 * HEAD), 1) < HEAD
    return low_half, jnp.logical_not(low_half)


def attend_kernel(
    block, marks_ref, x_ref, norm_ref, qkv_ref, proj_ref, seg_ref, task_ref,
    joined_ref, key_t_ref, mixed_ref, mixed_t_ref, logs_ref, hidden_ref, u_ref, value_t, column,
):
    tokens = x_ref.shape[0]
    blocks = tokens // block
    qkv_low = qkv_ref[...].astype(jnp.bfloat16)
    proj_low = proj_ref[...].astype(jnp.bfloat16)
    column[...] = as_column(seg_ref[...])

    def project(index, carry):
        span = pl.ds(pl.multiple_of(index * block, block), block)
        unit, _ = unit_rows(x_ref[span, :].astype(jnp.float32))
        attn_in = (unit * norm_ref[0:1, :] + norm_ref[1:2, :]).astype(jnp.bfloat16)
        joined = mxu(attn_in, qkv_low)
        joined_ref[span, :] = joined.astype(jnp.bfloat16)
        key_t_ref[:, span] = jnp.transpose(joined[:, D : 2 * D]).astype(jnp.bfloat16)
        value_t[:, span] = jnp.transpose(joined[:, 2 * D :]).astype(jnp.bfloat16)
        return carry

    lax.fori_loop(0, blocks, project, 0)

    def rows(index, carry):
        start = pl.multiple_of(index * block, block)
        span = pl.ds(start, block)
        begin, end = key_range(marks_ref, index * block, block, blocks)
        seg_row = seg_ref[:, span].astype(jnp.float32)
        masks = head_masks(block)
        for pair in range(HEADS // 2):
            lanes = slice(pair * 2 * HEAD, (pair + 1) * 2 * HEAD)
            query = joined_ref[span, lanes] * jnp.bfloat16(HEAD ** (-0.5))
            queries = [jnp.where(m, query, jnp.zeros_like(query)) for m in masks]

            def keys(at, state):
                key_span = pl.ds(pl.multiple_of(at * block, block), block)
                key_pair = joined_ref[key_span, D + pair * 2 * HEAD : D + (pair + 1) * 2 * HEAD]
                seg_col = jnp.concatenate([column[key_span, :]] * (block // 128), axis=1)
                same = seg_col == seg_row
                out = []
                for side in range(2):
                    peak, total, acc = state[side]
                    head = 2 * pair + side
                    scores = jnp.where(same, mxu(key_pair, queries[side], NT), MASKED)
                    new_peak = jnp.maximum(peak, jnp.max(scores, axis=0, keepdims=True))
                    weights = jnp.exp(scores - new_peak)
                    fix = jnp.exp(peak - new_peak)
                    total = total * fix + jnp.sum(weights, axis=0, keepdims=True)
                    value = value_t[head * HEAD : (head + 1) * HEAD, key_span]
                    acc = acc * fix + mxu(value, weights.astype(jnp.bfloat16))
                    out.append((new_peak, total, acc))
                return tuple(out)

            zero = (
                jnp.full((1, block), MASKED, jnp.float32),
                jnp.zeros((1, block), jnp.float32),
                jnp.zeros((HEAD, block), jnp.float32),
            )
            done = lax.fori_loop(begin, end, keys, (zero, zero))
            for side in range(2):
                peak, total, acc = done[side]
                head = 2 * pair + side
                mixed_t_ref[head * HEAD : (head + 1) * HEAD, span] = (acc / total).astype(jnp.bfloat16)
                logs_ref[head : head + 1, span] = peak + jnp.log(total)
        mixed = jnp.transpose(mixed_t_ref[:, span].astype(jnp.float32)).astype(jnp.bfloat16)
        mixed_ref[span, :] = mixed
        hidden = x_ref[span, :].astype(jnp.float32) + mxu(mixed, proj_low)
        hidden_ref[span, :] = hidden
        task = jnp.concatenate([as_column(task_ref[:, span])] * (D // 128), axis=1) > 0.5
        gain = jnp.where(task, norm_ref[3:4, :], norm_ref[2:3, :])
        bias = jnp.where(task, norm_ref[5:6, :], norm_ref[4:5, :])
        unit, _ = unit_rows(hidden)
        u_ref[span, :] = (unit * gain + bias).astype(jnp.bfloat16)
        return carry

    lax.fori_loop(0, blocks, rows, 0)


def attend(marks, x, norm, qkv, proj, seg, task):
    tokens = x.shape[0]
    block = min(256, tokens)
    vmem = pl.BlockSpec(memory_space=pltpu.VMEM)
    low = jnp.bfloat16
    return pl.pallas_call(
        functools.partial(attend_kernel, block),
        out_shape=(
            jax.ShapeDtypeStruct((tokens, 3 * D), low),
            jax.ShapeDtypeStruct((D, tokens), low),
            jax.ShapeDtypeStruct((tokens, D), low),
            jax.ShapeDtypeStruct((D, tokens), low),
            jax.ShapeDtypeStruct((8, tokens), jnp.float32),
            jax.ShapeDtypeStruct((tokens, D), jnp.float32),
            jax.ShapeDtypeStruct((tokens, D), low),
        ),
        in_specs=[pl.BlockSpec(memory_space=pltpu.SMEM)] + [vmem] * 6,
        out_specs=(vmem,) * 7,
        scratch_shapes=[pltpu.VMEM((D, tokens), low), pltpu.VMEM((tokens, 128), jnp.float32)],
        compiler_params=pltpu.CompilerParams(vmem_limit_bytes=48 << 20),
        cost_estimate=pl.CostEstimate(flops=8 << 30, bytes_accessed=12 << 20, transcendentals=6 << 20),
        name="attend",
    )(marks, x, norm, qkv, proj, seg, task)


def attend_back_kernel(
    block, slots, marks_ref, x_ref, norm_ref, qkv_ref, proj_ref, seg_ref, task_ref, out_grad_ref,
    joined_ref, key_t_ref, mixed_ref, mixed_t_ref, logs_ref, hidden_ref, *rest
):
    du_refs, digits_ref, rest = rest[:slots], rest[slots], rest[slots + 1 :]
    patch_ref, weight_ref, grads, attn_in, norms_ref, key_grad, value_grad, column = rest
    tokens = x_ref.shape[0]
    blocks = tokens // block
    qkv_low = qkv_ref[...].astype(jnp.bfloat16)
    proj_low = proj_ref[...].astype(jnp.bfloat16)
    column[...] = as_column(seg_ref[...])
    key_grad[...] = jnp.zeros_like(key_grad)
    value_grad[...] = jnp.zeros_like(value_grad)
    norms_ref[...] = jnp.zeros_like(norms_ref)
    weight_ref[...] = jnp.zeros_like(weight_ref)

    def rows(index, carry):
        start = pl.multiple_of(index * block, block)
        span = pl.ds(start, block)
        du = du_refs[0][span, :].astype(jnp.float32)
        for ref in du_refs[1:]:
            du = du + ref[span, :].astype(jnp.float32)
        task = jnp.concatenate([as_column(task_ref[:, span])] * (D // 128), axis=1) > 0.5
        gain = jnp.where(task, norm_ref[3:4, :], norm_ref[2:3, :])
        unit, rate = unit_rows(hidden_ref[span, :])
        first = jnp.where(task, 0.0, du)
        second = jnp.where(task, du, 0.0)
        norms_ref[2:3, :] += jnp.sum(first * unit, axis=0, keepdims=True)
        norms_ref[3:4, :] += jnp.sum(second * unit, axis=0, keepdims=True)
        norms_ref[4:5, :] += jnp.sum(first, axis=0, keepdims=True)
        norms_ref[5:6, :] += jnp.sum(second, axis=0, keepdims=True)
        hidden_grad = out_grad_ref[span, :].astype(jnp.float32) + unit_rows_back(unit, rate, du * gain)
        patch_ref[span, :] = hidden_grad
        grad_low = hidden_grad.astype(jnp.bfloat16)
        weight_ref[D:, D : 2 * D] += mxu(mixed_ref[span, :], grad_low, TN)
        mixed_grad = mxu(grad_low, proj_low, NT).astype(jnp.bfloat16)
        mixed_grad_t = mxu(proj_low, grad_low, NT).astype(jnp.bfloat16).astype(jnp.float32)
        dots = mixed_grad_t * mixed_t_ref[:, span].astype(jnp.float32)
        begin, end = key_range(marks_ref, index * block, block, blocks)
        seg_row = seg_ref[:, span].astype(jnp.float32)
        masks = head_masks(block)
        query_grads = []
        for pair in range(HEADS // 2):
            lanes = slice(pair * 2 * HEAD, (pair + 1) * 2 * HEAD)
            query = joined_ref[span, lanes] * jnp.bfloat16(HEAD ** (-0.5))
            queries = [jnp.where(m, query, jnp.zeros_like(query)) for m in masks]
            grad_pair = mixed_grad[:, lanes]
            out_grads = [jnp.where(m, grad_pair, jnp.zeros_like(grad_pair)) for m in masks]
            deltas = []
            logs = []
            for side in range(2):
                head = 2 * pair + side
                deltas.append(jnp.sum(dots[head * HEAD : (head + 1) * HEAD], axis=0, keepdims=True))
                logs.append(logs_ref[head : head + 1, span])

            def keys(at, state):
                key_span = pl.ds(pl.multiple_of(at * block, block), block)
                key_pair = joined_ref[key_span, D + pair * 2 * HEAD : D + (pair + 1) * 2 * HEAD]
                value_pair = joined_ref[key_span, 2 * D + pair * 2 * HEAD : 2 * D + (pair + 1) * 2 * HEAD]
                seg_col = jnp.concatenate([column[key_span, :]] * (block // 128), axis=1)
                same = seg_col == seg_row
                out = []
                key_sum = key_grad[key_span, lanes]
                value_sum = value_grad[key_span, lanes]
                for side in range(2):
                    head = 2 * pair + side
                    scores = jnp.where(same, mxu(key_pair, queries[side], NT), MASKED)
                    probs = jnp.exp(scores - logs[side])
                    prob_grad = mxu(value_pair, out_grads[side], NT)
                    score_grad = (probs * (prob_grad - deltas[side])).astype(jnp.bfloat16)
                    value_sum = value_sum + mxu(probs.astype(jnp.bfloat16), out_grads[side])
                    key_sum = key_sum + mxu(score_grad, queries[side])
                    key_t = key_t_ref[head * HEAD : (head + 1) * HEAD, key_span]
                    out.append(state[side] + mxu(key_t, score_grad))
                key_grad[key_span, lanes] = key_sum
                value_grad[key_span, lanes] = value_sum
                return tuple(out)

            zero = jnp.zeros((HEAD, block), jnp.float32)
            query_grads.extend(lax.fori_loop(begin, end, keys, (zero, zero)))
        query_grad_t = jnp.concatenate(query_grads, axis=0) * HEAD ** (-0.5)
        grads[span, :D] = jnp.transpose(query_grad_t).astype(jnp.bfloat16)
        return carry

    lax.fori_loop(0, blocks, rows, 0)

    def finish(index, carry):
        span = pl.ds(pl.multiple_of(index * block, block), block)
        grads[span, D : 2 * D] = key_grad[span, :].astype(jnp.bfloat16)
        grads[span, 2 * D :] = value_grad[span, :].astype(jnp.bfloat16)
        unit, rate = unit_rows(x_ref[span, :].astype(jnp.float32))
        attn_in[span, :] = (unit * norm_ref[0:1, :] + norm_ref[1:2, :]).astype(jnp.bfloat16)
        joined_grad = grads[span, :]
        in_grad = mxu(joined_grad, qkv_low, NT)
        norms_ref[0:1, :] += jnp.sum(in_grad * unit, axis=0, keepdims=True)
        norms_ref[1:2, :] += jnp.sum(in_grad, axis=0, keepdims=True)
        patch_ref[span, :] += unit_rows_back(unit, rate, in_grad * norm_ref[0:1, :])
        return carry

    lax.fori_loop(0, blocks, finish, 0)
    weight_ref[:D, : 2 * D] = mxu(attn_in[...], grads[:, : 2 * D], TN)
    weight_ref[D:, :D] = mxu(attn_in[...], grads[:, 2 * D :], TN)
    for part in range(D // 128):
        weight_ref[part * 8 : part * 8 + 8, 2 * D :] = norms_ref[:, part * 128 : (part + 1) * 128]
    weight_ref[24 : 24 + digits_ref.shape[0], 2 * D :] = digits_ref[...]


def attend_back(marks, x, norm, qkv, proj, seg, task, out_grad, saved, du_parts, digits):
    tokens = x.shape[0]
    block = min(256, tokens)
    vmem = pl.BlockSpec(memory_space=pltpu.VMEM)
    operands = [marks, x, norm, qkv, proj, seg, task, out_grad, *saved, *du_parts, digits]
    return pl.pallas_call(
        functools.partial(attend_back_kernel, block, len(du_parts)),
        out_shape=(
            jax.ShapeDtypeStruct((tokens, D), jnp.float32),
            jax.ShapeDtypeStruct((2 * D, 2 * D + 128), jnp.float32),
        ),
        in_specs=[pl.BlockSpec(memory_space=pltpu.SMEM)] + [vmem] * (len(operands) - 1),
        out_specs=(vmem,) * 2,
        scratch_shapes=[
            pltpu.VMEM((tokens, 3 * D), jnp.bfloat16),
            pltpu.VMEM((tokens, D), jnp.bfloat16),
            pltpu.VMEM((8, D), jnp.float32),
            pltpu.VMEM((tokens, D), jnp.float32),
            pltpu.VMEM((tokens, D), jnp.float32),
            pltpu.VMEM((tokens, 128), jnp.float32),
        ],
        compiler_params=pltpu.CompilerParams(vmem_limit_bytes=52 << 20),
        cost_estimate=pl.CostEstimate(flops=24 << 30, bytes_accessed=24 << 20, transcendentals=6 << 20),
        name="attend_back",
    )(*operands)


def to_peers(arrays, groups):
    return [arrays[0]] + [
        lax.ppermute(arrays[k], "expert", [(i, i ^ k) for i in range(groups)]) for k in range(1, groups)
    ]


def butterfly_sum(value, wire):
    sizes = [("hidden", lax.axis_size("hidden")), ("expert", lax.axis_size("expert"))]
    steps = []
    for axis, size in sizes:
        bit = 1
        while bit < size:
            steps.append((axis, size, bit))
            bit *= 2
    steps = steps[:1] + [s for s in steps if s[0] == "expert"] + [s for s in steps[1:] if s[0] == "hidden"]
    value = value.astype(jnp.float32)
    done = []
    for axis, size, bit in steps:
        half = value.shape[0] // 2
        if value.shape[0] % 2 or half % 8:
            break
        done.append((axis, size, bit))
        upper = (lax.axis_index(axis) & bit) > 0
        low_half, high_half = value[:half], value[half:]
        keep = jnp.where(upper, high_half, low_half)
        send = jnp.where(upper, low_half, high_half).astype(wire)
        got = lax.ppermute(send, axis, [(i, i ^ bit) for i in range(size)])
        value = keep + got.astype(jnp.float32)
    for axis, size, bit in steps[len(done):]:
        got = lax.ppermute(value.astype(wire), axis, [(i, i ^ bit) for i in range(size)])
        value = value + got.astype(jnp.float32)
    value = value.astype(wire)
    for axis, size, bit in done[::-1]:
        upper = (lax.axis_index(axis) & bit) > 0
        got = lax.ppermute(value, axis, [(i, i ^ bit) for i in range(size)])
        first = jnp.where(upper, got, value)
        second = jnp.where(upper, value, got)
        value = jnp.concatenate([first, second], axis=0)
    return value.astype(jnp.float32)


def nesterov(weight, moment, average, grad, rate):
    moment_new = MOMENT_DECAY * moment + grad
    weight_new = weight - rate * (grad + MOMENT_DECAY * moment_new)
    average_new = AVERAGE_DECAY * average + (1.0 - AVERAGE_DECAY) * weight_new
    return (weight_new, moment_new, average_new)


def body(
    patches,
    cotangent,
    expert_ids,
    gates,
    task_ids,
    segments,
    norm_params,
    attn_qkv,
    attn_proj,
    expert_inner,
    expert_outer,
    norm_moment,
    qkv_moment,
    proj_moment,
    inner_moment,
    outer_moment,
    norm_average,
    qkv_average,
    proj_average,
    inner_average,
    outer_average,
):
    groups = lax.axis_size("expert")
    tok_count = patches.shape[0]
    tokens_all = tok_count * groups * lax.axis_size("hidden")
    local_count = EXPERTS // groups
    own_units = expert_inner.shape[0]
    half = local_count // 2 * 2 * D
    both = jnp.stack([expert_inner, expert_outer], axis=2).astype(jnp.bfloat16)
    both = both.reshape(own_units, local_count * 2 * D)
    weights = [
        lax.all_gather(both[:, :half], "hidden", axis=0, tiled=True),
        lax.all_gather(both[:, half:], "hidden", axis=0, tiled=True),
    ]
    table = jnp.concatenate([expert_ids.astype(jnp.float32).T, gates.T], axis=0)
    tables = to_peers([table] * groups, groups)
    g_all = to_peers([cotangent] * groups, groups)
    first_expert = (lax.axis_index("expert") * local_count).astype(jnp.int32).reshape(1)
    tables = jnp.stack(tables)
    rows, gate_rows, cols = route(first_expert, tables[:, :TOP], tables[:, TOP:], local_count)
    named = jnp.sum(
        (expert_ids[:, :, None] == jnp.arange(EXPERTS, dtype=jnp.int32)).astype(jnp.int32), axis=(0, 1)
    )
    counts = jnp.minimum(named, CAP)
    digits = (counts[None, :] >> jnp.arange(16, dtype=jnp.int32)[:, None]) & 1
    digits = jnp.pad(digits.astype(jnp.float32), ((0, 0), (0, 128 - EXPERTS)))
    marks = segments[0]
    task_row = task_ids[None]
    *saved, moe_in = attend(marks, patches, norm_params, attn_qkv, attn_proj, segments, task_row)
    hidden_one = saved[-1]
    u_all = to_peers([moe_in] * groups, groups)
    second = local_count // 2
    y_sums, du_sums, grads_first = moe_full(rows, gate_rows, cols, u_all, g_all, weights[0], 0)
    outs = moe_front(rows, gate_rows, cols, u_all, g_all, weights[1], second, du_sums)
    du_parts = to_peers(outs[:groups], groups)
    *y_own, grads_second = moe_rest(cols, outs[groups:], weights[1], second, local_count, y_sums)
    y_parts = to_peers(y_own, groups)
    moe_sum = sum(p.astype(jnp.float32) for p in y_parts)
    block_out = (hidden_one + moe_sum).astype(jnp.bfloat16)
    owned = []
    for grads in (grads_first, grads_second):
        owned.append(lax.psum_scatter(grads, "hidden", scatter_dimension=0, tiled=True))
    owned = jnp.concatenate(owned, axis=1).astype(jnp.float32)
    owned = owned.reshape(own_units, local_count, 2, D)
    inner_grad, outer_grad = owned[:, :, 0], owned[:, :, 1]
    patch_grad, big = attend_back(
        marks, patches, norm_params, attn_qkv, attn_proj, segments, task_row, cotangent, saved,
        du_parts, digits,
    )
    big_sum = butterfly_sum(big, jnp.bfloat16)
    qkv_sum = jnp.concatenate([big_sum[:D, : 2 * D], big_sum[D:, :D]], axis=1)
    proj_sum = big_sum[D:, D : 2 * D]
    extra = big_sum[:, 2 * D :]
    norm_sum = jnp.concatenate([extra[8 * p : 8 * p + 6] for p in range(D // 128)], axis=1)
    powers = 2.0 ** jnp.arange(DIGITS, dtype=jnp.float32)
    count_sum = jnp.sum(extra[24 : 24 + DIGITS, :EXPERTS] * powers[:, None], axis=0)
    expert_load = count_sum * (EXPERTS / (tokens_all * TOP))
    root_tokens = math.sqrt(tokens_all)
    norm_new = nesterov(norm_params, norm_moment, norm_average, norm_sum, RATE_NORM / root_tokens)
    qkv_new = nesterov(attn_qkv, qkv_moment, qkv_average, qkv_sum, RATE_QKV / root_tokens)
    proj_new = nesterov(attn_proj, proj_moment, proj_average, proj_sum, RATE_PROJ / root_tokens)
    inner_new = nesterov(
        expert_inner, inner_moment, inner_average, inner_grad, RATE_INNER / root_tokens
    )
    outer_new = nesterov(
        expert_outer, outer_moment, outer_average, outer_grad, RATE_OUTER / root_tokens
    )
    return (
        block_out,
        patch_grad,
        expert_load,
        norm_new[0],
        norm_new[1],
        norm_new[2],
        qkv_new[0],
        qkv_new[1],
        qkv_new[2],
        proj_new[0],
        proj_new[1],
        proj_new[2],
        inner_new[0],
        inner_new[1],
        inner_new[2],
        outer_new[0],
        outer_new[1],
        outer_new[2],
    )


def solution(mesh):
    return jax.shard_map(
        body,
        mesh=mesh,
        in_specs=(
            P(("expert", "hidden"), None),
            P(("expert", "hidden"), None),
            P(("expert", "hidden"), None),
            P(("expert", "hidden"), None),
            P(("expert", "hidden")),
            P(("expert", "hidden"), None),
            P(),
            P(),
            P(),
            P("hidden", "expert", None),
            P("hidden", "expert", None),
            P(),
            P(),
            P(),
            P("hidden", "expert", None),
            P("hidden", "expert", None),
            P(),
            P(),
            P(),
            P("hidden", "expert", None),
            P("hidden", "expert", None),
        ),
        out_specs=(
            P(("expert", "hidden"), None),
            P(("expert", "hidden"), None),
            P(),
            P(),
            P(),
            P(),
            P(),
            P(),
            P(),
            P(),
            P(),
            P(),
            P("hidden", "expert", None),
            P("hidden", "expert", None),
            P("hidden", "expert", None),
            P("hidden", "expert", None),
            P("hidden", "expert", None),
            P("hidden", "expert", None),
        ),
        check_vma=False,
    )
```

```python
import functools
import math

import jax
import jax.numpy as jnp
from jax import lax
from jax.experimental import pallas as pl
from jax.experimental.pallas import tpu as pltpu
from jax.sharding import PartitionSpec as P

D = 384
HEADS = 6
HEAD = 64
EXPERTS = 16
TOP = 4
CAP = 320


MOMENT_DECAY = 0.9
AVERAGE_DECAY = 0.9
RATE_NORM = 0.23
RATE_QKV = 0.064
RATE_PROJ = 1.4
RATE_INNER = 0.21
RATE_OUTER = 0.73
NORM_EPS = 1e-06
MASKED = -1e30
VMEM_MOST = 67043328
DIGITS = 9


def route_kernel(first_expert, ids_ref, gates_ref, rows_ref, gate_rows_ref, cols_ref):
    slots, _, tokens = ids_ref.shape
    count = rows_ref.shape[1]
    before = (
        lax.broadcasted_iota(jnp.int32, (tokens, tokens), 0)
        <= lax.broadcasted_iota(jnp.int32, (tokens, tokens), 1)
    )
    before = jnp.where(before, 1.0, 0.0).astype(jnp.bfloat16)
    hot_rows = []
    for slot in range(slots):
        for expert in range(count):
            hot = jnp.zeros((1, tokens), jnp.float32)
            gate = jnp.zeros((1, tokens), jnp.float32)
            name = (first_expert[0] + expert).astype(jnp.float32)
            for choice in range(TOP):
                same = ids_ref[slot, choice : choice + 1, :] == name
                hot = jnp.where(same, 1.0, hot)
                gate = jnp.where(same, gates_ref[slot, choice : choice + 1, :], gate)
            hot_rows.append(hot)
            gate_rows_ref[slot, expert : expert + 1, :] = gate
    hot_all = jnp.concatenate(hot_rows, axis=0)
    place = jnp.dot(hot_all.astype(jnp.bfloat16), before, preferred_element_type=jnp.float32) - 1.0
    place = jnp.where((hot_all > 0.5) & (place < CAP), place, -1.0)
    for slot in range(slots):
        rows_ref[slot] = place[slot * count : (slot + 1) * count].astype(jnp.int32)
    wide = jnp.concatenate([place, jnp.full((128 - place.shape[0], tokens), -1.0, jnp.float32)], axis=0)
    cols_ref[...] = jnp.transpose(wide).astype(jnp.int32)


def route(first_expert, ids_all, gates_all, count):
    slots, _, tokens = ids_all.shape
    vmem = pl.BlockSpec(memory_space=pltpu.VMEM)
    return pl.pallas_call(
        route_kernel,
        out_shape=(
            jax.ShapeDtypeStruct((slots, count, tokens), jnp.int32),
            jax.ShapeDtypeStruct((slots, count, tokens), jnp.float32),
            jax.ShapeDtypeStruct((tokens, 128), jnp.int32),
        ),
        in_specs=[pl.BlockSpec(memory_space=pltpu.SMEM), vmem, vmem],
        out_specs=(vmem, vmem, vmem),
        name="route",
    )(first_expert, ids_all, gates_all)


NT = (((1,), (1,)), ((), ()))
NN = (((1,), (0,)), ((), ()))
TN = (((0,), (0,)), ((), ()))


def mxu(left, right, dims=NN):
    return lax.dot_general(left, right, dims, preferred_element_type=jnp.float32)


def moe_early_kernel(slots, rows_ref, gate_rows_ref, *rest):
    g_refs, dy_ref, gate_ref = rest[:slots], rest[slots], rest[slots + 1]
    tokens = rows_ref.shape[2]
    lane = pl.program_id(0)
    for slot in range(slots):
        same = lax.broadcasted_iota(jnp.int32, (CAP, tokens), 0) == rows_ref[slot, pl.ds(lane, 1), :]
        pick = jnp.where(same, 1.0, 0.0).astype(jnp.bfloat16)
        gate = jnp.sum(jnp.where(same, gate_rows_ref[slot, pl.ds(lane, 1), :], 0.0), axis=1, keepdims=True)
        span = pl.ds(slot * CAP, CAP)
        dy_ref[span, :] = (gate * mxu(pick, g_refs[slot][...])).astype(jnp.bfloat16)
        gate_ref[span, :] = jnp.broadcast_to(gate, (CAP, 128))


def moe_early(rows, gate_rows, g_all):
    slots, count, tokens = rows.shape
    width = g_all[0].shape[1]
    pairs = slots * CAP
    operands = [rows, gate_rows, *g_all]
    shapes = [((pairs, width), jnp.bfloat16), ((pairs, 128), jnp.float32)]
    return moe_call(
        functools.partial(moe_early_kernel, slots), count, operands,
        [once(a) for a in operands],
        [jax.ShapeDtypeStruct((count,) + shape, kind) for shape, kind in shapes],
        [pl.BlockSpec((pl.Squeezed(),) + shape, lambda e: (e, 0, 0)) for shape, _ in shapes],
        [], count * pairs * width * 2 * tokens,
    )


def dispatch(rows_ref, u_refs, lane, x_out):
    slots, _, tokens = rows_ref.shape
    for slot in range(slots):
        same = lax.broadcasted_iota(jnp.int32, (CAP, tokens), 0) == rows_ref[slot, pl.ds(lane, 1), :]
        pick = jnp.where(same, 1.0, 0.0).astype(jnp.bfloat16)
        x_out[pl.ds(slot * CAP, CAP), :] = mxu(pick, u_refs[slot][...]).astype(jnp.bfloat16)


def combine(cols_ref, lanes, step, buf, sum_buf, fresh):
    tokens = cols_ref.shape[0]
    for slot, lane in enumerate(lanes):
        wide = lax.broadcasted_iota(jnp.int32, (tokens, 128), 1) == lane
        column = jnp.sum(jnp.where(wide, cols_ref[...], 0), axis=1, keepdims=True)
        same = lax.broadcasted_iota(jnp.int32, (tokens, CAP), 1) == column
        spread = jnp.where(same, 1.0, 0.0).astype(jnp.bfloat16)
        add = mxu(spread, buf[pl.ds(slot * CAP, CAP), :])
        old = sum_buf[slot]
        if fresh:
            old = jnp.where(step > 0, old, 0.0)
        sum_buf[slot] = old + add


def gelu_pair(pre, act_grad):
    phi = 0.5 + 0.5 * lax.erf(pre * math.sqrt(0.5))
    bell = jnp.exp(pre * pre * -0.5) * (1.0 / math.sqrt(2.0 * math.pi))
    return (pre * phi).astype(jnp.bfloat16), (act_grad * (phi + pre * bell)).astype(jnp.bfloat16)


def times_gate(gate, result):
    gate_wide = jnp.concatenate([gate] * (result.shape[1] // 128), axis=1)
    return (gate_wide * result).astype(jnp.bfloat16)


def slot_lanes(slots, count, offset, step):
    return [slot * count + offset + step for slot in range(slots)]


def moe_full_kernel(offset, chunk, slots, rows_ref, cols_ref, dy_ref, gate_ref, *rest):
    u_refs, rest = rest[:slots], rest[slots:]
    inner_ref, outer_ref, y_ref, du_ref, grads_ref = rest[:5]
    x_buf, dy_buf, act_buf, dpre_buf, y_buf, du_buf = rest[5:]
    step = pl.program_id(0)
    width = inner_ref.shape[1]
    dispatch(rows_ref, u_refs, offset + step, x_buf)

    def part(index, carry):
        span = pl.ds(pl.multiple_of(index * chunk, chunk), chunk)
        rows_in = x_buf[...]
        rows_grad = dy_ref[...]
        act, dpre = gelu_pair(mxu(rows_in, inner_ref[span, :], NT), mxu(rows_grad, outer_ref[span, :], NT))
        act_buf[:, span] = act
        dpre_buf[:, span] = dpre
        grads_ref[span, :width] = mxu(dpre, rows_in, TN).astype(jnp.bfloat16)
        grads_ref[span, width:] = mxu(act, rows_grad, TN).astype(jnp.bfloat16)
        return carry

    lax.fori_loop(0, inner_ref.shape[0] // chunk, part, 0)
    x_buf[...] = times_gate(gate_ref[...], mxu(act_buf[...], outer_ref[...]))
    dy_buf[...] = mxu(dpre_buf[...], inner_ref[...]).astype(jnp.bfloat16)
    lanes = slot_lanes(slots, rows_ref.shape[1], offset, step)
    combine(cols_ref, lanes, step, x_buf, y_buf, True)
    combine(cols_ref, lanes, step, dy_buf, du_buf, True)

    @pl.when(step == pl.num_programs(0) - 1)
    def _():
        y_ref[...] = y_buf[...]
        du_ref[...] = du_buf[...]


def fetch(start_ref, sum_buf, sem):
    @pl.when(pl.program_id(0) == 0)
    def _():
        copy = pltpu.make_async_copy(start_ref, sum_buf, sem)
        copy.start()
        copy.wait()


def finish_sums(out_refs, sum_buf):
    @pl.when(pl.program_id(0) == pl.num_programs(0) - 1)
    def _():
        for slot, ref in enumerate(out_refs):
            ref[...] = sum_buf[slot].astype(jnp.bfloat16)


def moe_front_kernel(offset, chunk, slots, rows_ref, cols_ref, dy_ref, *rest):
    u_refs, rest = rest[:slots], rest[slots:]
    inner_ref, outer_ref, start_ref, rest = rest[0], rest[1], rest[2], rest[3:]
    du_refs, rest = rest[:slots], rest[slots:]
    x_ref, act_ref, dpre_ref, buf, sum_buf, sem = rest
    step = pl.program_id(0)
    fetch(start_ref, sum_buf, sem)
    dispatch(rows_ref, u_refs, offset + step, x_ref)

    def part(index, carry):
        span = pl.ds(pl.multiple_of(index * chunk, chunk), chunk)
        act, dpre = gelu_pair(mxu(x_ref[...], inner_ref[span, :], NT), mxu(dy_ref[...], outer_ref[span, :], NT))
        act_ref[:, span] = act
        dpre_ref[:, span] = dpre
        return carry

    lax.fori_loop(0, inner_ref.shape[0] // chunk, part, 0)
    buf[...] = mxu(dpre_ref[...], inner_ref[...]).astype(jnp.bfloat16)
    combine(cols_ref, slot_lanes(slots, rows_ref.shape[1], offset, step), step, buf, sum_buf, False)
    finish_sums(du_refs, sum_buf)


def moe_rest_kernel(offset, chunk, slots, count, cols_ref, x_ref, dy_ref, gate_ref, act_ref, dpre_ref, *rest):
    outer_ref, start_ref, rest = rest[0], rest[1], rest[2:]
    y_refs, rest = rest[:slots], rest[slots:]
    grads_ref, buf, sum_buf, sem = rest
    step = pl.program_id(0)
    width = x_ref.shape[1]
    fetch(start_ref, sum_buf, sem)

    def part(index, carry):
        span = pl.ds(pl.multiple_of(index * chunk, chunk), chunk)
        grads_ref[span, :width] = mxu(dpre_ref[:, span], x_ref[...], TN).astype(jnp.bfloat16)
        grads_ref[span, width:] = mxu(act_ref[:, span], dy_ref[...], TN).astype(jnp.bfloat16)
        return carry

    lax.fori_loop(0, outer_ref.shape[0] // chunk, part, 0)
    buf[...] = times_gate(gate_ref[...], mxu(act_ref[...], outer_ref[...]))
    combine(cols_ref, slot_lanes(slots, count, offset, step), step, buf, sum_buf, False)
    finish_sums(y_refs, sum_buf)


def once(array):
    return pl.BlockSpec(array.shape, lambda e: (0,) * len(array.shape), pipeline_mode=pl.Buffered(1))


def moe_call(kernel, steps, operands, in_specs, outs, out_specs, scratch, flops):
    return pl.pallas_call(
        kernel,
        out_shape=tuple(outs),
        grid_spec=pltpu.PrefetchScalarGridSpec(
            num_scalar_prefetch=0, grid=(steps,), in_specs=in_specs, out_specs=tuple(out_specs),
            scratch_shapes=scratch,
        ),
        compiler_params=pltpu.CompilerParams(
            dimension_semantics=("arbitrary",), vmem_limit_bytes=VMEM_MOST
        ),
        cost_estimate=pl.CostEstimate(flops=flops, bytes_accessed=40 << 20, transcendentals=0),
    )(*operands)


def moe_sizes(slots, tokens, weights, width):
    units = weights.shape[0]
    steps = weights.shape[1] // (2 * width)
    pairs = slots * CAP
    low, full = jnp.bfloat16, jnp.float32
    sums = jax.ShapeDtypeStruct((slots, tokens, width), full)
    part = jax.ShapeDtypeStruct((tokens, width), low)
    inner = pl.BlockSpec((units, width), lambda e: (0, 2 * e))
    outer = pl.BlockSpec((units, width), lambda e: (0, 2 * e + 1))
    grads = jax.ShapeDtypeStruct((units, steps * 2 * width), low)
    grads_spec = pl.BlockSpec((units, 2 * width), lambda e: (0, e))
    return units, steps, pairs, sums, part, inner, outer, grads, grads_spec


def expert_block(array, offset):
    return pl.BlockSpec((pl.Squeezed(),) + array.shape[1:], lambda e: (offset + e, 0, 0))


def moe_full(rows, cols, early, u_all, weights, offset):
    slots, _, tokens = rows.shape
    width = u_all[0].shape[1]
    units, steps, pairs, sums, _, inner, outer, grads, grads_spec = moe_sizes(slots, tokens, weights, width)
    operands = [rows, cols, *early, *u_all, weights, weights]
    low, full = jnp.bfloat16, jnp.float32
    scratch = [pltpu.VMEM((pairs, width), low)] * 2 + [pltpu.VMEM((pairs, units), low)] * 2
    scratch += [pltpu.VMEM(sums.shape, full)] * 2
    return moe_call(
        functools.partial(moe_full_kernel, offset, units // 3, slots), steps, operands,
        [once(rows), once(cols)] + [expert_block(a, offset) for a in early]
        + [once(a) for a in u_all] + [inner, outer],
        [sums, sums, grads], [once(sums), once(sums), grads_spec], scratch,
        steps * pairs * width * (12 * units + 6 * tokens),
    )


def moe_front(rows, cols, early, u_all, weights, offset, start):
    slots, _, tokens = rows.shape
    width = u_all[0].shape[1]
    units, steps, pairs, sums, part, inner, outer, _, _ = moe_sizes(slots, tokens, weights, width)
    operands = [rows, cols, early[0], *u_all, weights, weights, start]
    low, full = jnp.bfloat16, jnp.float32
    kept = [((pairs, width), low), ((pairs, units), low), ((pairs, units), low)]
    outs = [part] * slots + [jax.ShapeDtypeStruct((steps,) + shape, kind) for shape, kind in kept]
    specs = [once(part)] * slots
    specs += [pl.BlockSpec((pl.Squeezed(),) + shape, lambda e: (e, 0, 0)) for shape, _ in kept]
    return moe_call(
        functools.partial(moe_front_kernel, offset, units // 3, slots), steps, operands,
        [once(rows), once(cols), expert_block(early[0], offset)]
        + [once(a) for a in u_all] + [inner, outer, pl.BlockSpec(memory_space=pl.ANY)],
        outs, specs,
        [pltpu.VMEM((pairs, width), low), pltpu.VMEM(sums.shape, full), pltpu.SemaphoreType.DMA],
        steps * pairs * width * (6 * units + 4 * tokens),
    )


def moe_rest(cols, kept, early, weights, offset, count, start):
    slots, tokens, width = start.shape
    units, steps, pairs, sums, part, _, outer, grads, grads_spec = moe_sizes(slots, tokens, weights, width)
    operands = [cols, kept[0], *early, *kept[1:], weights, start]
    low, full = jnp.bfloat16, jnp.float32
    in_specs = [once(cols)]
    in_specs += [expert_block(kept[0], 0)] + [expert_block(a, offset) for a in early]
    in_specs += [expert_block(a, 0) for a in kept[1:]]
    return moe_call(
        functools.partial(moe_rest_kernel, offset, units // 3, slots, count), steps, operands,
        in_specs + [outer, pl.BlockSpec(memory_space=pl.ANY)],
        [part] * slots + [grads], [once(part)] * slots + [grads_spec],
        [pltpu.VMEM((pairs, width), low), pltpu.VMEM(sums.shape, full), pltpu.SemaphoreType.DMA],
        steps * pairs * width * (6 * units + 2 * tokens),
    )


def unit_rows(values):
    center = values - jnp.mean(values, axis=1, keepdims=True)
    rate = lax.rsqrt(jnp.mean(center * center, axis=1, keepdims=True) + NORM_EPS)
    return center * rate, rate


def unit_rows_back(unit, rate, grad):
    mean_grad = jnp.mean(grad, axis=1, keepdims=True)
    mean_dot = jnp.mean(grad * unit, axis=1, keepdims=True)
    return rate * (grad - mean_grad - unit * mean_dot)


def as_column(row):
    wide = jnp.broadcast_to(row.astype(jnp.float32), (128, row.shape[1]))
    return jnp.transpose(wide)


def key_range(marks_ref, row_start, block, blocks):
    first = marks_ref[row_start]
    last = marks_ref[row_start + block - 1]
    begin = jnp.int32(0)
    end = jnp.int32(0)
    for index in range(blocks):
        begin = begin + jnp.where(marks_ref[index * block + block - 1] < first, 1, 0)
        end = end + jnp.where(marks_ref[index * block] <= last, 1, 0)
    return begin, end


def head_masks(block):
    low_half = lax.broadcasted_iota(jnp.int32, (block, 2 * HEAD), 1) < HEAD
    return low_half, jnp.logical_not(low_half)


def attend_kernel(
    block, marks_ref, x_ref, norm_ref, qkv_ref, proj_ref, seg_ref, task_ref,
    joined_ref, key_t_ref, mixed_ref, mixed_t_ref, logs_ref, hidden_ref, u_ref, value_t, column,
):
    tokens = x_ref.shape[0]
    blocks = tokens // block
    qkv_low = qkv_ref[...].astype(jnp.bfloat16)
    proj_low = proj_ref[...].astype(jnp.bfloat16)
    column[...] = as_column(seg_ref[...])

    def project(index, carry):
        span = pl.ds(pl.multiple_of(index * block, block), block)
        unit, _ = unit_rows(x_ref[span, :].astype(jnp.float32))
        attn_in = (unit * norm_ref[0:1, :] + norm_ref[1:2, :]).astype(jnp.bfloat16)
        joined = mxu(attn_in, qkv_low)
        joined_ref[span, :] = joined.astype(jnp.bfloat16)
        key_t_ref[:, span] = jnp.transpose(joined[:, D : 2 * D]).astype(jnp.bfloat16)
        value_t[:, span] = jnp.transpose(joined[:, 2 * D :]).astype(jnp.bfloat16)
        return carry

    lax.fori_loop(0, blocks, project, 0)

    def rows(index, carry):
        start = pl.multiple_of(index * block, block)
        span = pl.ds(start, block)
        begin, end = key_range(marks_ref, index * block, block, blocks)
        seg_row = seg_ref[:, span].astype(jnp.float32)
        masks = head_masks(block)
        queries = []
        for pair in range(HEADS // 2):
            lanes = slice(pair * 2 * HEAD, (pair + 1) * 2 * HEAD)
            query = joined_ref[span, lanes] * jnp.bfloat16(HEAD ** (-0.5))
            queries.extend(jnp.where(m, query, jnp.zeros_like(query)) for m in masks)

        def keys(at, state):
            key_span = pl.ds(pl.multiple_of(at * block, block), block)
            seg_col = jnp.concatenate([column[key_span, :]] * (block // 128), axis=1)
            same = seg_col == seg_row
            out = []
            for head in range(HEADS):
                first = D + head // 2 * 2 * HEAD
                key_pair = joined_ref[key_span, first : first + 2 * HEAD]
                peak, total, acc = state[head]
                scores = jnp.where(same, mxu(key_pair, queries[head], NT), MASKED)
                new_peak = jnp.maximum(peak, jnp.max(scores, axis=0, keepdims=True))
                weights = jnp.exp(scores - new_peak)
                fix = jnp.exp(peak - new_peak)
                total = total * fix + jnp.sum(weights, axis=0, keepdims=True)
                value = value_t[head * HEAD : (head + 1) * HEAD, key_span]
                acc = acc * fix + mxu(value, weights.astype(jnp.bfloat16))
                out.append((new_peak, total, acc))
            return tuple(out)

        zero = (
            jnp.full((1, block), MASKED, jnp.float32),
            jnp.zeros((1, block), jnp.float32),
            jnp.zeros((HEAD, block), jnp.float32),
        )
        done = lax.fori_loop(begin, end, keys, (zero,) * HEADS)
        for head in range(HEADS):
            peak, total, acc = done[head]
            mixed_t_ref[head * HEAD : (head + 1) * HEAD, span] = (acc / total).astype(jnp.bfloat16)
            logs_ref[head : head + 1, span] = peak + jnp.log(total)
        mixed = jnp.transpose(mixed_t_ref[:, span].astype(jnp.float32)).astype(jnp.bfloat16)
        mixed_ref[span, :] = mixed
        hidden = x_ref[span, :].astype(jnp.float32) + mxu(mixed, proj_low)
        hidden_ref[span, :] = hidden
        task = jnp.concatenate([as_column(task_ref[:, span])] * (D // 128), axis=1) > 0.5
        gain = jnp.where(task, norm_ref[3:4, :], norm_ref[2:3, :])
        bias = jnp.where(task, norm_ref[5:6, :], norm_ref[4:5, :])
        unit, _ = unit_rows(hidden)
        u_ref[span, :] = (unit * gain + bias).astype(jnp.bfloat16)
        return carry

    lax.fori_loop(0, blocks, rows, 0)


def attend(marks, x, norm, qkv, proj, seg, task):
    tokens = x.shape[0]
    block = min(256, tokens)
    vmem = pl.BlockSpec(memory_space=pltpu.VMEM)
    low = jnp.bfloat16
    return pl.pallas_call(
        functools.partial(attend_kernel, block),
        out_shape=(
            jax.ShapeDtypeStruct((tokens, 3 * D), low),
            jax.ShapeDtypeStruct((D, tokens), low),
            jax.ShapeDtypeStruct((tokens, D), low),
            jax.ShapeDtypeStruct((D, tokens), low),
            jax.ShapeDtypeStruct((8, tokens), jnp.float32),
            jax.ShapeDtypeStruct((tokens, D), jnp.float32),
            jax.ShapeDtypeStruct((tokens, D), low),
        ),
        in_specs=[pl.BlockSpec(memory_space=pltpu.SMEM)] + [vmem] * 6,
        out_specs=(vmem,) * 7,
        scratch_shapes=[pltpu.VMEM((D, tokens), low), pltpu.VMEM((tokens, 128), jnp.float32)],
        compiler_params=pltpu.CompilerParams(vmem_limit_bytes=48 << 20),
        cost_estimate=pl.CostEstimate(flops=8 << 30, bytes_accessed=12 << 20, transcendentals=6 << 20),
        name="attend",
    )(marks, x, norm, qkv, proj, seg, task)


def attend_back_kernel(
    block, slots, marks_ref, x_ref, norm_ref, qkv_ref, proj_ref, seg_ref, task_ref, out_grad_ref,
    joined_ref, key_t_ref, mixed_ref, mixed_t_ref, logs_ref, hidden_ref, *rest
):
    du_refs, digits_ref, rest = rest[:slots], rest[slots], rest[slots + 1 :]
    patch_ref, weight_ref, grads, attn_in, norms_ref, key_grad, value_grad, column = rest
    tokens = x_ref.shape[0]
    blocks = tokens // block
    qkv_low = qkv_ref[...].astype(jnp.bfloat16)
    proj_low = proj_ref[...].astype(jnp.bfloat16)
    column[...] = as_column(seg_ref[...])
    key_grad[...] = jnp.zeros_like(key_grad)
    value_grad[...] = jnp.zeros_like(value_grad)
    norms_ref[...] = jnp.zeros_like(norms_ref)
    weight_ref[...] = jnp.zeros_like(weight_ref)

    def rows(index, carry):
        start = pl.multiple_of(index * block, block)
        span = pl.ds(start, block)
        du = du_refs[0][span, :].astype(jnp.float32)
        for ref in du_refs[1:]:
            du = du + ref[span, :].astype(jnp.float32)
        task = jnp.concatenate([as_column(task_ref[:, span])] * (D // 128), axis=1) > 0.5
        gain = jnp.where(task, norm_ref[3:4, :], norm_ref[2:3, :])
        unit, rate = unit_rows(hidden_ref[span, :])
        first = jnp.where(task, 0.0, du)
        second = jnp.where(task, du, 0.0)
        norms_ref[2:3, :] += jnp.sum(first * unit, axis=0, keepdims=True)
        norms_ref[3:4, :] += jnp.sum(second * unit, axis=0, keepdims=True)
        norms_ref[4:5, :] += jnp.sum(first, axis=0, keepdims=True)
        norms_ref[5:6, :] += jnp.sum(second, axis=0, keepdims=True)
        hidden_grad = out_grad_ref[span, :].astype(jnp.float32) + unit_rows_back(unit, rate, du * gain)
        patch_ref[span, :] = hidden_grad
        grad_low = hidden_grad.astype(jnp.bfloat16)
        weight_ref[D:, D : 2 * D] += mxu(mixed_ref[span, :], grad_low, TN)
        mixed_grad = mxu(grad_low, proj_low, NT).astype(jnp.bfloat16)
        mixed_grad_t = mxu(proj_low, grad_low, NT).astype(jnp.bfloat16).astype(jnp.float32)
        dots = mixed_grad_t * mixed_t_ref[:, span].astype(jnp.float32)
        begin, end = key_range(marks_ref, index * block, block, blocks)
        seg_row = seg_ref[:, span].astype(jnp.float32)
        masks = head_masks(block)
        queries = []
        out_grads = []
        deltas = []
        logs = []
        for pair in range(HEADS // 2):
            lanes = slice(pair * 2 * HEAD, (pair + 1) * 2 * HEAD)
            query = joined_ref[span, lanes] * jnp.bfloat16(HEAD ** (-0.5))
            queries.extend(jnp.where(m, query, jnp.zeros_like(query)) for m in masks)
            grad_pair = mixed_grad[:, lanes]
            out_grads.extend(jnp.where(m, grad_pair, jnp.zeros_like(grad_pair)) for m in masks)
        for head in range(HEADS):
            deltas.append(jnp.sum(dots[head * HEAD : (head + 1) * HEAD], axis=0, keepdims=True))
            logs.append(logs_ref[head : head + 1, span])

        def keys(at, state):
            key_span = pl.ds(pl.multiple_of(at * block, block), block)
            seg_col = jnp.concatenate([column[key_span, :]] * (block // 128), axis=1)
            same = seg_col == seg_row
            out = []
            for pair in range(HEADS // 2):
                first = pair * 2 * HEAD
                lanes = slice(first, first + 2 * HEAD)
                key_pair = joined_ref[key_span, D + first : D + first + 2 * HEAD]
                value_pair = joined_ref[key_span, 2 * D + first : 2 * D + first + 2 * HEAD]
                key_sum = key_grad[key_span, lanes]
                value_sum = value_grad[key_span, lanes]
                for head in (2 * pair, 2 * pair + 1):
                    scores = jnp.where(same, mxu(key_pair, queries[head], NT), MASKED)
                    probs = jnp.exp(scores - logs[head])
                    prob_grad = mxu(value_pair, out_grads[head], NT)
                    score_grad = (probs * (prob_grad - deltas[head])).astype(jnp.bfloat16)
                    value_sum = value_sum + mxu(probs.astype(jnp.bfloat16), out_grads[head])
                    key_sum = key_sum + mxu(score_grad, queries[head])
                    key_t = key_t_ref[head * HEAD : (head + 1) * HEAD, key_span]
                    out.append(state[head] + mxu(key_t, score_grad))
                key_grad[key_span, lanes] = key_sum
                value_grad[key_span, lanes] = value_sum
            return tuple(out)

        zero = jnp.zeros((HEAD, block), jnp.float32)
        query_grads = lax.fori_loop(begin, end, keys, (zero,) * HEADS)
        query_grad_t = jnp.concatenate(query_grads, axis=0) * HEAD ** (-0.5)
        grads[span, :D] = jnp.transpose(query_grad_t).astype(jnp.bfloat16)
        return carry

    lax.fori_loop(0, blocks, rows, 0)

    def finish(index, carry):
        span = pl.ds(pl.multiple_of(index * block, block), block)
        grads[span, D : 2 * D] = key_grad[span, :].astype(jnp.bfloat16)
        grads[span, 2 * D :] = value_grad[span, :].astype(jnp.bfloat16)
        unit, rate = unit_rows(x_ref[span, :].astype(jnp.float32))
        attn_in[span, :] = (unit * norm_ref[0:1, :] + norm_ref[1:2, :]).astype(jnp.bfloat16)
        joined_grad = grads[span, :]
        in_grad = mxu(joined_grad, qkv_low, NT)
        norms_ref[0:1, :] += jnp.sum(in_grad * unit, axis=0, keepdims=True)
        norms_ref[1:2, :] += jnp.sum(in_grad, axis=0, keepdims=True)
        patch_ref[span, :] += unit_rows_back(unit, rate, in_grad * norm_ref[0:1, :])
        return carry

    lax.fori_loop(0, blocks, finish, 0)
    weight_ref[:D, : 2 * D] = mxu(attn_in[...], grads[:, : 2 * D], TN)
    weight_ref[D:, :D] = mxu(attn_in[...], grads[:, 2 * D :], TN)
    for part in range(D // 128):
        weight_ref[part * 8 : part * 8 + 8, 2 * D :] = norms_ref[:, part * 128 : (part + 1) * 128]
    weight_ref[24 : 24 + digits_ref.shape[0], 2 * D :] = digits_ref[...]


def attend_back(marks, x, norm, qkv, proj, seg, task, out_grad, saved, du_parts, digits):
    tokens = x.shape[0]
    block = min(256, tokens)
    vmem = pl.BlockSpec(memory_space=pltpu.VMEM)
    operands = [marks, x, norm, qkv, proj, seg, task, out_grad, *saved, *du_parts, digits]
    return pl.pallas_call(
        functools.partial(attend_back_kernel, block, len(du_parts)),
        out_shape=(
            jax.ShapeDtypeStruct((tokens, D), jnp.float32),
            jax.ShapeDtypeStruct((2 * D, 2 * D + 128), jnp.float32),
        ),
        in_specs=[pl.BlockSpec(memory_space=pltpu.SMEM)] + [vmem] * (len(operands) - 1),
        out_specs=(vmem,) * 2,
        scratch_shapes=[
            pltpu.VMEM((tokens, 3 * D), jnp.bfloat16),
            pltpu.VMEM((tokens, D), jnp.bfloat16),
            pltpu.VMEM((8, D), jnp.float32),
            pltpu.VMEM((tokens, D), jnp.float32),
            pltpu.VMEM((tokens, D), jnp.float32),
            pltpu.VMEM((tokens, 128), jnp.float32),
        ],
        compiler_params=pltpu.CompilerParams(vmem_limit_bytes=52 << 20),
        cost_estimate=pl.CostEstimate(flops=24 << 30, bytes_accessed=24 << 20, transcendentals=6 << 20),
        name="attend_back",
    )(*operands)


def to_peers(arrays, groups):
    return [arrays[0]] + [
        lax.ppermute(arrays[k], "expert", [(i, i ^ k) for i in range(groups)]) for k in range(1, groups)
    ]


def butterfly_sum(value, wire):
    sizes = [("hidden", lax.axis_size("hidden")), ("expert", lax.axis_size("expert"))]
    steps = []
    for axis, size in sizes:
        bit = 1
        while bit < size:
            steps.append((axis, size, bit))
            bit *= 2
    steps = steps[:1] + [s for s in steps if s[0] == "expert"] + [s for s in steps[1:] if s[0] == "hidden"]
    value = value.astype(jnp.float32)
    done = []
    for axis, size, bit in steps:
        half = value.shape[0] // 2
        if value.shape[0] % 2 or half % 8:
            break
        done.append((axis, size, bit))
        upper = (lax.axis_index(axis) & bit) > 0
        low_half, high_half = value[:half], value[half:]
        keep = jnp.where(upper, high_half, low_half)
        send = jnp.where(upper, low_half, high_half).astype(wire)
        got = lax.ppermute(send, axis, [(i, i ^ bit) for i in range(size)])
        value = keep + got.astype(jnp.float32)
    for axis, size, bit in steps[len(done):]:
        got = lax.ppermute(value.astype(wire), axis, [(i, i ^ bit) for i in range(size)])
        value = value + got.astype(jnp.float32)
    value = value.astype(wire)
    for axis, size, bit in done[::-1]:
        upper = (lax.axis_index(axis) & bit) > 0
        got = lax.ppermute(value, axis, [(i, i ^ bit) for i in range(size)])
        first = jnp.where(upper, got, value)
        second = jnp.where(upper, value, got)
        value = jnp.concatenate([first, second], axis=0)
    return value.astype(jnp.float32)


def nesterov(weight, moment, average, grad, rate):
    moment_new = MOMENT_DECAY * moment + grad
    weight_new = weight - rate * (grad + MOMENT_DECAY * moment_new)
    average_new = AVERAGE_DECAY * average + (1.0 - AVERAGE_DECAY) * weight_new
    return (weight_new, moment_new, average_new)


def body(
    patches,
    cotangent,
    expert_ids,
    gates,
    task_ids,
    segments,
    norm_params,
    attn_qkv,
    attn_proj,
    expert_inner,
    expert_outer,
    norm_moment,
    qkv_moment,
    proj_moment,
    inner_moment,
    outer_moment,
    norm_average,
    qkv_average,
    proj_average,
    inner_average,
    outer_average,
):
    groups = lax.axis_size("expert")
    tok_count = patches.shape[0]
    tokens_all = tok_count * groups * lax.axis_size("hidden")
    local_count = EXPERTS // groups
    own_units = expert_inner.shape[0]
    half = local_count // 2 * 2 * D
    both = jnp.stack([expert_inner, expert_outer], axis=2).astype(jnp.bfloat16)
    both = both.reshape(own_units, local_count * 2 * D)
    weights = [
        lax.all_gather(both[:, :half], "hidden", axis=0, tiled=True),
        lax.all_gather(both[:, half:], "hidden", axis=0, tiled=True),
    ]
    table = jnp.concatenate([expert_ids.astype(jnp.float32).T, gates.T], axis=0)
    tables = to_peers([table] * groups, groups)
    g_all = to_peers([cotangent] * groups, groups)
    first_expert = (lax.axis_index("expert") * local_count).astype(jnp.int32).reshape(1)
    tables = jnp.stack(tables)
    rows, gate_rows, cols = route(first_expert, tables[:, :TOP], tables[:, TOP:], local_count)
    named = jnp.sum(
        (expert_ids[:, :, None] == jnp.arange(EXPERTS, dtype=jnp.int32)).astype(jnp.int32), axis=(0, 1)
    )
    counts = jnp.minimum(named, CAP)
    digits = (counts[None, :] >> jnp.arange(16, dtype=jnp.int32)[:, None]) & 1
    digits = jnp.pad(digits.astype(jnp.float32), ((0, 0), (0, 128 - EXPERTS)))
    marks = segments[0]
    task_row = task_ids[None]
    *saved, moe_in = attend(marks, patches, norm_params, attn_qkv, attn_proj, segments, task_row)
    hidden_one = saved[-1]
    u_all = to_peers([moe_in] * groups, groups)
    second = local_count // 2
    early = moe_early(rows, gate_rows, g_all)
    y_sums, du_sums, grads_first = moe_full(rows, cols, early, u_all, weights[0], 0)
    outs = moe_front(rows, cols, early, u_all, weights[1], second, du_sums)
    du_parts = to_peers(outs[:groups], groups)
    *y_own, grads_second = moe_rest(cols, outs[groups:], early, weights[1], second, local_count, y_sums)
    y_parts = to_peers(y_own, groups)
    moe_sum = sum(p.astype(jnp.float32) for p in y_parts)
    block_out = (hidden_one + moe_sum).astype(jnp.bfloat16)
    owned = []
    for grads in (grads_first, grads_second):
        owned.append(lax.psum_scatter(grads, "hidden", scatter_dimension=0, tiled=True))
    owned = jnp.concatenate(owned, axis=1).astype(jnp.float32)
    owned = owned.reshape(own_units, local_count, 2, D)
    inner_grad, outer_grad = owned[:, :, 0], owned[:, :, 1]
    patch_grad, big = attend_back(
        marks, patches, norm_params, attn_qkv, attn_proj, segments, task_row, cotangent, saved,
        du_parts, digits,
    )
    big_sum = butterfly_sum(big, jnp.bfloat16)
    qkv_sum = jnp.concatenate([big_sum[:D, : 2 * D], big_sum[D:, :D]], axis=1)
    proj_sum = big_sum[D:, D : 2 * D]
    extra = big_sum[:, 2 * D :]
    norm_sum = jnp.concatenate([extra[8 * p : 8 * p + 6] for p in range(D // 128)], axis=1)
    powers = 2.0 ** jnp.arange(DIGITS, dtype=jnp.float32)
    count_sum = jnp.sum(extra[24 : 24 + DIGITS, :EXPERTS] * powers[:, None], axis=0)
    expert_load = count_sum * (EXPERTS / (tokens_all * TOP))
    root_tokens = math.sqrt(tokens_all)
    norm_new = nesterov(norm_params, norm_moment, norm_average, norm_sum, RATE_NORM / root_tokens)
    qkv_new = nesterov(attn_qkv, qkv_moment, qkv_average, qkv_sum, RATE_QKV / root_tokens)
    proj_new = nesterov(attn_proj, proj_moment, proj_average, proj_sum, RATE_PROJ / root_tokens)
    inner_new = nesterov(
        expert_inner, inner_moment, inner_average, inner_grad, RATE_INNER / root_tokens
    )
    outer_new = nesterov(
        expert_outer, outer_moment, outer_average, outer_grad, RATE_OUTER / root_tokens
    )
    return (
        block_out,
        patch_grad,
        expert_load,
        norm_new[0],
        norm_new[1],
        norm_new[2],
        qkv_new[0],
        qkv_new[1],
        qkv_new[2],
        proj_new[0],
        proj_new[1],
        proj_new[2],
        inner_new[0],
        inner_new[1],
        inner_new[2],
        outer_new[0],
        outer_new[1],
        outer_new[2],
    )


def solution(mesh):
    return jax.shard_map(
        body,
        mesh=mesh,
        in_specs=(
            P(("expert", "hidden"), None),
            P(("expert", "hidden"), None),
            P(("expert", "hidden"), None),
            P(("expert", "hidden"), None),
            P(("expert", "hidden")),
            P(("expert", "hidden"), None),
            P(),
            P(),
            P(),
            P("hidden", "expert", None),
            P("hidden", "expert", None),
            P(),
            P(),
            P(),
            P("hidden", "expert", None),
            P("hidden", "expert", None),
            P(),
            P(),
            P(),
            P("hidden", "expert", None),
            P("hidden", "expert", None),
        ),
        out_specs=(
            P(("expert", "hidden"), None),
            P(("expert", "hidden"), None),
            P(),
            P(),
            P(),
            P(),
            P(),
            P(),
            P(),
            P(),
            P(),
            P(),
            P("hidden", "expert", None),
            P("hidden", "expert", None),
            P("hidden", "expert", None),
            P("hidden", "expert", None),
            P("hidden", "expert", None),
            P("hidden", "expert", None),
        ),
        check_vma=False,
    )
```

```python
import functools
import math

import jax
import jax.numpy as jnp
from jax import lax
from jax.experimental import pallas as pl
from jax.experimental.pallas import tpu as pltpu
from jax.sharding import PartitionSpec as P

D = 384
HEADS = 6
HEAD = 64
EXPERTS = 16
TOP = 4
CAP = 320


MOMENT_DECAY = 0.9
AVERAGE_DECAY = 0.9
RATE_NORM = 0.23
RATE_QKV = 0.064
RATE_PROJ = 1.4
RATE_INNER = 0.21
RATE_OUTER = 0.73
NORM_EPS = 1e-06
MASKED = -1e30
VMEM_MOST = 67043328
DIGITS = 9


def route_kernel(first_expert, ids_ref, gates_ref, rows_ref, gate_rows_ref, cols_ref):
    slots, _, tokens = ids_ref.shape
    count = rows_ref.shape[1]
    before = (
        lax.broadcasted_iota(jnp.int32, (tokens, tokens), 0)
        <= lax.broadcasted_iota(jnp.int32, (tokens, tokens), 1)
    )
    before = jnp.where(before, 1.0, 0.0).astype(jnp.bfloat16)
    hot_rows = []
    for slot in range(slots):
        for expert in range(count):
            hot = jnp.zeros((1, tokens), jnp.float32)
            gate = jnp.zeros((1, tokens), jnp.float32)
            name = (first_expert[0] + expert).astype(jnp.float32)
            for choice in range(TOP):
                same = ids_ref[slot, choice : choice + 1, :] == name
                hot = jnp.where(same, 1.0, hot)
                gate = jnp.where(same, gates_ref[slot, choice : choice + 1, :], gate)
            hot_rows.append(hot)
            gate_rows_ref[slot, expert : expert + 1, :] = gate
    hot_all = jnp.concatenate(hot_rows, axis=0)
    place = jnp.dot(hot_all.astype(jnp.bfloat16), before, preferred_element_type=jnp.float32) - 1.0
    place = jnp.where((hot_all > 0.5) & (place < CAP), place, -1.0)
    for slot in range(slots):
        rows_ref[slot] = place[slot * count : (slot + 1) * count].astype(jnp.int32)
    wide = jnp.concatenate([place, jnp.full((128 - place.shape[0], tokens), -1.0, jnp.float32)], axis=0)
    cols_ref[...] = jnp.transpose(wide).astype(jnp.int32)


def route(first_expert, ids_all, gates_all, count):
    slots, _, tokens = ids_all.shape
    vmem = pl.BlockSpec(memory_space=pltpu.VMEM)
    return pl.pallas_call(
        route_kernel,
        out_shape=(
            jax.ShapeDtypeStruct((slots, count, tokens), jnp.int32),
            jax.ShapeDtypeStruct((slots, count, tokens), jnp.float32),
            jax.ShapeDtypeStruct((tokens, 128), jnp.int32),
        ),
        in_specs=[pl.BlockSpec(memory_space=pltpu.SMEM), vmem, vmem],
        out_specs=(vmem, vmem, vmem),
        name="route",
    )(first_expert, ids_all, gates_all)


NT = (((1,), (1,)), ((), ()))
NN = (((1,), (0,)), ((), ()))
TN = (((0,), (0,)), ((), ()))


def mxu(left, right, dims=NN):
    return lax.dot_general(left, right, dims, preferred_element_type=jnp.float32)


def moe_early_kernel(slots, rows_ref, gate_rows_ref, *rest):
    g_refs, dy_ref, gate_ref = rest[:slots], rest[slots], rest[slots + 1]
    tokens = rows_ref.shape[2]
    lane = pl.program_id(0)
    for slot in range(slots):
        same = lax.broadcasted_iota(jnp.int32, (CAP, tokens), 0) == rows_ref[slot, pl.ds(lane, 1), :]
        pick = jnp.where(same, 1.0, 0.0).astype(jnp.bfloat16)
        gate = jnp.sum(jnp.where(same, gate_rows_ref[slot, pl.ds(lane, 1), :], 0.0), axis=1, keepdims=True)
        span = pl.ds(slot * CAP, CAP)
        dy_ref[span, :] = (gate * mxu(pick, g_refs[slot][...])).astype(jnp.bfloat16)
        gate_ref[span, :] = jnp.broadcast_to(gate, (CAP, 128))


def moe_early(rows, gate_rows, g_all):
    slots, count, tokens = rows.shape
    width = g_all[0].shape[1]
    pairs = slots * CAP
    operands = [rows, gate_rows, *g_all]
    shapes = [((pairs, width), jnp.bfloat16), ((pairs, 128), jnp.float32)]
    return moe_call(
        functools.partial(moe_early_kernel, slots), count, operands,
        [once(a) for a in operands],
        [jax.ShapeDtypeStruct((count,) + shape, kind) for shape, kind in shapes],
        [pl.BlockSpec((pl.Squeezed(),) + shape, lambda e: (e, 0, 0)) for shape, _ in shapes],
        [], count * pairs * width * 2 * tokens,
    )


def dispatch(rows_ref, u_refs, lane, x_out):
    slots, _, tokens = rows_ref.shape
    for slot in range(slots):
        same = lax.broadcasted_iota(jnp.int32, (CAP, tokens), 0) == rows_ref[slot, pl.ds(lane, 1), :]
        pick = jnp.where(same, 1.0, 0.0).astype(jnp.bfloat16)
        x_out[pl.ds(slot * CAP, CAP), :] = mxu(pick, u_refs[slot][...]).astype(jnp.bfloat16)


def combine(cols_ref, lanes, step, buf, sum_buf, fresh):
    tokens = cols_ref.shape[0]
    for slot, lane in enumerate(lanes):
        wide = lax.broadcasted_iota(jnp.int32, (tokens, 128), 1) == lane
        column = jnp.sum(jnp.where(wide, cols_ref[...], 0), axis=1, keepdims=True)
        same = lax.broadcasted_iota(jnp.int32, (tokens, CAP), 1) == column
        spread = jnp.where(same, 1.0, 0.0).astype(jnp.bfloat16)
        add = mxu(spread, buf[pl.ds(slot * CAP, CAP), :])
        old = sum_buf[slot]
        if fresh:
            old = jnp.where(step > 0, old, 0.0)
        sum_buf[slot] = old + add


def gelu_pair(pre, act_grad):
    phi = 0.5 + 0.5 * lax.erf(pre * math.sqrt(0.5))
    bell = jnp.exp(pre * pre * -0.5) * (1.0 / math.sqrt(2.0 * math.pi))
    return (pre * phi).astype(jnp.bfloat16), (act_grad * (phi + pre * bell)).astype(jnp.bfloat16)


def times_gate(gate, result):
    gate_wide = jnp.concatenate([gate] * (result.shape[1] // 128), axis=1)
    return (gate_wide * result).astype(jnp.bfloat16)


def slot_lanes(slots, count, offset, step):
    return [slot * count + offset + step for slot in range(slots)]


def moe_full_kernel(offset, chunk, slots, rows_ref, cols_ref, dy_ref, gate_ref, *rest):
    u_refs, rest = rest[:slots], rest[slots:]
    inner_ref, outer_ref, y_ref, du_ref, grads_ref = rest[:5]
    x_buf, dy_buf, act_buf, dpre_buf, y_buf, du_buf = rest[5:]
    step = pl.program_id(0)
    width = inner_ref.shape[1]
    dispatch(rows_ref, u_refs, offset + step, x_buf)

    def part(index, carry):
        span = pl.ds(pl.multiple_of(index * chunk, chunk), chunk)
        rows_in = x_buf[...]
        rows_grad = dy_ref[...]
        act, dpre = gelu_pair(mxu(rows_in, inner_ref[span, :], NT), mxu(rows_grad, outer_ref[span, :], NT))
        act_buf[:, span] = act
        dpre_buf[:, span] = dpre
        grads_ref[span, :width] = mxu(dpre, rows_in, TN).astype(jnp.bfloat16)
        grads_ref[span, width:] = mxu(act, rows_grad, TN).astype(jnp.bfloat16)
        return carry

    lax.fori_loop(0, inner_ref.shape[0] // chunk, part, 0)
    x_buf[...] = times_gate(gate_ref[...], mxu(act_buf[...], outer_ref[...]))
    dy_buf[...] = mxu(dpre_buf[...], inner_ref[...]).astype(jnp.bfloat16)
    lanes = slot_lanes(slots, rows_ref.shape[1], offset, step)
    combine(cols_ref, lanes, step, x_buf, y_buf, True)
    combine(cols_ref, lanes, step, dy_buf, du_buf, True)

    @pl.when(step == pl.num_programs(0) - 1)
    def _():
        y_ref[...] = y_buf[...]
        du_ref[...] = du_buf[...]


def fetch(start_ref, sum_buf, sem):
    @pl.when(pl.program_id(0) == 0)
    def _():
        copy = pltpu.make_async_copy(start_ref, sum_buf, sem)
        copy.start()
        copy.wait()


def finish_sums(out_refs, sum_buf):
    @pl.when(pl.program_id(0) == pl.num_programs(0) - 1)
    def _():
        for slot, ref in enumerate(out_refs):
            ref[...] = sum_buf[slot].astype(jnp.bfloat16)


def moe_front_kernel(offset, chunk, slots, rows_ref, cols_ref, dy_ref, *rest):
    u_refs, rest = rest[:slots], rest[slots:]
    inner_ref, outer_ref, start_ref, rest = rest[0], rest[1], rest[2], rest[3:]
    du_refs, rest = rest[:slots], rest[slots:]
    x_ref, act_ref, dpre_ref, buf, sum_buf, sem = rest
    step = pl.program_id(0)
    fetch(start_ref, sum_buf, sem)
    dispatch(rows_ref, u_refs, offset + step, x_ref)

    def part(index, carry):
        span = pl.ds(pl.multiple_of(index * chunk, chunk), chunk)
        act, dpre = gelu_pair(mxu(x_ref[...], inner_ref[span, :], NT), mxu(dy_ref[...], outer_ref[span, :], NT))
        act_ref[:, span] = act
        dpre_ref[:, span] = dpre
        return carry

    lax.fori_loop(0, inner_ref.shape[0] // chunk, part, 0)
    buf[...] = mxu(dpre_ref[...], inner_ref[...]).astype(jnp.bfloat16)
    combine(cols_ref, slot_lanes(slots, rows_ref.shape[1], offset, step), step, buf, sum_buf, False)
    finish_sums(du_refs, sum_buf)


def moe_rest_kernel(offset, chunk, slots, count, cols_ref, x_ref, dy_ref, gate_ref, act_ref, dpre_ref, *rest):
    outer_ref, start_ref, rest = rest[0], rest[1], rest[2:]
    y_refs, rest = rest[:slots], rest[slots:]
    grads_ref, buf, sum_buf, sem = rest
    step = pl.program_id(0)
    width = x_ref.shape[1]
    fetch(start_ref, sum_buf, sem)

    def part(index, carry):
        span = pl.ds(pl.multiple_of(index * chunk, chunk), chunk)
        grads_ref[span, :width] = mxu(dpre_ref[:, span], x_ref[...], TN).astype(jnp.bfloat16)
        grads_ref[span, width:] = mxu(act_ref[:, span], dy_ref[...], TN).astype(jnp.bfloat16)
        return carry

    lax.fori_loop(0, outer_ref.shape[0] // chunk, part, 0)
    buf[...] = times_gate(gate_ref[...], mxu(act_ref[...], outer_ref[...]))
    combine(cols_ref, slot_lanes(slots, count, offset, step), step, buf, sum_buf, False)
    finish_sums(y_refs, sum_buf)


def once(array):
    return pl.BlockSpec(array.shape, lambda e: (0,) * len(array.shape), pipeline_mode=pl.Buffered(1))


def moe_call(kernel, steps, operands, in_specs, outs, out_specs, scratch, flops):
    return pl.pallas_call(
        kernel,
        out_shape=tuple(outs),
        grid_spec=pltpu.PrefetchScalarGridSpec(
            num_scalar_prefetch=0, grid=(steps,), in_specs=in_specs, out_specs=tuple(out_specs),
            scratch_shapes=scratch,
        ),
        compiler_params=pltpu.CompilerParams(
            dimension_semantics=("arbitrary",), vmem_limit_bytes=VMEM_MOST
        ),
        cost_estimate=pl.CostEstimate(flops=flops, bytes_accessed=40 << 20, transcendentals=0),
    )(*operands)


def moe_sizes(slots, tokens, weights, width):
    units = weights.shape[0]
    steps = weights.shape[1] // (2 * width)
    pairs = slots * CAP
    low, full = jnp.bfloat16, jnp.float32
    sums = jax.ShapeDtypeStruct((slots, tokens, width), full)
    part = jax.ShapeDtypeStruct((tokens, width), low)
    inner = pl.BlockSpec((units, width), lambda e: (0, 2 * e))
    outer = pl.BlockSpec((units, width), lambda e: (0, 2 * e + 1))
    grads = jax.ShapeDtypeStruct((units, steps * 2 * width), low)
    grads_spec = pl.BlockSpec((units, 2 * width), lambda e: (0, e))
    return units, steps, pairs, sums, part, inner, outer, grads, grads_spec


def expert_block(array, offset):
    return pl.BlockSpec((pl.Squeezed(),) + array.shape[1:], lambda e: (offset + e, 0, 0))


def moe_full(rows, cols, early, u_all, weights, offset):
    slots, _, tokens = rows.shape
    width = u_all[0].shape[1]
    units, steps, pairs, sums, _, inner, outer, grads, grads_spec = moe_sizes(slots, tokens, weights, width)
    operands = [rows, cols, *early, *u_all, weights, weights]
    low, full = jnp.bfloat16, jnp.float32
    scratch = [pltpu.VMEM((pairs, width), low)] * 2 + [pltpu.VMEM((pairs, units), low)] * 2
    scratch += [pltpu.VMEM(sums.shape, full)] * 2
    return moe_call(
        functools.partial(moe_full_kernel, offset, units // 3, slots), steps, operands,
        [once(rows), once(cols)] + [expert_block(a, offset) for a in early]
        + [once(a) for a in u_all] + [inner, outer],
        [sums, sums, grads], [once(sums), once(sums), grads_spec], scratch,
        steps * pairs * width * (12 * units + 6 * tokens),
    )


def moe_front(rows, cols, early, u_all, weights, offset, start):
    slots, _, tokens = rows.shape
    width = u_all[0].shape[1]
    units, steps, pairs, sums, part, inner, outer, _, _ = moe_sizes(slots, tokens, weights, width)
    operands = [rows, cols, early[0], *u_all, weights, weights, start]
    low, full = jnp.bfloat16, jnp.float32
    kept = [((pairs, width), low), ((pairs, units), low), ((pairs, units), low)]
    outs = [part] * slots + [jax.ShapeDtypeStruct((steps,) + shape, kind) for shape, kind in kept]
    specs = [once(part)] * slots
    specs += [pl.BlockSpec((pl.Squeezed(),) + shape, lambda e: (e, 0, 0)) for shape, _ in kept]
    return moe_call(
        functools.partial(moe_front_kernel, offset, units // 3, slots), steps, operands,
        [once(rows), once(cols), expert_block(early[0], offset)]
        + [once(a) for a in u_all] + [inner, outer, pl.BlockSpec(memory_space=pl.ANY)],
        outs, specs,
        [pltpu.VMEM((pairs, width), low), pltpu.VMEM(sums.shape, full), pltpu.SemaphoreType.DMA],
        steps * pairs * width * (6 * units + 4 * tokens),
    )


def moe_rest(cols, kept, early, weights, offset, count, start):
    slots, tokens, width = start.shape
    units, steps, pairs, sums, part, _, outer, grads, grads_spec = moe_sizes(slots, tokens, weights, width)
    operands = [cols, kept[0], *early, *kept[1:], weights, start]
    low, full = jnp.bfloat16, jnp.float32
    in_specs = [once(cols)]
    in_specs += [expert_block(kept[0], 0)] + [expert_block(a, offset) for a in early]
    in_specs += [expert_block(a, 0) for a in kept[1:]]
    return moe_call(
        functools.partial(moe_rest_kernel, offset, units // 3, slots, count), steps, operands,
        in_specs + [outer, pl.BlockSpec(memory_space=pl.ANY)],
        [part] * slots + [grads], [once(part)] * slots + [grads_spec],
        [pltpu.VMEM((pairs, width), low), pltpu.VMEM(sums.shape, full), pltpu.SemaphoreType.DMA],
        steps * pairs * width * (6 * units + 2 * tokens),
    )


def unit_rows(values):
    center = values - jnp.mean(values, axis=1, keepdims=True)
    rate = lax.rsqrt(jnp.mean(center * center, axis=1, keepdims=True) + NORM_EPS)
    return center * rate, rate


def unit_rows_back(unit, rate, grad):
    mean_grad = jnp.mean(grad, axis=1, keepdims=True)
    mean_dot = jnp.mean(grad * unit, axis=1, keepdims=True)
    return rate * (grad - mean_grad - unit * mean_dot)


def as_column(row):
    wide = jnp.broadcast_to(row.astype(jnp.float32), (128, row.shape[1]))
    return jnp.transpose(wide)


def key_range(marks_ref, row_start, block, blocks):
    first = marks_ref[row_start]
    last = marks_ref[row_start + block - 1]
    begin = jnp.int32(0)
    end = jnp.int32(0)
    for index in range(blocks):
        begin = begin + jnp.where(marks_ref[index * block + block - 1] < first, 1, 0)
        end = end + jnp.where(marks_ref[index * block] <= last, 1, 0)
    return begin, end


def head_masks(block):
    low_half = lax.broadcasted_iota(jnp.int32, (block, 2 * HEAD), 1) < HEAD
    return low_half, jnp.logical_not(low_half)


def attend_kernel(
    block, marks_ref, x_ref, norm_ref, qkv_ref, proj_ref, seg_ref, task_ref,
    joined_ref, key_t_ref, mixed_ref, mixed_t_ref, logs_ref, hidden_ref, u_ref, value_t, column,
):
    tokens = x_ref.shape[0]
    blocks = tokens // block
    qkv_low = qkv_ref[...].astype(jnp.bfloat16)
    proj_low = proj_ref[...].astype(jnp.bfloat16)
    column[...] = as_column(seg_ref[...])

    def project(index, carry):
        span = pl.ds(pl.multiple_of(index * block, block), block)
        unit, _ = unit_rows(x_ref[span, :].astype(jnp.float32))
        attn_in = (unit * norm_ref[0:1, :] + norm_ref[1:2, :]).astype(jnp.bfloat16)
        joined = mxu(attn_in, qkv_low)
        joined_ref[span, :] = joined.astype(jnp.bfloat16)
        key_t_ref[:, span] = jnp.transpose(joined[:, D : 2 * D]).astype(jnp.bfloat16)
        value_t[:, span] = jnp.transpose(joined[:, 2 * D :]).astype(jnp.bfloat16)
        return carry

    lax.fori_loop(0, blocks, project, 0)

    def rows(index, carry):
        start = pl.multiple_of(index * block, block)
        span = pl.ds(start, block)
        begin, end = key_range(marks_ref, index * block, block, blocks)
        seg_row = seg_ref[:, span].astype(jnp.float32)
        masks = head_masks(block)
        queries = []
        for pair in range(HEADS // 2):
            lanes = slice(pair * 2 * HEAD, (pair + 1) * 2 * HEAD)
            query = joined_ref[span, lanes] * jnp.bfloat16(HEAD ** (-0.5))
            queries.extend(jnp.where(m, query, jnp.zeros_like(query)) for m in masks)

        def keys(at, state):
            key_span = pl.ds(pl.multiple_of(at * block, block), block)
            seg_col = jnp.concatenate([column[key_span, :]] * (block // 128), axis=1)
            same = seg_col == seg_row
            out = []
            for head in range(HEADS):
                first = D + head // 2 * 2 * HEAD
                key_pair = joined_ref[key_span, first : first + 2 * HEAD]
                peak, total, acc = state[head]
                scores = jnp.where(same, mxu(key_pair, queries[head], NT), MASKED)
                new_peak = jnp.maximum(peak, jnp.max(scores, axis=0, keepdims=True))
                weights = jnp.exp(scores - new_peak)
                fix = jnp.exp(peak - new_peak)
                total = total * fix + jnp.sum(weights, axis=0, keepdims=True)
                value = value_t[head * HEAD : (head + 1) * HEAD, key_span]
                acc = acc * fix + mxu(value, weights.astype(jnp.bfloat16))
                out.append((new_peak, total, acc))
            return tuple(out)

        zero = (
            jnp.full((1, block), MASKED, jnp.float32),
            jnp.zeros((1, block), jnp.float32),
            jnp.zeros((HEAD, block), jnp.float32),
        )
        done = lax.fori_loop(begin, end, keys, (zero,) * HEADS)
        for head in range(HEADS):
            peak, total, acc = done[head]
            mixed_t_ref[head * HEAD : (head + 1) * HEAD, span] = (acc / total).astype(jnp.bfloat16)
            logs_ref[head : head + 1, span] = peak + jnp.log(total)
        mixed = jnp.transpose(mixed_t_ref[:, span].astype(jnp.float32)).astype(jnp.bfloat16)
        mixed_ref[span, :] = mixed
        hidden = x_ref[span, :].astype(jnp.float32) + mxu(mixed, proj_low)
        hidden_ref[span, :] = hidden
        task = jnp.concatenate([as_column(task_ref[:, span])] * (D // 128), axis=1) > 0.5
        gain = jnp.where(task, norm_ref[3:4, :], norm_ref[2:3, :])
        bias = jnp.where(task, norm_ref[5:6, :], norm_ref[4:5, :])
        unit, _ = unit_rows(hidden)
        u_ref[span, :] = (unit * gain + bias).astype(jnp.bfloat16)
        return carry

    lax.fori_loop(0, blocks, rows, 0)


def attend(marks, x, norm, qkv, proj, seg, task):
    tokens = x.shape[0]
    block = min(256, tokens)
    vmem = pl.BlockSpec(memory_space=pltpu.VMEM)
    low = jnp.bfloat16
    return pl.pallas_call(
        functools.partial(attend_kernel, block),
        out_shape=(
            jax.ShapeDtypeStruct((tokens, 3 * D), low),
            jax.ShapeDtypeStruct((D, tokens), low),
            jax.ShapeDtypeStruct((tokens, D), low),
            jax.ShapeDtypeStruct((D, tokens), low),
            jax.ShapeDtypeStruct((8, tokens), jnp.float32),
            jax.ShapeDtypeStruct((tokens, D), jnp.float32),
            jax.ShapeDtypeStruct((tokens, D), low),
        ),
        in_specs=[pl.BlockSpec(memory_space=pltpu.SMEM)] + [vmem] * 6,
        out_specs=(vmem,) * 7,
        scratch_shapes=[pltpu.VMEM((D, tokens), low), pltpu.VMEM((tokens, 128), jnp.float32)],
        compiler_params=pltpu.CompilerParams(vmem_limit_bytes=48 << 20),
        cost_estimate=pl.CostEstimate(flops=8 << 30, bytes_accessed=12 << 20, transcendentals=6 << 20),
        name="attend",
    )(marks, x, norm, qkv, proj, seg, task)


def attend_back_kernel(
    block, slots, marks_ref, x_ref, norm_ref, qkv_ref, proj_ref, seg_ref, task_ref, out_grad_ref,
    joined_ref, key_t_ref, mixed_ref, mixed_t_ref, logs_ref, hidden_ref, *rest
):
    du_refs, digits_ref, rest = rest[:slots], rest[slots], rest[slots + 1 :]
    patch_ref, weight_ref, grads, attn_in, norms_ref, key_grad, value_grad, column = rest
    tokens = x_ref.shape[0]
    blocks = tokens // block
    qkv_low = qkv_ref[...].astype(jnp.bfloat16)
    proj_low = proj_ref[...].astype(jnp.bfloat16)
    column[...] = as_column(seg_ref[...])
    key_grad[...] = jnp.zeros_like(key_grad)
    value_grad[...] = jnp.zeros_like(value_grad)
    norms_ref[...] = jnp.zeros_like(norms_ref)
    weight_ref[...] = jnp.zeros_like(weight_ref)

    def rows(index, carry):
        start = pl.multiple_of(index * block, block)
        span = pl.ds(start, block)
        du = du_refs[0][span, :].astype(jnp.float32)
        for ref in du_refs[1:]:
            du = du + ref[span, :].astype(jnp.float32)
        task = jnp.concatenate([as_column(task_ref[:, span])] * (D // 128), axis=1) > 0.5
        gain = jnp.where(task, norm_ref[3:4, :], norm_ref[2:3, :])
        unit, rate = unit_rows(hidden_ref[span, :])
        first = jnp.where(task, 0.0, du)
        second = jnp.where(task, du, 0.0)
        norms_ref[2:3, :] += jnp.sum(first * unit, axis=0, keepdims=True)
        norms_ref[3:4, :] += jnp.sum(second * unit, axis=0, keepdims=True)
        norms_ref[4:5, :] += jnp.sum(first, axis=0, keepdims=True)
        norms_ref[5:6, :] += jnp.sum(second, axis=0, keepdims=True)
        hidden_grad = out_grad_ref[span, :].astype(jnp.float32) + unit_rows_back(unit, rate, du * gain)
        patch_ref[span, :] = hidden_grad
        grad_low = hidden_grad.astype(jnp.bfloat16)
        weight_ref[D:, D : 2 * D] += mxu(mixed_ref[span, :], grad_low, TN)
        mixed_grad = mxu(grad_low, proj_low, NT).astype(jnp.bfloat16)
        mixed_grad_t = mxu(proj_low, grad_low, NT).astype(jnp.bfloat16).astype(jnp.float32)
        dots = mixed_grad_t * mixed_t_ref[:, span].astype(jnp.float32)
        begin, end = key_range(marks_ref, index * block, block, blocks)
        seg_row = seg_ref[:, span].astype(jnp.float32)
        masks = head_masks(block)
        queries = []
        out_grads = []
        deltas = []
        logs = []
        for pair in range(HEADS // 2):
            lanes = slice(pair * 2 * HEAD, (pair + 1) * 2 * HEAD)
            query = joined_ref[span, lanes] * jnp.bfloat16(HEAD ** (-0.5))
            queries.extend(jnp.where(m, query, jnp.zeros_like(query)) for m in masks)
            grad_pair = mixed_grad[:, lanes]
            out_grads.extend(jnp.where(m, grad_pair, jnp.zeros_like(grad_pair)) for m in masks)
        for head in range(HEADS):
            deltas.append(jnp.sum(dots[head * HEAD : (head + 1) * HEAD], axis=0, keepdims=True))
            logs.append(logs_ref[head : head + 1, span])

        def keys(at, state):
            key_span = pl.ds(pl.multiple_of(at * block, block), block)
            seg_col = jnp.concatenate([column[key_span, :]] * (block // 128), axis=1)
            same = seg_col == seg_row
            out = []
            for pair in range(HEADS // 2):
                first = pair * 2 * HEAD
                lanes = slice(first, first + 2 * HEAD)
                key_pair = joined_ref[key_span, D + first : D + first + 2 * HEAD]
                value_pair = joined_ref[key_span, 2 * D + first : 2 * D + first + 2 * HEAD]
                key_sum = key_grad[key_span, lanes]
                value_sum = value_grad[key_span, lanes]
                for head in (2 * pair, 2 * pair + 1):
                    scores = jnp.where(same, mxu(key_pair, queries[head], NT), MASKED)
                    probs = jnp.exp(scores - logs[head])
                    prob_grad = mxu(value_pair, out_grads[head], NT)
                    score_grad = (probs * (prob_grad - deltas[head])).astype(jnp.bfloat16)
                    value_sum = value_sum + mxu(probs.astype(jnp.bfloat16), out_grads[head])
                    key_sum = key_sum + mxu(score_grad, queries[head])
                    key_t = key_t_ref[head * HEAD : (head + 1) * HEAD, key_span]
                    out.append(state[head] + mxu(key_t, score_grad))
                key_grad[key_span, lanes] = key_sum
                value_grad[key_span, lanes] = value_sum
            return tuple(out)

        zero = jnp.zeros((HEAD, block), jnp.float32)
        query_grads = lax.fori_loop(begin, end, keys, (zero,) * HEADS)
        query_grad_t = jnp.concatenate(query_grads, axis=0) * HEAD ** (-0.5)
        grads[span, :D] = jnp.transpose(query_grad_t).astype(jnp.bfloat16)
        return carry

    lax.fori_loop(0, blocks, rows, 0)

    def finish(index, carry):
        span = pl.ds(pl.multiple_of(index * block, block), block)
        grads[span, D : 2 * D] = key_grad[span, :].astype(jnp.bfloat16)
        grads[span, 2 * D :] = value_grad[span, :].astype(jnp.bfloat16)
        unit, rate = unit_rows(x_ref[span, :].astype(jnp.float32))
        attn_in[span, :] = (unit * norm_ref[0:1, :] + norm_ref[1:2, :]).astype(jnp.bfloat16)
        joined_grad = grads[span, :]
        in_grad = mxu(joined_grad, qkv_low, NT)
        norms_ref[0:1, :] += jnp.sum(in_grad * unit, axis=0, keepdims=True)
        norms_ref[1:2, :] += jnp.sum(in_grad, axis=0, keepdims=True)
        patch_ref[span, :] += unit_rows_back(unit, rate, in_grad * norm_ref[0:1, :])
        return carry

    lax.fori_loop(0, blocks, finish, 0)
    weight_ref[:D, : 2 * D] = mxu(attn_in[...], grads[:, : 2 * D], TN)
    weight_ref[D:, :D] = mxu(attn_in[...], grads[:, 2 * D :], TN)
    for part in range(D // 128):
        weight_ref[part * 8 : part * 8 + 8, 2 * D :] = norms_ref[:, part * 128 : (part + 1) * 128]
    weight_ref[24 : 24 + digits_ref.shape[0], 2 * D :] = digits_ref[...]


def attend_back(marks, x, norm, qkv, proj, seg, task, out_grad, saved, du_parts, digits):
    tokens = x.shape[0]
    block = min(256, tokens)
    vmem = pl.BlockSpec(memory_space=pltpu.VMEM)
    operands = [marks, x, norm, qkv, proj, seg, task, out_grad, *saved, *du_parts, digits]
    return pl.pallas_call(
        functools.partial(attend_back_kernel, block, len(du_parts)),
        out_shape=(
            jax.ShapeDtypeStruct((tokens, D), jnp.float32),
            jax.ShapeDtypeStruct((2 * D, 2 * D + 128), jnp.float32),
        ),
        in_specs=[pl.BlockSpec(memory_space=pltpu.SMEM)] + [vmem] * (len(operands) - 1),
        out_specs=(vmem,) * 2,
        scratch_shapes=[
            pltpu.VMEM((tokens, 3 * D), jnp.bfloat16),
            pltpu.VMEM((tokens, D), jnp.bfloat16),
            pltpu.VMEM((8, D), jnp.float32),
            pltpu.VMEM((tokens, D), jnp.float32),
            pltpu.VMEM((tokens, D), jnp.float32),
            pltpu.VMEM((tokens, 128), jnp.float32),
        ],
        compiler_params=pltpu.CompilerParams(vmem_limit_bytes=52 << 20),
        cost_estimate=pl.CostEstimate(flops=24 << 30, bytes_accessed=24 << 20, transcendentals=6 << 20),
        name="attend_back",
    )(*operands)


def to_peers(arrays, groups):
    return [arrays[0]] + [
        lax.ppermute(arrays[k], "expert", [(i, i ^ k) for i in range(groups)]) for k in range(1, groups)
    ]


def sum_stages():
    stages = []
    sizes = (("hidden", 1, 2), ("expert", 1, lax.axis_size("expert")), ("hidden", 2, lax.axis_size("hidden")))
    for axis, bit, size in sizes:
        while bit < size:
            ways = 4 if bit * 4 <= size else 2
            stages.append((axis, bit, ways))
            bit *= ways
    return stages


def exchange(pieces, axis, bit):
    size = lax.axis_size(axis)
    return [
        lax.ppermute(piece, axis, [(i, i ^ (bit * k)) for i in range(size)])
        for k, piece in enumerate(pieces, 1)
    ]


def butterfly_sum(value, wire):
    done = []
    for axis, bit, ways in sum_stages():
        rows = value.shape[0] // ways
        mine = lax.axis_index(axis) // bit % ways
        split = value.shape[0] % ways == 0 and rows % 8 == 0
        if split:
            pieces = [lax.dynamic_slice_in_dim(value, (mine ^ k) * rows, rows) for k in range(ways)]
        else:
            pieces = [value] * ways
        got = exchange([p.astype(wire) for p in pieces[1:]], axis, bit)
        value = pieces[0] + sum(g.astype(jnp.float32) for g in got)
        if split:
            done.append((axis, bit, ways, mine))
    value = value.astype(wire)
    for axis, bit, ways, mine in done[::-1]:
        got = [value] + exchange([value] * (ways - 1), axis, bit)
        ordered = []
        for k in range(ways):
            piece = got[0]
            for j in range(1, ways):
                piece = jnp.where((mine ^ k) == j, got[j], piece)
            ordered.append(piece)
        value = jnp.concatenate(ordered, axis=0)
    return value.astype(jnp.float32)


def update_kernel(rates, first_ref, second_ref, *refs):
    ins, outs = refs[:6], refs[6:]
    width = first_ref.shape[1] // 4
    count = ins[0].shape[1]
    for expert in range(count):
        source = first_ref if expert < count // 2 else second_ref
        for side in range(2):
            at = (expert % (count // 2) * 2 + side) * width
            grad = source[:, at : at + width].astype(jnp.float32)
            weight, moment, average = (ref[:, expert, :] for ref in ins[3 * side : 3 * side + 3])
            results = nesterov(weight, moment, average, grad, rates[side])
            for ref, result in zip(outs[3 * side : 3 * side + 3], results):
                ref[:, expert, :] = result


def expert_update(first, second, arrays, rates):
    rows, count, width = arrays[0].shape
    block = rows // 3
    flat = pl.BlockSpec((block, first.shape[1]), lambda i: (i, 0))
    deep = pl.BlockSpec((block, count, width), lambda i: (i, 0, 0))
    return pl.pallas_call(
        functools.partial(update_kernel, rates),
        out_shape=(jax.ShapeDtypeStruct(arrays[0].shape, jnp.float32),) * 6,
        grid=(3,),
        in_specs=[flat, flat] + [deep] * 6,
        out_specs=(deep,) * 6,
        compiler_params=pltpu.CompilerParams(vmem_limit_bytes=40 << 20),
        cost_estimate=pl.CostEstimate(flops=1 << 23, bytes_accessed=16 << 20, transcendentals=0),
        name="expert_update",
    )(first, second, *arrays)


def nesterov(weight, moment, average, grad, rate):
    moment_new = MOMENT_DECAY * moment + grad
    weight_new = weight - rate * (grad + MOMENT_DECAY * moment_new)
    average_new = AVERAGE_DECAY * average + (1.0 - AVERAGE_DECAY) * weight_new
    return (weight_new, moment_new, average_new)


def body(
    patches,
    cotangent,
    expert_ids,
    gates,
    task_ids,
    segments,
    norm_params,
    attn_qkv,
    attn_proj,
    expert_inner,
    expert_outer,
    norm_moment,
    qkv_moment,
    proj_moment,
    inner_moment,
    outer_moment,
    norm_average,
    qkv_average,
    proj_average,
    inner_average,
    outer_average,
):
    groups = lax.axis_size("expert")
    tok_count = patches.shape[0]
    tokens_all = tok_count * groups * lax.axis_size("hidden")
    local_count = EXPERTS // groups
    own_units = expert_inner.shape[0]
    half = local_count // 2 * 2 * D
    both = jnp.stack([expert_inner, expert_outer], axis=2).astype(jnp.bfloat16)
    both = both.reshape(own_units, local_count * 2 * D)
    weights = [
        lax.all_gather(both[:, :half], "hidden", axis=0, tiled=True),
        lax.all_gather(both[:, half:], "hidden", axis=0, tiled=True),
    ]
    table = jnp.concatenate([expert_ids.astype(jnp.float32).T, gates.T], axis=0)
    tables = to_peers([table] * groups, groups)
    g_all = to_peers([cotangent] * groups, groups)
    first_expert = (lax.axis_index("expert") * local_count).astype(jnp.int32).reshape(1)
    tables = jnp.stack(tables)
    rows, gate_rows, cols = route(first_expert, tables[:, :TOP], tables[:, TOP:], local_count)
    named = jnp.sum(
        (expert_ids[:, :, None] == jnp.arange(EXPERTS, dtype=jnp.int32)).astype(jnp.int32), axis=(0, 1)
    )
    counts = jnp.minimum(named, CAP)
    digits = (counts[None, :] >> jnp.arange(16, dtype=jnp.int32)[:, None]) & 1
    digits = jnp.pad(digits.astype(jnp.float32), ((0, 0), (0, 128 - EXPERTS)))
    marks = segments[0]
    task_row = task_ids[None]
    *saved, moe_in = attend(marks, patches, norm_params, attn_qkv, attn_proj, segments, task_row)
    hidden_one = saved[-1]
    u_all = to_peers([moe_in] * groups, groups)
    second = local_count // 2
    early = moe_early(rows, gate_rows, g_all)
    y_sums, du_sums, grads_first = moe_full(rows, cols, early, u_all, weights[0], 0)
    outs = moe_front(rows, cols, early, u_all, weights[1], second, du_sums)
    du_parts = to_peers(outs[:groups], groups)
    *y_own, grads_second = moe_rest(cols, outs[groups:], early, weights[1], second, local_count, y_sums)
    y_parts = to_peers(y_own, groups)
    moe_sum = sum(p.astype(jnp.float32) for p in y_parts)
    block_out = (hidden_one + moe_sum).astype(jnp.bfloat16)
    owned = []
    for grads in (grads_first, grads_second):
        owned.append(lax.psum_scatter(grads, "hidden", scatter_dimension=0, tiled=True))
    patch_grad, big = attend_back(
        marks, patches, norm_params, attn_qkv, attn_proj, segments, task_row, cotangent, saved,
        du_parts, digits,
    )
    big_sum = butterfly_sum(big, jnp.bfloat16)
    qkv_sum = jnp.concatenate([big_sum[:D, : 2 * D], big_sum[D:, :D]], axis=1)
    proj_sum = big_sum[D:, D : 2 * D]
    extra = big_sum[:, 2 * D :]
    norm_sum = jnp.concatenate([extra[8 * p : 8 * p + 6] for p in range(D // 128)], axis=1)
    powers = 2.0 ** jnp.arange(DIGITS, dtype=jnp.float32)
    count_sum = jnp.sum(extra[24 : 24 + DIGITS, :EXPERTS] * powers[:, None], axis=0)
    expert_load = count_sum * (EXPERTS / (tokens_all * TOP))
    root_tokens = math.sqrt(tokens_all)
    norm_new = nesterov(norm_params, norm_moment, norm_average, norm_sum, RATE_NORM / root_tokens)
    qkv_new = nesterov(attn_qkv, qkv_moment, qkv_average, qkv_sum, RATE_QKV / root_tokens)
    proj_new = nesterov(attn_proj, proj_moment, proj_average, proj_sum, RATE_PROJ / root_tokens)
    new = expert_update(
        *owned,
        [expert_inner, inner_moment, inner_average, expert_outer, outer_moment, outer_average],
        (RATE_INNER / root_tokens, RATE_OUTER / root_tokens),
    )
    inner_new, outer_new = new[:3], new[3:]
    return (
        block_out,
        patch_grad,
        expert_load,
        norm_new[0],
        norm_new[1],
        norm_new[2],
        qkv_new[0],
        qkv_new[1],
        qkv_new[2],
        proj_new[0],
        proj_new[1],
        proj_new[2],
        inner_new[0],
        inner_new[1],
        inner_new[2],
        outer_new[0],
        outer_new[1],
        outer_new[2],
    )


def solution(mesh):
    return jax.shard_map(
        body,
        mesh=mesh,
        in_specs=(
            P(("expert", "hidden"), None),
            P(("expert", "hidden"), None),
            P(("expert", "hidden"), None),
            P(("expert", "hidden"), None),
            P(("expert", "hidden")),
            P(("expert", "hidden"), None),
            P(),
            P(),
            P(),
            P("hidden", "expert", None),
            P("hidden", "expert", None),
            P(),
            P(),
            P(),
            P("hidden", "expert", None),
            P("hidden", "expert", None),
            P(),
            P(),
            P(),
            P("hidden", "expert", None),
            P("hidden", "expert", None),
        ),
        out_specs=(
            P(("expert", "hidden"), None),
            P(("expert", "hidden"), None),
            P(),
            P(),
            P(),
            P(),
            P(),
            P(),
            P(),
            P(),
            P(),
            P(),
            P("hidden", "expert", None),
            P("hidden", "expert", None),
            P("hidden", "expert", None),
            P("hidden", "expert", None),
            P("hidden", "expert", None),
            P("hidden", "expert", None),
        ),
        check_vma=False,
    )
```
